128 devices in a mesh: dp: 8 (over x, core), tp: 16 (over y, z).
Axes of the slice: x: 4, y: 4, z: 4, core: 2. Of those that a mesh axis runs over, the one named last changes fastest.
Arguments:
- queries: bfloat16 [1024, 128, 576], P(('dp', 'tp')), may hold values from -10 to 10
- new_latent: bfloat16 [1024, 576], P(('dp', 'tp')), may hold values from -6 to 6
- resident: bfloat16 [768, 256, 576], P(('dp', 'tp')), may hold values from -6 to 6
- leaving: bfloat16 [256, 2, 256, 576], P(('dp', 'tp')), may hold values from -6 to 6
- res_len: int32 [768], P(('dp', 'tp')), may hold values from 1 to 256, as said below
- leave_len: int32 [128, 2], replicated, may hold values from 1 to 256, as said below
- mig_dest: int32 [128, 2], replicated, may hold values from 0 to 15, as said below
- stream: bfloat16 [1024, 7168], P(('dp', 'tp')), may hold values from -6 to 6
- dense_gain: float32 [7168], replicated, may hold values from 0.1 to 1.9
- w_gate: bfloat16 [7168, 18432], P('dp', 'tp'), may hold values from -0.0625 to 0.0625
- w_up: bfloat16 [7168, 18432], P('dp', 'tp'), may hold values from -0.0625 to 0.0625
- w_down: bfloat16 [18432, 7168], P('tp', 'dp'), may hold values from -0.046875 to 0.046875
- moe_gain: float32 [7168], replicated, may hold values from 0.1 to 1.9
- expert_gate: bfloat16 [16, 7168, 2048], P('tp', None, 'dp'), may hold values from -0.0625 to 0.0625
- expert_up: bfloat16 [16, 7168, 2048], P('tp', None, 'dp'), may hold values from -0.0625 to 0.0625
- expert_down: bfloat16 [16, 2048, 7168], P('tp', 'dp'), may hold values from -0.125 to 0.125
- expert_ids: int32 [1024, 8], P(('dp', 'tp')), may hold values from 0 to 15, all different within a row; in each aligned block of 8 rows (0 to 7, 8 to 15, ...) at most 5 rows name the same one
- gate_scores: float32 [1024, 8], P(('dp', 'tp')), may hold values from 0.05 to 1
Outputs:
- context: bfloat16 [1024, 128, 512], P(('dp', 'tp'))
- arrived: bfloat16 [256, 2, 256, 576], P(('dp', 'tp'))
- stream_out: bfloat16 [1024, 7168], P(('dp', 'tp'))
The draws below stay inside these ranges and needn't reach their ends.
Inputs may be any that keep to these rules, and one draw needn't show every extreme that they name: `mig_dest`: each device sends its 2 leaving requests to 2 different other devices of its dp index, and every device receives exactly 2 requests. `res_len`: some request holds all 256 positions. `leave_len`: some request holds all 256 positions. `expert_ids`: among the 8 rows of one device no expert is chosen by more than 5 rows, a bound that some block reaches; a row names 8 different experts.
All inputs are finite; a program needn't handle non-finite values.
Results may differ from the reference program's by a relative error of at most 0.023.
Values may be sent and summed in bfloat16 or wider, within the bound.
A program may use at most 128 MiB of HBM per device.

```python
import math
import jax
import jax.numpy as jnp
import numpy as np
from jax import lax

D = 7168
FF = 18432
EH = 2048
HEADS = 128
VDIM = 512
QKD = 192
TOP = 8
ROWS_DEV = 8
CACHE = 256
LAYERS = 2
MIG = 2
LAT = 576
STAY = 6
EXPERTS = 16
CAP = 5
ROWS = 1024
N_DP = 8
N_TP = 16
DEVICES = 128


def latent_field(key, shape):
    base_key = jax.random.fold_in(key, 0)
    values = jnp.clip(jax.random.normal(base_key, shape, jnp.float32), -6.0, 6.0)
    return values.astype(jnp.bfloat16)


def draw_queries(key, part):
    base_key = jax.random.fold_in(jax.random.fold_in(key, 11), 0)
    shape = (ROWS, HEADS, LAT)
    values = jnp.clip(jax.random.normal(base_key, shape, jnp.float32), -6.0, 6.0)
    return values.astype(jnp.bfloat16)


def draw_resident(key, part):
    return latent_field(jax.random.fold_in(key, 21), (DEVICES * STAY, CACHE, LAT))


def draw_leaving(key, part):
    return latent_field(jax.random.fold_in(key, 31), (DEVICES * MIG, LAYERS, CACHE, LAT))


def ragged_lengths(key, count, per_device):
    cap_key, len_key, pick_key = jax.random.split(key, 3)
    device_cap = jax.random.randint(cap_key, (DEVICES, 1), CACHE // 4, CACHE + 1)
    lengths = jax.random.randint(len_key, (DEVICES, per_device), 1, device_cap + 1).reshape(-1)
    pick = jax.random.randint(pick_key, (), 0, count)
    return jnp.where(jnp.arange(count) == pick, CACHE, lengths).astype(jnp.int32)


def draw_res_len(key, part):
    return ragged_lengths(jax.random.fold_in(key, 41), DEVICES * STAY, STAY)


def draw_leave_len(key, part):
    return ragged_lengths(jax.random.fold_in(key, 51), DEVICES * MIG, MIG).reshape(DEVICES, MIG)


def draw_mig_dest(key, part):
    keys = jax.random.split(jax.random.fold_in(key, 61), N_DP)
    perms = jax.vmap(lambda one: jax.random.permutation(one, N_TP))(keys).astype(jnp.int32)
    inverse = jnp.argsort(perms, axis=1, stable=True).astype(jnp.int32)
    steps = jnp.arange(MIG, dtype=jnp.int32)
    positions = (inverse[:, :, None] + 1 + steps[None, None, :]) % N_TP
    dest = jnp.take_along_axis(perms, positions.reshape(N_DP, N_TP * MIG), axis=1)
    return dest.reshape(DEVICES, MIG).astype(jnp.int32)


def block_scale(key, extent, cuts, least, top_value):
    def one(axis_at, parts):
        steps = jax.random.uniform(jax.random.fold_in(jax.random.fold_in(key, 6), axis_at), (parts,), jnp.float32, least / len(cuts), top_value / len(cuts))
        return jnp.repeat(jnp.exp(steps), extent[axis_at] // parts).reshape((-1,) + (1,) * (len(extent) - axis_at - 1))

    level = one(*cuts[0])
    for cut in cuts[1:]:
        level = level * one(*cut)
    return level


def shared_out(own_key, own, number, rows, number_of, top, most, skew):
    order = jax.random.permutation(own_key, number_of)
    packed, usual = load_shares(number_of, rows * top, most, skew, True), load_shares(number_of, rows * top, most, skew, False)
    places = jnp.arange(number_of)

    def named(tallies, rotation):
        used = int((tallies > 0).sum())
        fixed = max(1, used // 4)
        moved = fixed + (places - fixed + rotation * (used - fixed)) % max(1, number_of - fixed)
        return jnp.zeros((number_of,), jnp.int32).at[order[jnp.where(places < fixed, places, moved)]].set(jnp.asarray(tallies, jnp.int32))

    tallies = jnp.where(number % 4 == 0, named(packed, number // 4), named(usual, number - number // 4 - 1))
    mixed = jax.random.permutation(jax.random.fold_in(own, 3), number_of)
    donor, taker = mixed[0:number_of // 2 * 2:2], mixed[1:number_of // 2 * 2:2]
    slack = jnp.minimum(tallies[donor] - 1, most - tallies[taker]) // 2
    slack = jnp.where((donor == order[0]) | (taker == order[0]) | (tallies[taker] == 0), 0, jnp.maximum(slack, 0))
    moved = jax.random.randint(jax.random.fold_in(own, 4), (number_of // 2,), 0, 1 << 20) % (slack + 1)
    tallies = tallies.at[donor].add(-moved).at[taker].add(moved)
    items = jnp.searchsorted(jnp.cumsum(tallies), jnp.arange(rows * top), side="right").astype(jnp.int32)
    table = items.reshape(top, rows).T
    table = table[jax.random.permutation(jax.random.fold_in(own, 1), rows)]
    rotation = jax.random.randint(jax.random.fold_in(own, 2), (rows, 1), 0, top)
    return jnp.take_along_axis(table, (jnp.arange(top)[None, :] + rotation) % top, axis=1)


def load_shares(amount, total, bound, slope, full):
    portions = [(1 << 20) // math.isqrt(grade ** slope) + 1 for grade in range(1, amount + 1)]
    largest = bound if full else min(bound, max(-(-total // amount), total * portions[0] // sum(portions)))
    least = 1 if total - largest >= amount - 1 else 0
    given, rest = [largest] + [least] * (amount - 1), total - largest - least * (amount - 1)
    while rest > 0:
        candidates = [i for i in range(1, amount) if given[i] < largest] or [i for i in range(1, amount) if given[i] < bound]
        pool, left = sum([portions[i] for i in candidates]), rest
        for i in candidates:
            more = min(bound - given[i], max(1, left * portions[i] // pool), rest)
            given[i] = given[i] + more
            rest = rest - more
    return np.array(given)


def centred(stream_key, shape, scale, limit, shards=(), kind=jnp.bfloat16):
    entries = jax.random.normal(stream_key, shape, jnp.float32) * scale
    if len(shards) > 0:
        entries = block_scale(stream_key, shape, shards, -0.22, 0.18) * entries
    return jnp.clip(entries, min=-limit, max=limit).astype(kind)


def setup_inputs(seed: int = 0) -> dict:
    key_list = jax.random.split(jax.random.key(seed), 19)
    queries = draw_queries(jax.random.fold_in(key_list[18], 71), 0)
    new_latent = centred(key_list[1], (ROWS, LAT), 1.0, 6.0, ((0, 128),))
    resident = draw_resident(jax.random.fold_in(key_list[18], 71), 0)
    leaving = draw_leaving(jax.random.fold_in(key_list[18], 71), 0)
    res_len = draw_res_len(jax.random.fold_in(key_list[18], 71), 0)
    leave_len = draw_leave_len(jax.random.fold_in(key_list[18], 71), 0)
    mig_dest = draw_mig_dest(jax.random.fold_in(key_list[18], 71), 0)
    stream = centred(key_list[7], (ROWS, D), 1.0, 6.0, ((0, 128),))
    dense_gain = jnp.clip(1.0 + 0.18 * jax.random.normal(key_list[8], (D,), jnp.float32), 0.1, 1.9)
    w_gate = centred(key_list[9], (D, FF), D ** -0.5, 0.0625, ((0, 8), (1, 16)))
    w_up = centred(key_list[10], (D, FF), D ** -0.5, 0.0625, ((0, 8), (1, 16)))
    w_down = centred(key_list[11], (FF, D), FF ** -0.5, 0.046875, ((0, 16), (1, 8)))
    moe_gain = jnp.clip(1.0 + 0.18 * jax.random.normal(key_list[12], (D,), jnp.float32), 0.1, 1.9)
    expert_gate = centred(key_list[13], (EXPERTS, D, EH), D ** -0.5, 0.0625, ((0, 16), (2, 8)))
    expert_up = centred(key_list[14], (EXPERTS, D, EH), D ** -0.5, 0.0625, ((0, 16), (2, 8)))
    expert_down = centred(key_list[15], (EXPERTS, EH, D), EH ** -0.5, 0.125, ((0, 16), (1, 8)))
    expert_ids_keys = jax.random.split(jax.random.fold_in(key_list[16], 1), ROWS // ROWS_DEV)
    expert_ids_turns = jax.random.permutation(jax.random.fold_in(key_list[16], 3), ROWS // ROWS_DEV)
    expert_ids = jax.vmap(lambda own, number: shared_out(jax.random.fold_in(key_list[16], 2), own, number, ROWS_DEV, EXPERTS, TOP, CAP, 2))(expert_ids_keys, expert_ids_turns).reshape((ROWS, TOP))
    gate_scores = jnp.clip(jnp.exp(math.log(1.0) - 2.9957323 * jax.random.uniform(key_list[17], (ROWS, TOP), jnp.float32) ** block_scale(key_list[17], (ROWS, TOP), ((0, 128),), -0.2, 0.2)), 0.05, 1.0)
    return {"queries": queries, "new_latent": new_latent, "resident": resident, "leaving": leaving, "res_len": res_len, "leave_len": leave_len, "mig_dest": mig_dest, "stream": stream, "dense_gain": dense_gain, "w_gate": w_gate, "w_up": w_up, "w_down": w_down, "moe_gain": moe_gain, "expert_gate": expert_gate, "expert_up": expert_up, "expert_down": expert_down, "expert_ids": expert_ids, "gate_scores": gate_scores}


EPS = 1e-06
ROUTE_SCALE = 2.5

def rms_scale(rows, gain):
    values = rows.astype(jnp.float32)
    mean_square = lax.optimization_barrier(jnp.mean(values * values, axis=-1, keepdims=True))
    return (values * lax.rsqrt(mean_square + EPS) * gain).astype(jnp.bfloat16)

def attend(item):
    queries, keys, lengths, newest = item
    scale = QKD ** (-0.5)
    query_f = queries.astype(jnp.float32)
    key_f = keys.astype(jnp.float32)
    new_f = newest.astype(jnp.float32)
    scores = jnp.einsum('rhl,rcl->rhc', query_f, key_f) * scale
    positions = jnp.arange(keys.shape[1], dtype=jnp.int32)
    valid = positions[None, None, :] < lengths[:, None, None]
    masked = jnp.where(valid, scores, -1e+30)
    own_score = jnp.einsum('rhl,rl->rh', query_f, new_f) * scale
    top = jnp.maximum(lax.optimization_barrier(jnp.max(masked, axis=-1)), own_score)
    expo = jnp.where(valid, jnp.exp(masked - top[..., None]), 0.0)
    own_expo = jnp.exp(own_score - top)
    total = lax.optimization_barrier(jnp.sum(expo, axis=-1)) + own_expo
    weights = (expo / total[..., None]).astype(jnp.bfloat16)
    own_weight = (own_expo / total).astype(jnp.bfloat16)
    context = jnp.einsum('rhc,rcv->rhv', weights.astype(jnp.float32), key_f[:, :, :VDIM])
    context = context + own_weight.astype(jnp.float32)[..., None] * new_f[:, None, :VDIM]
    return context.astype(jnp.bfloat16)

def arrival_index(mig_dest):
    dest = mig_dest.reshape(N_DP, N_TP, MIG).astype(jnp.int32)
    peers = jnp.arange(N_TP, dtype=jnp.int32)
    slots = jnp.arange(MIG, dtype=jnp.int32)
    match = dest[:, None, :, :] == peers[None, :, None, None]
    is_source = jnp.any(match, axis=3)
    which = lax.optimization_barrier(jnp.sum(jnp.where(match, slots, 0), axis=3)).astype(jnp.int32)
    order = (jnp.cumsum(is_source.astype(jnp.int32), axis=2) - 1).astype(jnp.int32)
    groups = jnp.arange(N_DP, dtype=jnp.int32)[:, None]
    picks = []
    for arrival in range(MIG):
        pick = is_source & (order == arrival)
        source = lax.optimization_barrier(jnp.sum(jnp.where(pick, peers, 0), axis=2)).astype(jnp.int32)
        slot = lax.optimization_barrier(jnp.sum(jnp.where(pick, which, 0), axis=2)).astype(jnp.int32)
        picks.append((groups * N_TP + source) * MIG + slot)
    return jnp.stack(picks, axis=2).reshape(-1).astype(jnp.int32)

def run_expert(item):
    rows, gate_w, up_w, down_w = item
    block = EH // N_DP
    total = jnp.zeros((rows.shape[0], D), jnp.float32)
    for part in range(N_DP):
        gate = jnp.dot(rows, gate_w[:, part * block:(part + 1) * block], preferred_element_type=jnp.float32)
        up = jnp.dot(rows, up_w[:, part * block:(part + 1) * block], preferred_element_type=jnp.float32)
        inner = (jax.nn.silu(gate) * up).astype(jnp.bfloat16)
        piece = jnp.dot(inner, down_w[part * block:(part + 1) * block], preferred_element_type=jnp.float32)
        piece = lax.optimization_barrier(piece.astype(jnp.bfloat16))
        total = total + piece.astype(jnp.float32)
    return total.astype(jnp.bfloat16)

def reference(queries, new_latent, resident, leaving, res_len, leave_len, mig_dest, stream, dense_gain, w_gate, w_up, w_down, moe_gain, expert_gate, expert_up, expert_down, expert_ids, gate_scores):
    arrive = arrival_index(mig_dest)
    arrived = leaving[arrive]
    arrive_len = leave_len.reshape(-1)[arrive]
    keys = jnp.concatenate([resident.reshape(DEVICES, STAY, CACHE, LAT), arrived[:, 0].reshape(DEVICES, MIG, CACHE, LAT)], axis=1)
    lengths = jnp.concatenate([res_len.reshape(DEVICES, STAY), arrive_len.reshape(DEVICES, MIG)], axis=1).astype(jnp.int32)
    context = lax.map(attend, (queries.reshape(DEVICES, ROWS_DEV, HEADS, LAT), keys, lengths, new_latent.reshape(DEVICES, ROWS_DEV, LAT)))
    context = context.reshape(ROWS, HEADS, VDIM)
    normed = rms_scale(stream, dense_gain)
    gate = jnp.dot(normed, w_gate, preferred_element_type=jnp.float32)
    up = jnp.dot(normed, w_up, preferred_element_type=jnp.float32)
    hidden = (jax.nn.silu(gate) * up).astype(jnp.bfloat16)
    ffn = jnp.dot(hidden, w_down, preferred_element_type=jnp.float32)
    middle = (stream.astype(jnp.float32) + ffn).astype(jnp.bfloat16)
    mixed = rms_scale(middle, moe_gain)
    ids = expert_ids.reshape(DEVICES, ROWS_DEV, TOP).astype(jnp.int32)
    hits = (ids[..., None] == jnp.arange(EXPERTS, dtype=jnp.int32)).astype(jnp.int32)
    row_hits = lax.optimization_barrier(jnp.sum(hits, axis=2)).astype(jnp.int32)
    before = (jnp.cumsum(row_hits, axis=1) - row_hits).astype(jnp.int32)
    slot = lax.optimization_barrier(jnp.sum(hits * before[:, :, None, :], axis=3)).astype(jnp.int32)
    target = (ids * CAP + slot).astype(jnp.int32)
    device_idx = jnp.arange(DEVICES, dtype=jnp.int32)[:, None, None]
    source = jnp.broadcast_to(mixed.reshape(DEVICES, ROWS_DEV, 1, D), (DEVICES, ROWS_DEV, TOP, D))
    buffer = jnp.zeros((DEVICES, EXPERTS * CAP, D), jnp.bfloat16).at[device_idx, target].set(source)
    per_expert = buffer.reshape(DEVICES, EXPERTS, CAP, D).transpose(1, 0, 2, 3).reshape(EXPERTS, DEVICES * CAP, D)
    outputs = lax.map(run_expert, (per_expert, expert_gate, expert_up, expert_down))
    back = outputs.reshape(EXPERTS, DEVICES, CAP, D).transpose(1, 0, 2, 3).reshape(DEVICES, EXPERTS * CAP, D)
    picked = jnp.take_along_axis(back, target.reshape(DEVICES, ROWS_DEV * TOP)[:, :, None], axis=1)
    picked = picked.reshape(ROWS, TOP, D).astype(jnp.float32)
    shares = gate_scores / lax.optimization_barrier(jnp.sum(gate_scores, axis=1, keepdims=True)) * ROUTE_SCALE
    routed = jnp.einsum('rk,rkd->rd', shares, picked)
    stream_out = (middle.astype(jnp.float32) + routed).astype(jnp.bfloat16)
    return (context, arrived, stream_out)
```

```python
import jax
import jax.numpy as jnp
from jax import lax
from jax.sharding import PartitionSpec as P

VDIM = 512
QKD = 192


EPS = 1e-06
ROUTE_SCALE = 2.5


def rms_scale(rows, gain):
    values = rows.astype(jnp.float32)
    mean_square = jnp.mean(values * values, axis=-1, keepdims=True)
    return (values * lax.rsqrt(mean_square + EPS) * gain).astype(jnp.bfloat16)


def attend(queries, keys, lengths, newest):
    scale = QKD ** (-0.5)
    scores = jnp.einsum("rhl,rcl->rhc", queries, keys, preferred_element_type=jnp.float32) * scale
    positions = jnp.arange(keys.shape[1])
    valid = positions[None, None, :] < lengths[:, None, None]
    masked = jnp.where(valid, scores, -1e30)
    own_score = (
        jnp.einsum("rhl,rl->rh", queries, newest, preferred_element_type=jnp.float32) * scale
    )
    top = jnp.maximum(jnp.max(masked, axis=-1), own_score)
    expo = jnp.where(valid, jnp.exp(masked - top[..., None]), 0.0)
    own_expo = jnp.exp(own_score - top)
    total = jnp.sum(expo, axis=-1) + own_expo
    weights = (expo / total[..., None]).astype(jnp.bfloat16)
    own_weight = (own_expo / total).astype(jnp.bfloat16)
    context = jnp.einsum(
        "rhc,rcv->rhv", weights, keys[:, :, :VDIM], preferred_element_type=jnp.float32
    )
    context = context + own_weight.astype(jnp.float32)[..., None] * newest[:, None, :VDIM].astype(
        jnp.float32
    )
    return context.astype(jnp.bfloat16)


def on_device(
    queries,
    new_latent,
    resident,
    leaving,
    res_len,
    leave_len,
    mig_dest,
    stream,
    dense_gain,
    w_gate,
    w_up,
    w_down,
    moe_gain,
    expert_gate,
    expert_up,
    expert_down,
    expert_ids,
    gate_scores,
):
    tp_count = lax.axis_size("tp")
    dp_count = lax.axis_size("dp")
    tp_rank = lax.axis_index("tp")
    dp_rank = lax.axis_index("dp")
    moving = leaving.shape[0]
    device = dp_rank * tp_count + tp_rank
    peers = jnp.arange(tp_count)
    own_dest = lax.dynamic_index_in_dim(mig_dest, device, 0, keepdims=False)
    outgoing = jnp.zeros((tp_count,) + leaving.shape[1:], jnp.bfloat16)
    for slot in range(moving):
        outgoing = jnp.where(
            (peers == own_dest[slot])[:, None, None, None], leaving[slot][None], outgoing
        )
    incoming = lax.all_to_all(outgoing, "tp", split_axis=0, concat_axis=0, tiled=True)
    group_dest = lax.dynamic_slice_in_dim(mig_dest, dp_rank * tp_count, tp_count, 0)
    group_len = lax.dynamic_slice_in_dim(leave_len, dp_rank * tp_count, tp_count, 0)
    match = group_dest == tp_rank
    is_source = jnp.any(match, axis=1)
    which = jnp.sum(jnp.where(match, jnp.arange(moving)[None, :], 0), axis=1)
    order = jnp.cumsum(is_source.astype(jnp.int32)) - 1
    arrivals = []
    arrival_len = []
    for arrival in range(moving):
        pick = is_source & (order == arrival)
        source = jnp.sum(jnp.where(pick, peers, 0))
        slot = jnp.sum(jnp.where(pick, which, 0))
        arrivals.append(lax.dynamic_index_in_dim(incoming, source, 0, keepdims=False))
        source_len = lax.dynamic_index_in_dim(group_len, source, 0, keepdims=False)
        arrival_len.append(lax.dynamic_index_in_dim(source_len, slot, 0, keepdims=False))
    arrived = jnp.stack(arrivals, axis=0)
    arrived_len = jnp.stack(arrival_len, axis=0)
    stay = resident.shape[0]
    context_stay = attend(queries[:stay], resident, res_len, new_latent[:stay])
    context_moved = attend(queries[stay:], arrived[:, 0], arrived_len, new_latent[stay:])
    context = jnp.concatenate([context_stay, context_moved], axis=0)
    rows_dev = stream.shape[0]
    width = stream.shape[1]
    both = ("dp", "tp")
    experts = expert_gate.shape[0] * tp_count
    shares = gate_scores / jnp.sum(gate_scores, axis=1, keepdims=True) * ROUTE_SCALE
    hits = expert_ids[:, :, None] == jnp.arange(experts)[None, None, :]
    spread = jnp.sum(jnp.where(hits, shares[:, :, None], 0.0), axis=1)
    spread = lax.all_gather(spread, both, axis=0, tiled=True)
    own_share = lax.dynamic_slice_in_dim(spread, tp_rank, 1, 1)
    normed = rms_scale(stream, dense_gain)
    blocks = lax.all_to_all(
        normed.reshape(rows_dev, dp_count, -1), "dp", split_axis=1, concat_axis=0, tiled=True
    )
    blocks = blocks.reshape(rows_dev * dp_count, -1)
    features = lax.all_gather(blocks, "tp", axis=0, tiled=True)
    gate_part = jnp.dot(features, w_gate, preferred_element_type=jnp.float32)
    up_part = jnp.dot(features, w_up, preferred_element_type=jnp.float32)
    gate = lax.psum_scatter(
        gate_part.astype(jnp.bfloat16), "dp", scatter_dimension=0, tiled=True
    ).astype(jnp.float32)
    up = lax.psum_scatter(
        up_part.astype(jnp.bfloat16), "dp", scatter_dimension=0, tiled=True
    ).astype(jnp.float32)
    hidden = (jax.nn.silu(gate) * up).astype(jnp.bfloat16)
    hidden_all = lax.all_gather(hidden, "dp", axis=0, tiled=True)
    ffn_share = lax.psum_scatter(
        jnp.dot(hidden_all, w_down, preferred_element_type=jnp.float32).astype(jnp.bfloat16),
        "tp",
        scatter_dimension=0,
        tiled=True,
    )
    ffn_rows = lax.all_to_all(
        ffn_share.reshape(dp_count, rows_dev, -1), "dp", split_axis=0, concat_axis=2, tiled=True
    ).astype(jnp.float32)
    middle = (stream.astype(jnp.float32) + ffn_rows[0]).astype(jnp.bfloat16)
    mixed = rms_scale(middle, moe_gain)
    pooled = lax.all_gather(mixed, both, axis=0, tiled=True)
    gate = jnp.dot(pooled, expert_gate[0], preferred_element_type=jnp.float32)
    up = jnp.dot(pooled, expert_up[0], preferred_element_type=jnp.float32)
    inner = jnp.where(own_share > 0.0, jax.nn.silu(gate) * up * own_share, 0.0)
    part = jnp.dot(
        inner.astype(jnp.bfloat16), expert_down[0], preferred_element_type=jnp.float32
    )
    routed = lax.psum_scatter(
        part.astype(jnp.bfloat16), both, scatter_dimension=0, tiled=True
    ).astype(jnp.float32)
    stream_out = (middle.astype(jnp.float32) + routed).astype(jnp.bfloat16)
    return (context, arrived, stream_out)


def solution(mesh):
    placed = (
        P(("dp", "tp"), None, None),
        P(("dp", "tp"), None),
        P(("dp", "tp"), None, None),
        P(("dp", "tp"), None, None, None),
        P(("dp", "tp")),
        P(),
        P(),
        P(("dp", "tp"), None),
        P(),
        P("dp", "tp"),
        P("dp", "tp"),
        P("tp", "dp"),
        P(),
        P("tp", None, "dp"),
        P("tp", None, "dp"),
        P("tp", "dp", None),
        P(("dp", "tp"), None),
        P(("dp", "tp"), None),
    )
    return jax.shard_map(
        on_device,
        mesh=mesh,
        in_specs=placed,
        out_specs=(
            P(("dp", "tp"), None, None),
            P(("dp", "tp"), None, None, None),
            P(("dp", "tp"), None),
        ),
        check_vma=False,
    )
```

```python
import functools

import jax
import jax.numpy as jnp
from jax import lax
from jax.experimental import pallas as pl
from jax.experimental.pallas import tpu as pltpu
from jax.sharding import PartitionSpec as P

MESH = pl.DeviceIdType.MESH

VDIM = 512
QKD = 192


EPS = 1e-06
ROUTE_SCALE = 2.5


def rms_scale(rows, gain):
    values = rows.astype(jnp.float32)
    mean_square = jnp.mean(values * values, axis=-1, keepdims=True)
    return (values * lax.rsqrt(mean_square + EPS) * gain).astype(jnp.bfloat16)


def attend(queries, keys, lengths, newest):
    scale = QKD ** (-0.5)
    scores = jnp.einsum("rhl,rcl->rhc", queries, keys, preferred_element_type=jnp.float32) * scale
    positions = jnp.arange(keys.shape[1])
    valid = positions[None, None, :] < lengths[:, None, None]
    masked = jnp.where(valid, scores, -1e30)
    own_score = (
        jnp.einsum("rhl,rl->rh", queries, newest, preferred_element_type=jnp.float32) * scale
    )
    top = jnp.maximum(jnp.max(masked, axis=-1), own_score)
    expo = jnp.where(valid, jnp.exp(masked - top[..., None]), 0.0)
    own_expo = jnp.exp(own_score - top)
    total = jnp.sum(expo, axis=-1) + own_expo
    weights = (expo / total[..., None]).astype(jnp.bfloat16)
    own_weight = (own_expo / total).astype(jnp.bfloat16)
    context = jnp.einsum(
        "rhc,rcv->rhv", weights, keys[:, :, :VDIM], preferred_element_type=jnp.float32
    )
    context = context + own_weight.astype(jnp.float32)[..., None] * newest[:, None, :VDIM].astype(
        jnp.float32
    )
    return context.astype(jnp.bfloat16)


HALF = 3584
OFFS = (0, 1280, 2432)
DATA = (1280, 1152, 1152)
WIDE = (1280, 1280, 1152)
ORDERS = ((0, 1, 2), (1, 2, 0), (2, 0, 1))
CUT = 640


def place():
    p, t = lax.axis_index("dp"), lax.axis_index("tp")
    return [p // 2, t // 4, t % 4], p % 2, p, t


def device(at, core):
    return (at[0] * 2 + core, at[1] * 4 + at[2])


def beside(at, axis, step):
    return [lax.rem(at[a] + 4 + step, 4) if a == axis else at[a] for a in range(3)]


class Wires:
    def __init__(self, send, recv):
        self.send, self.recv, self.used = send, recv, 0
        self.open = []

    def start(self, src, dst, peer):
        i = self.used
        self.used += 1
        copy = pltpu.make_async_remote_copy(
            src_ref=src, dst_ref=dst, send_sem=self.send.at[i], recv_sem=self.recv.at[i],
            device_id=peer, device_id_type=MESH,
        )
        copy.start()
        self.open.append(copy)
        return copy

    def close(self):
        for copy in self.open:
            copy.wait_send()


def greet(peers):
    barrier = pltpu.get_barrier_semaphore()
    for peer in peers:
        pl.semaphore_signal(barrier, inc=1, device_id=peer, device_id_type=MESH)
    pl.semaphore_wait(barrier, len(peers))


def rms(rows, gain):
    mean_square = jnp.mean(rows * rows, axis=-1, keepdims=True)
    return (rows * lax.rsqrt(mean_square + EPS) * gain).astype(jnp.bfloat16)


def picks(axes_values):
    return tuple(axes_values)


def moe_kernel(
    middle, gain, ids, scores, eg, eu, ed, out,
    wgu, wd, acc, inner, swap, swap2, swap3, swap4,
    ag0, ag1, ag2, ot0, ot1, ot2, po0, po1, po2, pt0, pt1, pt2, pr0, pr1, pr2,
    ra0, ra1, ra2, rb0, rb1, rb2, rc0, rc1, rc2, rd0, rd1, rd2,
    q0, q1, q2, qa0, qa1, qa2, qb0, qb1, qb2, qc0, qc1, qc2, qd0, qd1, qd2,
    s0, s1, s2, sa0, sa1, sa2, sb0, sb1, sb2, sc0, sc1, sc2, sd0, sd1, sd2,
    load_sem, send_sem, recv_sem, xsend, xrecv,
):
    at, core, p, t = place()
    ag, ot, po, pt, pr = (ag0, ag1, ag2), (ot0, ot1, ot2), (po0, po1, po2), (pt0, pt1, pt2), (pr0, pr1, pr2)
    loads = [
        pltpu.make_async_copy(eg, wgu.at[:, 0:256], load_sem.at[0]),
        pltpu.make_async_copy(eu, wgu.at[:, 256:512], load_sem.at[1]),
        pltpu.make_async_copy(ed.at[:, 0:HALF], wd.at[0], load_sem.at[2]),
        pltpu.make_async_copy(ed.at[:, HALF:2 * HALF], wd.at[1], load_sem.at[3]),
    ]
    for load in loads:
        load.start()
    partner = device(at, 1 - core)
    greet([partner] + [device(beside(at, a, s), core) for a in range(3) for s in (1, -1)])
    wires = Wires(send_sem, recv_sem)

    rows = middle[...].astype(jnp.float32)
    mixed = rms(rows, gain[...]).astype(jnp.float32)
    given = scores[...]
    share = given / jnp.sum(given, axis=1, keepdims=True) * ROUTE_SCALE
    lane = lax.broadcasted_iota(jnp.int32, (8, 128), 1)
    spread = jnp.zeros((8, 128), jnp.float32)
    for k in range(8):
        spread = spread + jnp.where(lane == ids[:, k:k + 1], share[:, k:k + 1], 0.0)
    high = spread.astype(jnp.bfloat16).astype(jnp.float32)
    low = (spread - high).astype(jnp.bfloat16).astype(jnp.float32)
    packed = high + pltpu.roll(low, 16, 1)
    is_one = core == 1
    swap[:, 0:HALF] = jnp.where(is_one, mixed[:, 0:HALF], mixed[:, HALF:])
    swap[:, HALF:] = packed
    over = wires.start(swap, swap2, partner)
    mine = jnp.where(is_one, mixed[:, HALF:], mixed[:, 0:HALF])
    over.wait_recv()
    theirs = swap2[:, 0:HALF]
    first = jnp.where(is_one, theirs, mine)
    second = jnp.where(is_one, mine, theirs)
    block = jnp.concatenate([first, second], axis=0).astype(jnp.bfloat16)
    other_pack = swap2[:, HALF:]
    pack = jnp.concatenate(
        [jnp.where(is_one, other_pack, packed), jnp.where(is_one, packed, other_pack)], axis=0
    ).astype(jnp.bfloat16)
    for k in range(3):
        ag[k][at[0], at[1], at[2], :, 0:DATA[k]] = block[:, OFFS[k]:OFFS[k] + DATA[k]]
    ag1[at[0], at[1], at[2], :, DATA[1]:WIDE[1]] = pack

    def spot(k, fixed):
        return tuple(fixed.get(a, slice(None)) for a in range(3))

    def cols(k, part):
        return slice(0, CUT) if part == 0 else slice(CUT, WIDE[k])

    def ring(k, axis, fixed):
        here = spot(k, fixed)
        up, down = device(beside(at, axis, 1), core), device(beside(at, axis, -1), core)
        a = wires.start(ag[k].at[here], ag[k].at[here], up)
        b = wires.start(ag[k].at[here], ag[k].at[here], down)
        return a, b

    def forward(k, axis, fixed, pair):
        up, down = device(beside(at, axis, 1), core), device(beside(at, axis, -1), core)
        below, above = dict(fixed), dict(fixed)
        below[axis], above[axis] = lax.rem(at[axis] + 3, 4), lax.rem(at[axis] + 1, 4)
        pair[0].wait_recv()
        s = spot(k, below) + (slice(None), cols(k, 0))
        a = wires.start(ag[k].at[s], ag[k].at[s], up)
        pair[1].wait_recv()
        s = spot(k, above) + (slice(None), cols(k, 1))
        b = wires.start(ag[k].at[s], ag[k].at[s], down)
        return a, b

    own = [{a: at[a] for a in range(3)} for _ in range(3)]
    pairs = [ring(k, ORDERS[k][0], own[k]) for k in range(3)]
    pairs = [forward(k, ORDERS[k][0], own[k], pairs[k]) for k in range(3)]
    second_pairs, third = [None] * 3, [[], [], []]
    for k in range(3):
        a1, a2, a3 = ORDERS[k]
        for c in pairs[k]:
            c.wait_recv()
        fixed = {a2: at[a2], a3: at[a3]}
        second_pairs[k] = ring(k, a2, fixed)
        third[k].append((fixed, ring(k, a3, fixed)))
    done2 = [None] * 3
    for k in range(3):
        a1, a2, a3 = ORDERS[k]
        fixed = {a2: at[a2], a3: at[a3]}
        done2[k] = forward(k, a2, fixed, second_pairs[k])
        for step in (1, 3):
            fixed = {a2: lax.rem(at[a2] + step, 4), a3: at[a3]}
            third[k].append((fixed, ring(k, a3, fixed)))
    last = [[], [], []]
    for k in range(3):
        a1, a2, a3 = ORDERS[k]
        for c in done2[k]:
            c.wait_recv()
        fixed = {a2: lax.rem(at[a2] + 2, 4), a3: at[a3]}
        third[k].append((fixed, ring(k, a3, fixed)))

    def plane(k, step):
        return spot(k, {ORDERS[k][2]: lax.rem(at[ORDERS[k][2]] + step, 4)})

    across = [[None] * 4 for _ in range(3)]

    def hand(k, step):
        s = plane(k, step)
        across[k][step] = wires.start(ag[k].at[s], ot[k].at[s], partner)

    for k in range(3):
        hand(k, 0)
    loads[0].wait()
    loads[1].wait()

    def product(bufs, half, k, step, fresh):
        s = plane(k, step)
        left = bufs[k][s + (slice(None), slice(0, DATA[k]))].reshape(256, DATA[k])
        base = pl.multiple_of(half * HALF + OFFS[k], 128)
        part = jnp.dot(left, wgu[pl.ds(base, DATA[k]), :], preferred_element_type=jnp.float32)
        part = part.reshape(4, 4, 16, 512)
        acc[s] = acc[s] + part

    acc[...] = jnp.zeros_like(acc)
    for k in range(3):
        product(ag, core, k, 0, False)
    for n in range(4):
        for k in range(3):
            fixed, pair = third[k][n]
            last[k].append(forward(k, ORDERS[k][2], fixed, pair))
    for k in range(3):
        hand(k, 1)
        hand(k, 3)

    def side(n, _):
        for k in range(3):
            product(ag, core, k, 2 * n + 1, False)
        return _

    lax.fori_loop(0, 2, side, 0)
    for k in range(3):
        for step in (0, 1, 3):
            across[k][step].wait_recv()

    def side_other(n, _):
        for k in range(3):
            product(ot, 1 - core, k, n + n // 2, False)
        return _

    lax.fori_loop(0, 3, side_other, 0)
    for k in range(3):
        for pair in last[k]:
            for c in pair:
                c.wait_recv()
        hand(k, 2)
    for k in range(3):
        product(ag, core, k, 2, False)
    for k in range(3):
        across[k][2].wait_recv()
        product(ot, 1 - core, k, 2, False)

    lane = lax.broadcasted_iota(jnp.int32, (256, 128), 1)

    def activate(n, _):
        both = acc[n].reshape(256, 512)
        gate, up = both[:, 0:256], both[:, 256:512]
        packs = ag1[n, :, :, :, DATA[1]:WIDE[1]].reshape(256, 128).astype(jnp.float32)
        keep = (lane == t) | (lane == t + 16)
        weight = jnp.sum(jnp.where(keep, packs, 0.0), axis=1, keepdims=True)
        value = gate / (1.0 + jnp.exp(-gate)) * up * weight
        inner[n] = value.astype(jnp.bfloat16).reshape(4, 4, 16, 256)
        return _

    lax.fori_loop(0, 4, activate, 0)
    loads[2].wait()
    loads[3].wait()

    def group(k, step):
        a1 = ORDERS[k][0]
        return spot(k, {a1: lax.rem(at[a1] + step, 4)})

    def trade(k, n, step):
        s = group(k, step)
        return pltpu.make_async_remote_copy(
            src_ref=pt[k].at[s], dst_ref=pr[k].at[s], send_sem=xsend.at[k, n], recv_sem=xrecv.at[k, n],
            device_id=partner, device_id_type=MESH,
        )

    def step_of(n):
        return lax.rem(n * 3 + 2, 4) if not isinstance(n, int) else (n * 3 + 2) % 4

    def expand(n, _):
        for k in range(3):
            s = group(k, step_of(n))
            left = inner[s].reshape(256, 256)
            part = jnp.dot(left, wd[1 - core, :, OFFS[k]:OFFS[k] + DATA[k]], preferred_element_type=jnp.float32)
            pt[k][s] = part.astype(jnp.bfloat16).reshape(4, 4, 16, DATA[k])
            trade(k, n, step_of(n)).start()
            part = jnp.dot(left, wd[core, :, OFFS[k]:OFFS[k] + DATA[k]], preferred_element_type=jnp.float32)
            po[k][s] = part.astype(jnp.bfloat16).reshape(4, 4, 16, DATA[k])
        return _

    lax.fori_loop(0, 4, expand, 0)

    ra, rb, rc, rd = (ra0, ra1, ra2), (rb0, rb1, rb2), (rc0, rc1, rc2), (rd0, rd1, rd2)

    def dcols(k, part):
        return slice(0, CUT) if part == 0 else slice(CUT, DATA[k])

    def meet(k, n):
        trade(k, n, step_of(n)).wait_recv()
        s = group(k, step_of(n))
        po[k][s] = (po[k][s].astype(jnp.float32) + pr[k][s].astype(jnp.float32)).astype(jnp.bfloat16)

    def scatter(bufs, index, axis_of, ra, rb, rc, rd, prepare):
        state = []
        for k in range(3):
            up, down = device(beside(at, axis_of(k), 1), core), device(beside(at, axis_of(k), -1), core)
            prepare(k, 2)
            src = index(k, 2)
            a = wires.start(bufs[k].at[src + (slice(None), dcols(k, 0))], ra[k], down)
            b = wires.start(bufs[k].at[src + (slice(None), dcols(k, 1))], rb[k], up)
            state.append([up, down, a, b])
        for k in range(3):
            up, down, a, b = state[k]
            prepare(k, 1)
            prepare(k, 3)
            left, right = index(k, 3), index(k, 1)
            c = wires.start(
                bufs[k].at[left + (slice(None), dcols(k, 1))], rc[k].at[(slice(None),) * (len(rc[k].shape) - 1) + (dcols(k, 1),)], down
            )
            d = wires.start(
                bufs[k].at[right + (slice(None), dcols(k, 0))], rd[k].at[(slice(None),) * (len(rd[k].shape) - 1) + (dcols(k, 0),)], up
            )
            state[k] += [c, d]
        for k in range(3):
            up, down, a, b, c, d = state[k]
            left, right = index(k, 3), index(k, 1)
            a.wait_recv()
            s = left + (slice(None), dcols(k, 0))
            bufs[k][s] = (bufs[k][s].astype(jnp.float32) + ra[k][...].astype(jnp.float32)).astype(jnp.bfloat16)
            e = wires.start(bufs[k].at[s], rc[k].at[(slice(None),) * (len(rc[k].shape) - 1) + (dcols(k, 0),)], down)
            b.wait_recv()
            s = right + (slice(None), dcols(k, 1))
            bufs[k][s] = (bufs[k][s].astype(jnp.float32) + rb[k][...].astype(jnp.float32)).astype(jnp.bfloat16)
            f = wires.start(bufs[k].at[s], rd[k].at[(slice(None),) * (len(rd[k].shape) - 1) + (dcols(k, 1),)], up)
            state[k] += [e, f]
        sums = []
        for k in range(3):
            prepare(k, 0)
            for c in state[k][4:]:
                c.wait_recv()
            yield k, (
                bufs[k][index(k, 0)].astype(jnp.float32)
                + rc[k][...].astype(jnp.float32)
                + rd[k][...].astype(jnp.float32)
            )

    turn = {2: 0, 1: 1, 3: 3, 0: 2}
    assert all(step_of(n) == s for s, n in turn.items())
    q = (q0, q1, q2)
    for k, total in scatter(
        po, group, lambda k: ORDERS[k][0], ra, rb, rc, rd, lambda k, step: meet(k, turn[step])
    ):
        q[k][...] = total.astype(jnp.bfloat16)

    def group2(k, step):
        a1, a2, a3 = ORDERS[k]
        rest = [a for a in range(3) if a != a1]
        return tuple(lax.rem(at[a] + step, 4) if a == a2 else slice(None) for a in rest)

    s_ = (s0, s1, s2)
    for k, total in scatter(
        q, group2, lambda k: ORDERS[k][1], (qa0, qa1, qa2), (qb0, qb1, qb2), (qc0, qc1, qc2), (qd0, qd1, qd2), lambda k, step: None
    ):
        s_[k][...] = total.astype(jnp.bfloat16)

    def group3(k, step):
        return (lax.rem(at[ORDERS[k][2]] + step, 4),)

    for k, total in scatter(
        s_, group3, lambda k: ORDERS[k][2], (sa0, sa1, sa2), (sb0, sb1, sb2), (sc0, sc1, sc2), (sd0, sd1, sd2), lambda k, step: None
    ):
        swap3[:, :, OFFS[k]:OFFS[k] + DATA[k]] = total.reshape(2, 8, DATA[k])
    over = wires.start(swap3.at[1 - core], swap4, partner)
    over.wait_recv()
    lead = jnp.where(is_one, swap4[...], swap3[0])
    tail = jnp.where(is_one, swap3[1], swap4[...])
    out[:, 0:HALF] = (rows[:, 0:HALF] + lead).astype(jnp.bfloat16)
    out[:, HALF:] = (rows[:, HALF:] + tail).astype(jnp.bfloat16)
    for k in range(3):
        for n in range(4):
            trade(k, n, step_of(n)).wait_send()
    wires.close()


def moe(middle, gain, ids, scores, eg, eu, ed):
    vm, an = pl.BlockSpec(memory_space=pltpu.VMEM), pl.BlockSpec(memory_space=pl.ANY)
    bf = jnp.bfloat16

    def three(shape, widths):
        return [pltpu.VMEM(shape + (w,), bf) for w in widths]

    lead, rest = (CUT,) * 3, tuple(w - CUT for w in DATA)
    cube, face, line, row = (4, 4, 4, 16), (4, 4, 16), (4, 16), (16,)
    scratch = [
        pltpu.VMEM((7168, 512), bf),
        pltpu.VMEM((2, 256, HALF), bf),
        pltpu.VMEM((4, 4, 4, 16, 512), jnp.float32),
        pltpu.VMEM((4, 4, 4, 16, 256), bf),
        pltpu.VMEM((8, HALF + 128), jnp.float32),
        pltpu.VMEM((8, HALF + 128), jnp.float32),
        pltpu.VMEM((2, 8, HALF), jnp.float32),
        pltpu.VMEM((8, HALF), jnp.float32),
    ]
    scratch += three(cube, WIDE) + three(cube, WIDE)
    scratch += three(cube, DATA) + three(cube, DATA) + three(cube, DATA)
    scratch += three(face, lead) + three(face, rest) + three(face, DATA) + three(face, DATA)
    for shape in (line, row):
        big = (4,) + shape
        scratch += three(big, DATA) + three(shape, lead) + three(shape, rest) + three(shape, DATA) + three(shape, DATA)
    scratch += [
        pltpu.SemaphoreType.DMA((4,)),
        pltpu.SemaphoreType.DMA((160,)),
        pltpu.SemaphoreType.DMA((160,)),
        pltpu.SemaphoreType.DMA((3, 4)),
        pltpu.SemaphoreType.DMA((3, 4)),
    ]
    return pl.pallas_call(
        moe_kernel,
        out_shape=jax.ShapeDtypeStruct((8, 7168), bf),
        in_specs=[vm, vm, vm, vm, an, an, an],
        out_specs=vm,
        scratch_shapes=scratch,
        compiler_params=pltpu.CompilerParams(
            collective_id=1, has_side_effects=True, vmem_limit_bytes=67043328
        ),
        name="experts",
    )(middle, gain, ids, scores, eg, eu, ed)


def on_device(
    queries,
    new_latent,
    resident,
    leaving,
    res_len,
    leave_len,
    mig_dest,
    stream,
    dense_gain,
    w_gate,
    w_up,
    w_down,
    moe_gain,
    expert_gate,
    expert_up,
    expert_down,
    expert_ids,
    gate_scores,
):
    tp_count = lax.axis_size("tp")
    dp_count = lax.axis_size("dp")
    tp_rank = lax.axis_index("tp")
    dp_rank = lax.axis_index("dp")
    moving = leaving.shape[0]
    device = dp_rank * tp_count + tp_rank
    peers = jnp.arange(tp_count)
    own_dest = lax.dynamic_index_in_dim(mig_dest, device, 0, keepdims=False)
    outgoing = jnp.zeros((tp_count,) + leaving.shape[1:], jnp.bfloat16)
    for slot in range(moving):
        outgoing = jnp.where(
            (peers == own_dest[slot])[:, None, None, None], leaving[slot][None], outgoing
        )
    incoming = lax.all_to_all(outgoing, "tp", split_axis=0, concat_axis=0, tiled=True)
    group_dest = lax.dynamic_slice_in_dim(mig_dest, dp_rank * tp_count, tp_count, 0)
    group_len = lax.dynamic_slice_in_dim(leave_len, dp_rank * tp_count, tp_count, 0)
    match = group_dest == tp_rank
    is_source = jnp.any(match, axis=1)
    which = jnp.sum(jnp.where(match, jnp.arange(moving)[None, :], 0), axis=1)
    order = jnp.cumsum(is_source.astype(jnp.int32)) - 1
    arrivals = []
    arrival_len = []
    for arrival in range(moving):
        pick = is_source & (order == arrival)
        source = jnp.sum(jnp.where(pick, peers, 0))
        slot = jnp.sum(jnp.where(pick, which, 0))
        arrivals.append(lax.dynamic_index_in_dim(incoming, source, 0, keepdims=False))
        source_len = lax.dynamic_index_in_dim(group_len, source, 0, keepdims=False)
        arrival_len.append(lax.dynamic_index_in_dim(source_len, slot, 0, keepdims=False))
    arrived = jnp.stack(arrivals, axis=0)
    arrived_len = jnp.stack(arrival_len, axis=0)
    stay = resident.shape[0]
    context_stay = attend(queries[:stay], resident, res_len, new_latent[:stay])
    context_moved = attend(queries[stay:], arrived[:, 0], arrived_len, new_latent[stay:])
    context = jnp.concatenate([context_stay, context_moved], axis=0)
    rows_dev = stream.shape[0]
    width = stream.shape[1]
    both = ("dp", "tp")
    normed = rms_scale(stream, dense_gain)
    blocks = lax.all_to_all(
        normed.reshape(rows_dev, dp_count, -1), "dp", split_axis=1, concat_axis=0, tiled=True
    )
    blocks = blocks.reshape(rows_dev * dp_count, -1)
    features = lax.all_gather(blocks, "tp", axis=0, tiled=True)
    gate_part = jnp.dot(features, w_gate, preferred_element_type=jnp.float32)
    up_part = jnp.dot(features, w_up, preferred_element_type=jnp.float32)
    gate = lax.psum_scatter(
        gate_part.astype(jnp.bfloat16), "dp", scatter_dimension=0, tiled=True
    ).astype(jnp.float32)
    up = lax.psum_scatter(
        up_part.astype(jnp.bfloat16), "dp", scatter_dimension=0, tiled=True
    ).astype(jnp.float32)
    hidden = (jax.nn.silu(gate) * up).astype(jnp.bfloat16)
    hidden_all = lax.all_gather(hidden, "dp", axis=0, tiled=True)
    ffn_share = lax.psum_scatter(
        jnp.dot(hidden_all, w_down, preferred_element_type=jnp.float32).astype(jnp.bfloat16),
        "tp",
        scatter_dimension=0,
        tiled=True,
    )
    ffn_rows = lax.all_to_all(
        ffn_share.reshape(dp_count, rows_dev, -1), "dp", split_axis=0, concat_axis=2, tiled=True
    ).astype(jnp.float32)
    middle = (stream.astype(jnp.float32) + ffn_rows[0]).astype(jnp.bfloat16)
    stream_out = moe(
        middle, moe_gain[None], expert_ids, gate_scores, expert_gate[0], expert_up[0], expert_down[0]
    )
    return (context, arrived, stream_out)


def solution(mesh):
    placed = (
        P(("dp", "tp"), None, None),
        P(("dp", "tp"), None),
        P(("dp", "tp"), None, None),
        P(("dp", "tp"), None, None, None),
        P(("dp", "tp")),
        P(),
        P(),
        P(("dp", "tp"), None),
        P(),
        P("dp", "tp"),
        P("dp", "tp"),
        P("tp", "dp"),
        P(),
        P("tp", None, "dp"),
        P("tp", None, "dp"),
        P("tp", "dp", None),
        P(("dp", "tp"), None),
        P(("dp", "tp"), None),
    )
    return jax.shard_map(
        on_device,
        mesh=mesh,
        in_specs=placed,
        out_specs=(
            P(("dp", "tp"), None, None),
            P(("dp", "tp"), None, None, None),
            P(("dp", "tp"), None),
        ),
        check_vma=False,
    )
```

```python
import functools

import jax
import jax.numpy as jnp
from jax import lax
from jax.experimental import pallas as pl
from jax.experimental.pallas import tpu as pltpu
from jax.sharding import PartitionSpec as P

MESH = pl.DeviceIdType.MESH

VDIM = 512
QKD = 192


EPS = 1e-06
ROUTE_SCALE = 2.5


def attend(queries, keys, lengths, newest):
    scale = QKD ** (-0.5)
    scores = jnp.einsum("rhl,rcl->rhc", queries, keys, preferred_element_type=jnp.float32) * scale
    positions = jnp.arange(keys.shape[1])
    valid = positions[None, None, :] < lengths[:, None, None]
    masked = jnp.where(valid, scores, -1e30)
    own_score = (
        jnp.einsum("rhl,rl->rh", queries, newest, preferred_element_type=jnp.float32) * scale
    )
    top = jnp.maximum(jnp.max(masked, axis=-1), own_score)
    expo = jnp.where(valid, jnp.exp(masked - top[..., None]), 0.0)
    own_expo = jnp.exp(own_score - top)
    total = jnp.sum(expo, axis=-1) + own_expo
    weights = (expo / total[..., None]).astype(jnp.bfloat16)
    own_weight = (own_expo / total).astype(jnp.bfloat16)
    context = jnp.einsum(
        "rhc,rcv->rhv", weights, keys[:, :, :VDIM], preferred_element_type=jnp.float32
    )
    context = context + own_weight.astype(jnp.float32)[..., None] * newest[:, None, :VDIM].astype(
        jnp.float32
    )
    return context.astype(jnp.bfloat16)


HALF = 3584
OFFS = (0, 1280, 2432)
DATA = (1280, 1152, 1152)
WIDE = (1280, 1280, 1152)
ORDERS = ((0, 1, 2), (1, 2, 0), (2, 0, 1))
CUT = 640


def place():
    p, t = lax.axis_index("dp"), lax.axis_index("tp")
    return [p // 2, t // 4, t % 4], p % 2, p, t


def device(at, core):
    return (at[0] * 2 + core, at[1] * 4 + at[2])


def beside(at, axis, step):
    return [lax.rem(at[a] + 4 + step, 4) if a == axis else at[a] for a in range(3)]


class Wires:
    def __init__(self, send, recv):
        self.send, self.recv, self.used = send, recv, 0
        self.open = []

    def start(self, src, dst, peer):
        i = self.used
        self.used += 1
        copy = pltpu.make_async_remote_copy(
            src_ref=src, dst_ref=dst, send_sem=self.send.at[i], recv_sem=self.recv.at[i],
            device_id=peer, device_id_type=MESH,
        )
        copy.start()
        self.open.append(copy)
        return copy

    def close(self):
        for copy in self.open:
            copy.wait_send()


def greet(peers):
    barrier = pltpu.get_barrier_semaphore()
    for peer in peers:
        pl.semaphore_signal(barrier, inc=1, device_id=peer, device_id_type=MESH)
    pl.semaphore_wait(barrier, len(peers))


def rms(rows, gain):
    mean_square = jnp.mean(rows * rows, axis=-1, keepdims=True)
    return (rows * lax.rsqrt(mean_square + EPS) * gain).astype(jnp.bfloat16)


def picks(axes_values):
    return tuple(axes_values)


def moe_kernel(
    middle, gain, ids, scores, eg, eu, ed, out,
    wgu, wd, acc, inner, swap, swap2, swap3, swap4,
    ag0, ag1, ag2, ot0, ot1, ot2, po0, po1, po2, pt0, pt1, pt2, pr0, pr1, pr2,
    ra0, ra1, ra2, rb0, rb1, rb2, rc0, rc1, rc2, rd0, rd1, rd2,
    q0, q1, q2, qa0, qa1, qa2, qb0, qb1, qb2, qc0, qc1, qc2, qd0, qd1, qd2,
    s0, s1, s2, sa0, sa1, sa2, sb0, sb1, sb2, sc0, sc1, sc2, sd0, sd1, sd2,
    load_sem, send_sem, recv_sem, xsend, xrecv,
):
    at, core, p, t = place()
    ag, ot, po, pt, pr = (ag0, ag1, ag2), (ot0, ot1, ot2), (po0, po1, po2), (pt0, pt1, pt2), (pr0, pr1, pr2)
    loads = [
        pltpu.make_async_copy(eg, wgu.at[:, 0:256], load_sem.at[0]),
        pltpu.make_async_copy(eu, wgu.at[:, 256:512], load_sem.at[1]),
        pltpu.make_async_copy(ed.at[:, 0:HALF], wd.at[0], load_sem.at[2]),
        pltpu.make_async_copy(ed.at[:, HALF:2 * HALF], wd.at[1], load_sem.at[3]),
    ]
    for load in loads:
        load.start()
    partner = device(at, 1 - core)
    greet([partner] + [device(beside(at, a, s), core) for a in range(3) for s in (1, -1)])
    wires = Wires(send_sem, recv_sem)

    rows = middle[...].astype(jnp.float32)
    mixed = rms(rows, gain[...]).astype(jnp.float32)
    given = scores[...]
    share = given / jnp.sum(given, axis=1, keepdims=True) * ROUTE_SCALE
    lane = lax.broadcasted_iota(jnp.int32, (8, 128), 1)
    spread = jnp.zeros((8, 128), jnp.float32)
    for k in range(8):
        spread = spread + jnp.where(lane == ids[:, k:k + 1], share[:, k:k + 1], 0.0)
    high = spread.astype(jnp.bfloat16).astype(jnp.float32)
    low = (spread - high).astype(jnp.bfloat16).astype(jnp.float32)
    packed = high + pltpu.roll(low, 16, 1)
    is_one = core == 1
    swap[:, 0:HALF] = jnp.where(is_one, mixed[:, 0:HALF], mixed[:, HALF:])
    swap[:, HALF:] = packed
    over = wires.start(swap, swap2, partner)
    mine = jnp.where(is_one, mixed[:, HALF:], mixed[:, 0:HALF])
    over.wait_recv()
    theirs = swap2[:, 0:HALF]
    first = jnp.where(is_one, theirs, mine)
    second = jnp.where(is_one, mine, theirs)
    block = jnp.concatenate([first, second], axis=0).astype(jnp.bfloat16)
    other_pack = swap2[:, HALF:]
    pack = jnp.concatenate(
        [jnp.where(is_one, other_pack, packed), jnp.where(is_one, packed, other_pack)], axis=0
    ).astype(jnp.bfloat16)
    for k in range(3):
        ag[k][at[0], at[1], at[2], :, 0:DATA[k]] = block[:, OFFS[k]:OFFS[k] + DATA[k]]
    ag1[at[0], at[1], at[2], :, DATA[1]:WIDE[1]] = pack

    def spot(k, fixed):
        return tuple(fixed.get(a, slice(None)) for a in range(3))

    def cols(k, part):
        return slice(0, CUT) if part == 0 else slice(CUT, WIDE[k])

    def ring(k, axis, fixed):
        here = spot(k, fixed)
        up, down = device(beside(at, axis, 1), core), device(beside(at, axis, -1), core)
        a = wires.start(ag[k].at[here], ag[k].at[here], up)
        b = wires.start(ag[k].at[here], ag[k].at[here], down)
        return a, b

    def forward(k, axis, fixed, pair):
        up, down = device(beside(at, axis, 1), core), device(beside(at, axis, -1), core)
        below, above = dict(fixed), dict(fixed)
        below[axis], above[axis] = lax.rem(at[axis] + 3, 4), lax.rem(at[axis] + 1, 4)
        pair[0].wait_recv()
        s = spot(k, below) + (slice(None), cols(k, 0))
        a = wires.start(ag[k].at[s], ag[k].at[s], up)
        pair[1].wait_recv()
        s = spot(k, above) + (slice(None), cols(k, 1))
        b = wires.start(ag[k].at[s], ag[k].at[s], down)
        return a, b

    own = [{a: at[a] for a in range(3)} for _ in range(3)]
    pairs = [ring(k, ORDERS[k][0], own[k]) for k in range(3)]
    pairs = [forward(k, ORDERS[k][0], own[k], pairs[k]) for k in range(3)]
    second_pairs, third = [None] * 3, [[], [], []]
    for k in range(3):
        a1, a2, a3 = ORDERS[k]
        for c in pairs[k]:
            c.wait_recv()
        fixed = {a2: at[a2], a3: at[a3]}
        second_pairs[k] = ring(k, a2, fixed)
        third[k].append((fixed, ring(k, a3, fixed)))
    done2 = [None] * 3
    for k in range(3):
        a1, a2, a3 = ORDERS[k]
        fixed = {a2: at[a2], a3: at[a3]}
        done2[k] = forward(k, a2, fixed, second_pairs[k])
        for step in (1, 3):
            fixed = {a2: lax.rem(at[a2] + step, 4), a3: at[a3]}
            third[k].append((fixed, ring(k, a3, fixed)))
    last = [[], [], []]
    for k in range(3):
        a1, a2, a3 = ORDERS[k]
        for c in done2[k]:
            c.wait_recv()
        fixed = {a2: lax.rem(at[a2] + 2, 4), a3: at[a3]}
        third[k].append((fixed, ring(k, a3, fixed)))

    def plane(k, step):
        return spot(k, {ORDERS[k][2]: lax.rem(at[ORDERS[k][2]] + step, 4)})

    across = [[None] * 4 for _ in range(3)]

    def hand(k, step):
        s = plane(k, step)
        across[k][step] = wires.start(ag[k].at[s], ot[k].at[s], partner)

    for k in range(3):
        hand(k, 0)
    loads[0].wait()
    loads[1].wait()

    def product(bufs, half, k, step, fresh):
        s = plane(k, step)
        left = bufs[k][s + (slice(None), slice(0, DATA[k]))].reshape(256, DATA[k])
        base = pl.multiple_of(half * HALF + OFFS[k], 128)
        part = jnp.dot(left, wgu[pl.ds(base, DATA[k]), :], preferred_element_type=jnp.float32)
        part = part.reshape(4, 4, 16, 512)
        acc[s] = acc[s] + part

    acc[...] = jnp.zeros_like(acc)
    for k in range(3):
        product(ag, core, k, 0, False)
    for n in range(4):
        for k in range(3):
            fixed, pair = third[k][n]
            last[k].append(forward(k, ORDERS[k][2], fixed, pair))
    for k in range(3):
        hand(k, 1)
        hand(k, 3)

    def side(n, _):
        for k in range(3):
            product(ag, core, k, 2 * n + 1, False)
        return _

    lax.fori_loop(0, 2, side, 0)
    for k in range(3):
        for step in (0, 1, 3):
            across[k][step].wait_recv()

    def side_other(n, _):
        for k in range(3):
            product(ot, 1 - core, k, n + n // 2, False)
        return _

    lax.fori_loop(0, 3, side_other, 0)
    for k in range(3):
        for pair in last[k]:
            for c in pair:
                c.wait_recv()
        hand(k, 2)
    for k in range(3):
        product(ag, core, k, 2, False)
    for k in range(3):
        across[k][2].wait_recv()
        product(ot, 1 - core, k, 2, False)

    lane = lax.broadcasted_iota(jnp.int32, (256, 128), 1)

    def activate(n, _):
        both = acc[n].reshape(256, 512)
        gate, up = both[:, 0:256], both[:, 256:512]
        packs = ag1[n, :, :, :, DATA[1]:WIDE[1]].reshape(256, 128).astype(jnp.float32)
        keep = (lane == t) | (lane == t + 16)
        weight = jnp.sum(jnp.where(keep, packs, 0.0), axis=1, keepdims=True)
        value = gate / (1.0 + jnp.exp(-gate)) * up * weight
        inner[n] = value.astype(jnp.bfloat16).reshape(4, 4, 16, 256)
        return _

    lax.fori_loop(0, 4, activate, 0)
    loads[2].wait()
    loads[3].wait()

    def group(k, step):
        a1 = ORDERS[k][0]
        return spot(k, {a1: lax.rem(at[a1] + step, 4)})

    def trade(k, n, step):
        s = group(k, step)
        return pltpu.make_async_remote_copy(
            src_ref=pt[k].at[s], dst_ref=pr[k].at[s], send_sem=xsend.at[k, n], recv_sem=xrecv.at[k, n],
            device_id=partner, device_id_type=MESH,
        )

    def step_of(n):
        return lax.rem(n * 3 + 2, 4) if not isinstance(n, int) else (n * 3 + 2) % 4

    def expand(n, _):
        for k in range(3):
            s = group(k, step_of(n))
            left = inner[s].reshape(256, 256)
            part = jnp.dot(left, wd[1 - core, :, OFFS[k]:OFFS[k] + DATA[k]], preferred_element_type=jnp.float32)
            pt[k][s] = part.astype(jnp.bfloat16).reshape(4, 4, 16, DATA[k])
            trade(k, n, step_of(n)).start()
            part = jnp.dot(left, wd[core, :, OFFS[k]:OFFS[k] + DATA[k]], preferred_element_type=jnp.float32)
            po[k][s] = part.astype(jnp.bfloat16).reshape(4, 4, 16, DATA[k])
        return _

    lax.fori_loop(0, 4, expand, 0)

    ra, rb, rc, rd = (ra0, ra1, ra2), (rb0, rb1, rb2), (rc0, rc1, rc2), (rd0, rd1, rd2)

    def dcols(k, part):
        return slice(0, CUT) if part == 0 else slice(CUT, DATA[k])

    def meet(k, n):
        trade(k, n, step_of(n)).wait_recv()
        s = group(k, step_of(n))
        po[k][s] = (po[k][s].astype(jnp.float32) + pr[k][s].astype(jnp.float32)).astype(jnp.bfloat16)

    def scatter(bufs, index, axis_of, ra, rb, rc, rd, prepare):
        state = []
        for k in range(3):
            up, down = device(beside(at, axis_of(k), 1), core), device(beside(at, axis_of(k), -1), core)
            prepare(k, 2)
            src = index(k, 2)
            a = wires.start(bufs[k].at[src + (slice(None), dcols(k, 0))], ra[k], down)
            b = wires.start(bufs[k].at[src + (slice(None), dcols(k, 1))], rb[k], up)
            state.append([up, down, a, b])
        for k in range(3):
            up, down, a, b = state[k]
            prepare(k, 1)
            prepare(k, 3)
            left, right = index(k, 3), index(k, 1)
            c = wires.start(
                bufs[k].at[left + (slice(None), dcols(k, 1))], rc[k].at[(slice(None),) * (len(rc[k].shape) - 1) + (dcols(k, 1),)], down
            )
            d = wires.start(
                bufs[k].at[right + (slice(None), dcols(k, 0))], rd[k].at[(slice(None),) * (len(rd[k].shape) - 1) + (dcols(k, 0),)], up
            )
            state[k] += [c, d]
        for k in range(3):
            up, down, a, b, c, d = state[k]
            left, right = index(k, 3), index(k, 1)
            a.wait_recv()
            s = left + (slice(None), dcols(k, 0))
            bufs[k][s] = (bufs[k][s].astype(jnp.float32) + ra[k][...].astype(jnp.float32)).astype(jnp.bfloat16)
            e = wires.start(bufs[k].at[s], rc[k].at[(slice(None),) * (len(rc[k].shape) - 1) + (dcols(k, 0),)], down)
            b.wait_recv()
            s = right + (slice(None), dcols(k, 1))
            bufs[k][s] = (bufs[k][s].astype(jnp.float32) + rb[k][...].astype(jnp.float32)).astype(jnp.bfloat16)
            f = wires.start(bufs[k].at[s], rd[k].at[(slice(None),) * (len(rd[k].shape) - 1) + (dcols(k, 1),)], up)
            state[k] += [e, f]
        sums = []
        for k in range(3):
            prepare(k, 0)
            for c in state[k][4:]:
                c.wait_recv()
            yield k, (
                bufs[k][index(k, 0)].astype(jnp.float32)
                + rc[k][...].astype(jnp.float32)
                + rd[k][...].astype(jnp.float32)
            )

    turn = {2: 0, 1: 1, 3: 3, 0: 2}
    assert all(step_of(n) == s for s, n in turn.items())
    q = (q0, q1, q2)
    for k, total in scatter(
        po, group, lambda k: ORDERS[k][0], ra, rb, rc, rd, lambda k, step: meet(k, turn[step])
    ):
        q[k][...] = total.astype(jnp.bfloat16)

    def group2(k, step):
        a1, a2, a3 = ORDERS[k]
        rest = [a for a in range(3) if a != a1]
        return tuple(lax.rem(at[a] + step, 4) if a == a2 else slice(None) for a in rest)

    s_ = (s0, s1, s2)
    for k, total in scatter(
        q, group2, lambda k: ORDERS[k][1], (qa0, qa1, qa2), (qb0, qb1, qb2), (qc0, qc1, qc2), (qd0, qd1, qd2), lambda k, step: None
    ):
        s_[k][...] = total.astype(jnp.bfloat16)

    def group3(k, step):
        return (lax.rem(at[ORDERS[k][2]] + step, 4),)

    for k, total in scatter(
        s_, group3, lambda k: ORDERS[k][2], (sa0, sa1, sa2), (sb0, sb1, sb2), (sc0, sc1, sc2), (sd0, sd1, sd2), lambda k, step: None
    ):
        swap3[:, :, OFFS[k]:OFFS[k] + DATA[k]] = total.reshape(2, 8, DATA[k])
    over = wires.start(swap3.at[1 - core], swap4, partner)
    over.wait_recv()
    lead = jnp.where(is_one, swap4[...], swap3[0])
    tail = jnp.where(is_one, swap3[1], swap4[...])
    out[:, 0:HALF] = (rows[:, 0:HALF] + lead).astype(jnp.bfloat16)
    out[:, HALF:] = (rows[:, HALF:] + tail).astype(jnp.bfloat16)
    for k in range(3):
        for n in range(4):
            trade(k, n, step_of(n)).wait_send()
    wires.close()


def moe(middle, gain, ids, scores, eg, eu, ed):
    vm, an = pl.BlockSpec(memory_space=pltpu.VMEM), pl.BlockSpec(memory_space=pl.ANY)
    bf = jnp.bfloat16

    def three(shape, widths):
        return [pltpu.VMEM(shape + (w,), bf) for w in widths]

    lead, rest = (CUT,) * 3, tuple(w - CUT for w in DATA)
    cube, face, line, row = (4, 4, 4, 16), (4, 4, 16), (4, 16), (16,)
    scratch = [
        pltpu.VMEM((7168, 512), bf),
        pltpu.VMEM((2, 256, HALF), bf),
        pltpu.VMEM((4, 4, 4, 16, 512), jnp.float32),
        pltpu.VMEM((4, 4, 4, 16, 256), bf),
        pltpu.VMEM((8, HALF + 128), jnp.float32),
        pltpu.VMEM((8, HALF + 128), jnp.float32),
        pltpu.VMEM((2, 8, HALF), jnp.float32),
        pltpu.VMEM((8, HALF), jnp.float32),
    ]
    scratch += three(cube, WIDE) + three(cube, WIDE)
    scratch += three(cube, DATA) + three(cube, DATA) + three(cube, DATA)
    scratch += three(face, lead) + three(face, rest) + three(face, DATA) + three(face, DATA)
    for shape in (line, row):
        big = (4,) + shape
        scratch += three(big, DATA) + three(shape, lead) + three(shape, rest) + three(shape, DATA) + three(shape, DATA)
    scratch += [
        pltpu.SemaphoreType.DMA((4,)),
        pltpu.SemaphoreType.DMA((160,)),
        pltpu.SemaphoreType.DMA((160,)),
        pltpu.SemaphoreType.DMA((3, 4)),
        pltpu.SemaphoreType.DMA((3, 4)),
    ]
    return pl.pallas_call(
        moe_kernel,
        out_shape=jax.ShapeDtypeStruct((8, 7168), bf),
        in_specs=[vm, vm, vm, vm, an, an, an],
        out_specs=vm,
        scratch_shapes=scratch,
        compiler_params=pltpu.CompilerParams(
            collective_id=1, has_side_effects=True, vmem_limit_bytes=67043328
        ),
        name="experts",
    )(middle, gain, ids, scores, eg, eu, ed)


class Sums:
    def __init__(self, wires, at, core, axis, buf, index, cut, width, ra, rb, rc, rd):
        self.wires, self.buf, self.index = wires, buf, index
        self.up, self.down = device(beside(at, axis, 1), core), device(beside(at, axis, -1), core)
        self.lead, self.rest = (slice(None), slice(0, cut)), (slice(None), slice(cut, width))
        self.ra, self.rb, self.rc, self.rd = ra, rb, rc, rd

    def part(self, ref, cols):
        return ref.at[(slice(None),) * (len(ref.shape) - 2) + cols]

    def far(self):
        s = self.index(2)
        self.a = self.wires.start(self.buf.at[s + self.lead], self.ra, self.down)
        self.b = self.wires.start(self.buf.at[s + self.rest], self.rb, self.up)

    def near(self):
        left, right = self.index(3), self.index(1)
        self.c = self.wires.start(self.buf.at[left + self.rest], self.part(self.rc, self.rest), self.down)
        self.d = self.wires.start(self.buf.at[right + self.lead], self.part(self.rd, self.lead), self.up)

    def add(self, s, other):
        self.buf[s] = (self.buf[s].astype(jnp.float32) + other[...].astype(jnp.float32)).astype(jnp.bfloat16)

    def relay(self):
        self.a.wait_recv()
        s = self.index(3) + self.lead
        self.add(s, self.ra)
        self.e = self.wires.start(self.buf.at[s], self.part(self.rc, self.lead), self.down)
        self.b.wait_recv()
        s = self.index(1) + self.rest
        self.add(s, self.rb)
        self.f = self.wires.start(self.buf.at[s], self.part(self.rd, self.rest), self.up)

    def total(self):
        for copy in (self.c, self.d, self.e, self.f):
            copy.wait_recv()
        return (
            self.buf[self.index(0)].astype(jnp.float32)
            + self.rc[...].astype(jnp.float32)
            + self.rd[...].astype(jnp.float32)
        )


class Spread:
    def __init__(self, wires, at, core, axis, buf, index, lead, rest):
        self.wires, self.buf, self.index, self.lead, self.rest = wires, buf, index, lead, rest
        self.up, self.down = device(beside(at, axis, 1), core), device(beside(at, axis, -1), core)

    def near(self):
        s = self.index(0)
        self.a = self.wires.start(self.buf.at[s], self.buf.at[s], self.up)
        self.b = self.wires.start(self.buf.at[s], self.buf.at[s], self.down)

    def relay(self):
        self.a.wait_recv()
        s = self.index(3) + self.lead
        self.c = self.wires.start(self.buf.at[s], self.buf.at[s], self.up)
        self.b.wait_recv()
        s = self.index(1) + self.rest
        self.d = self.wires.start(self.buf.at[s], self.buf.at[s], self.down)

    def finish(self):
        self.c.wait_recv()
        self.d.wait_recv()


PLANES = ((1, 2), (2, 1))
FF = 1152
FD = 896


def dense_kernel(
    stream, gain, wg, wu, wd, middle,
    vg, vu, vd, nbuf, land, ft, gu, gx, gra, grb, grc, grd, hid, dn,
    pa, pb, pc, pd, qs, qa, qb, qc, qd, fin, back,
    load_sem, send_sem, recv_sem,
):
    at, core, p, t = place()
    loads = [
        pltpu.make_async_copy(wg, vg, load_sem.at[0]),
        pltpu.make_async_copy(wu, vu, load_sem.at[1]),
        pltpu.make_async_copy(wd, vd, load_sem.at[2]),
    ]
    for load in loads:
        load.start()
    partner = device(at, 1 - core)
    line = [(lax.rem(p + q, 8), t) for q in range(1, 8)]
    greet(line + [device(beside(at, a, s), core) for a in (1, 2) for s in (1, -1)])
    wires = Wires(send_sem, recv_sem)

    rows = stream[...].astype(jnp.float32)
    normed = rms(rows, gain[...]).astype(jnp.float32)
    for o in range(8):
        nbuf[o] = normed[:, o * FD:(o + 1) * FD]
    sent = [wires.start(nbuf.at[peer[0]], land.at[p], peer) for peer in line]
    land[p] = nbuf[p]

    for copy in sent:
        copy.wait_recv()
    for x in range(4):
        ft[x // 2, x % 2, at[1], at[2]] = land[2 * x:2 * x + 2].reshape(16, FD).astype(jnp.bfloat16)

    def spots(b, k, fixed):
        return (b, k) + tuple(fixed.get(a, slice(None)) for a in (1, 2))

    fcut = ((slice(None), slice(0, 512)), (slice(None), slice(512, FD)))

    def spread_of(b, k, axis, other):
        def index(step):
            fixed = dict(other)
            fixed[axis] = lax.rem(at[axis] + step, 4)
            return spots(b, k, fixed)

        return Spread(wires, at, core, axis, ft, index, *fcut)

    def rem(axis, step):
        return lax.rem(at[axis] + step, 4)

    first = {(b, k): spread_of(b, k, PLANES[k][0], {PLANES[k][1]: at[PLANES[k][1]]}) for b in (0, 1) for k in (0, 1)}
    second = {
        (b, k, j): spread_of(b, k, PLANES[k][1], {PLANES[k][0]: rem(PLANES[k][0], j)})
        for b in (0, 1) for k in (0, 1) for j in range(4)
    }
    for b in (0, 1):
        for k in (0, 1):
            first[b, k].near()
            second[b, k, 0].near()
    for b in (0, 1):
        for k in (0, 1):
            first[b, k].relay()
            second[b, k, 3].near()
            second[b, k, 1].near()
            second[b, k, 0].relay()
        for k in (0, 1):
            first[b, k].finish()
            second[b, k, 2].near()
    for b in (0, 1):
        for j in (3, 1, 2):
            for k in (0, 1):
                second[b, k, j].relay()

    grows = [(gra.at[b], grb.at[b], grc.at[b], grd.at[b]) for b in (0, 1)]
    halves = [None, None]

    def project(b):
        for h in (0, 1):
            c = (1 - core) if h == 0 else core
            left = ft[b, c].reshape(256, FD)
            g = jnp.dot(left, vg[...], preferred_element_type=jnp.float32).astype(jnp.bfloat16)
            gu[b, c, :, :, 0:FF] = g.reshape(4, 64, FF)
            u = jnp.dot(left, vu[...], preferred_element_type=jnp.float32).astype(jnp.bfloat16)
            gu[b, c, :, :, FF:2 * FF] = u.reshape(4, 64, FF)
            if h == 0:
                halves[b] = wires.start(gu.at[b, c], gx.at[b], partner)

    def gsum(b):
        return Sums(
            wires, at, core, 0, gu, lambda step: (b, core, rem(0, step)), FF, 2 * FF, *grows[b]
        )

    gsums = [gsum(0), gsum(1)]

    def join(b):
        halves[b].wait_recv()

        def one(n, _):
            v = lax.rem(at[0] + n + 2, 4)
            gu[b, core, v] = (gu[b, core, v].astype(jnp.float32) + gx[b, v].astype(jnp.float32)).astype(jnp.bfloat16)
            return _

        lax.fori_loop(0, 4, one, 0)
        gsums[b].far()
        gsums[b].near()

    hspread = [
        Spread(wires, at, core, 0, hid, lambda step, b=b: (b, core, rem(0, step)),
               (slice(None), slice(0, 640)), (slice(None), slice(640, FF)))
        for b in (0, 1)
    ]
    hcross = [[], []]

    def cross(b, step):
        s = (b, core, rem(0, step))
        hcross[b].append(wires.start(hid.at[s], hid.at[s], partner))

    def activate(b):
        both = gsums[b].total()
        g, u = both[:, 0:FF], both[:, FF:2 * FF]
        hid[b, core, at[0]] = (g / (1.0 + jnp.exp(-g)) * u).astype(jnp.bfloat16)
        hspread[b].near()
        cross(b, 0)

    def hrelay(b):
        hspread[b].relay()
        cross(b, 3)
        cross(b, 1)

    def dsum(b, k):
        a1, a2 = PLANES[k]
        return Sums(
            wires, at, core, a1, dn, lambda step: spots(b, k, {a1: rem(a1, step)}), 512, FD,
            pa.at[b, k], pb.at[b, k], pc.at[b, k], pd.at[b, k],
        )

    def dsum2(b, k):
        a1, a2 = PLANES[k]
        return Sums(
            wires, at, core, a2, qs, lambda step: (b, k, rem(a2, step)), 512, FD,
            qa.at[b, k], qb.at[b, k], qc.at[b, k], qd.at[b, k],
        )

    ds = {(b, k): dsum(b, k) for b in (0, 1) for k in (0, 1)}
    ds2 = {(b, k): dsum2(b, k) for b in (0, 1) for k in (0, 1)}

    def contract(b):
        hspread[b].finish()
        cross(b, 2)
        for copy in hcross[b]:
            copy.wait_recv()
        for k in (0, 1):
            left = hid[b, k].reshape(256, FF)
            part = jnp.dot(left, vd[...], preferred_element_type=jnp.float32)
            dn[b, k] = part.astype(jnp.bfloat16).reshape(4, 4, 16, FD)
            ds[b, k].far()
            ds[b, k].near()

    def drelay(b):
        for k in (0, 1):
            ds[b, k].relay()

    def dturn(b):
        for k in (0, 1):
            qs[b, k] = ds[b, k].total().astype(jnp.bfloat16)
            ds2[b, k].far()
            ds2[b, k].near()

    def dend(b):
        for k in (0, 1):
            ds2[b, k].relay()
        for k in (0, 1):
            x = 2 * b + k
            fin[2 * x:2 * x + 2] = ds2[b, k].total().reshape(2, 8, FD)

    for j in range(4):
        for k in (0, 1):
            second[0, k, j].finish()
    loads[0].wait()
    loads[1].wait()
    project(0)
    for j in range(4):
        for k in (0, 1):
            second[1, k, j].finish()
    join(0)
    project(1)
    gsums[0].relay()
    join(1)
    activate(0)
    gsums[1].relay()
    hrelay(0)
    activate(1)
    loads[2].wait()
    contract(0)
    hrelay(1)
    contract(1)
    drelay(0)
    drelay(1)
    dturn(0)
    dturn(1)
    dend(0)
    dend(1)
    sent = [wires.start(fin.at[peer[0]], back.at[p], peer) for peer in line]
    back[p] = fin[p]
    for copy in sent:
        copy.wait_recv()
    for o in range(8):
        cols = slice(o * FD, (o + 1) * FD)
        middle[:, cols] = (rows[:, cols] + back[o]).astype(jnp.bfloat16)
    wires.close()


def dense(stream, gain, wg, wu, wd):
    vm, an = pl.BlockSpec(memory_space=pltpu.VMEM), pl.BlockSpec(memory_space=pl.ANY)
    bf, f32 = jnp.bfloat16, jnp.float32
    scratch = [
        pltpu.VMEM((FD, FF), bf), pltpu.VMEM((FD, FF), bf), pltpu.VMEM((FF, FD), bf),
        pltpu.VMEM((8, 8, FD), f32), pltpu.VMEM((8, 8, FD), f32),
        pltpu.VMEM((2, 2, 4, 4, 16, FD), bf),
        pltpu.VMEM((2, 2, 4, 64, 2 * FF), bf), pltpu.VMEM((2, 4, 64, 2 * FF), bf),
        pltpu.VMEM((2, 64, FF), bf), pltpu.VMEM((2, 64, FF), bf),
        pltpu.VMEM((2, 64, 2 * FF), bf), pltpu.VMEM((2, 64, 2 * FF), bf),
        pltpu.VMEM((2, 2, 4, 64, FF), bf),
        pltpu.VMEM((2, 2, 4, 4, 16, FD), bf),
    ]
    for lead in ((2, 2, 4, 16), (2, 2, 16)):
        if len(lead) == 3:
            scratch.append(pltpu.VMEM((2, 2, 4, 16, FD), bf))
        scratch += [
            pltpu.VMEM(lead + (512,), bf), pltpu.VMEM(lead + (FD - 512,), bf),
            pltpu.VMEM(lead + (FD,), bf), pltpu.VMEM(lead + (FD,), bf),
        ]
    scratch += [
        pltpu.VMEM((8, 8, FD), f32), pltpu.VMEM((8, 8, FD), f32),
        pltpu.SemaphoreType.DMA((3,)), pltpu.SemaphoreType.DMA((240,)), pltpu.SemaphoreType.DMA((240,)),
    ]
    return pl.pallas_call(
        dense_kernel,
        out_shape=jax.ShapeDtypeStruct((8, 7168), bf),
        in_specs=[vm, vm, an, an, an],
        out_specs=vm,
        scratch_shapes=scratch,
        compiler_params=pltpu.CompilerParams(
            collective_id=2, has_side_effects=True, vmem_limit_bytes=67043328
        ),
        name="dense",
    )(stream, gain, wg, wu, wd)


def migrate_kernel(
    mig, lens, leaving, arrived, got_len,
    held0, held1, far_out, far_in, near_out, near_in,
    load_sem, send_sem, recv_sem,
):
    at, core, p, t = place()
    loads = [
        pltpu.make_async_copy(leaving.at[:, 0], held0.at[at[2]], load_sem.at[0]),
        pltpu.make_async_copy(leaving.at[:, 1], held1.at[at[1]], load_sem.at[1]),
    ]
    for load in loads:
        load.start()
    greet([device(beside(at, a, s), core) for a in (1, 2) for s in (1, -1)])
    wires = Wires(send_sem, recv_sem)

    def rem(axis, step):
        return lax.rem(at[axis] + step, 4)

    def look(n, state):
        source, item = n // 2, lax.rem(n, 2)
        dest = mig[p * 16 + source, item]
        new = []
        for i, (count, s0, m0, s1, m1) in enumerate(state):
            aim = i * 4 + at[2] if i < 4 else at[1] * 4 + (i - 4)
            hit = dest == aim
            s0, m0 = jnp.where(hit & (count == 0), source, s0), jnp.where(hit & (count == 0), item, m0)
            s1, m1 = jnp.where(hit & (count == 1), source, s1), jnp.where(hit & (count == 1), item, m1)
            new.append((count + jnp.where(hit, 1, 0), s0, m0, s1, m1))
        return tuple(new)

    zero = jnp.int32(0)
    table = lax.fori_loop(0, 32, look, ((zero,) * 5,) * 8)

    def choose(values, index):
        r = values[0]
        for i in range(1, len(values)):
            r = jnp.where(index == i, values[i], r)
        return r

    loads[0].wait()
    loads[1].wait()

    held = (held0, held1)

    def mover(l):
        a1 = (2, 1)[l]

        def index(step):
            return (rem(a1, step),)

        return Spread(wires, at, core, a1, held[l], index, (0,), (1,))

    movers = [mover(0), mover(1)]

    def mine(l, step, slot):
        a1, a2 = ((2, 1), (1, 2))[l]
        options = [table[l * 4 + v] for v in range(4)]
        v = rem(a2, step)
        source = choose([o[1 + 2 * slot] for o in options], v)
        item = choose([o[2 + 2 * slot] for o in options], v)
        y, z = source // 4, lax.rem(source, 4)
        j, i = (z, y) if l == 0 else (y, z)
        return i, j, item

    peers2 = [[device(beside(at, a2, 1), core), device(beside(at, a2, -1), core)] for a2 in (1, 2)]
    far_copies, near_copies = {}, {}

    def merge_far(l):
        for slot in (0, 1):
            i, j, item = mine(l, 2, slot)
            far_out[l, slot] = held[l][j, item]
            far_copies[l, slot] = wires.start(far_out.at[l, slot], far_in.at[l, slot], peers2[l][1 - slot])

    def merge_near(l, slot, side):
        step = (3, 1)[side]
        i, j, item = mine(l, step, slot)
        if slot == side:
            far_copies[l, slot].wait_recv()
            a2 = (1, 2)[l]
            near_out[l, side, slot] = jnp.where(i == at[a2], held[l][j, item], far_in[l, slot])
        else:
            near_out[l, side, slot] = held[l][j, item]
        near_copies[l, side, slot] = wires.start(
            near_out.at[l, side, slot], near_in.at[l, side, slot], peers2[l][1 - side]
        )

    def merge_end(l):
        a2 = (1, 2)[l]
        for side in (0, 1):
            for slot in (0, 1):
                near_copies[l, side, slot].wait_recv()
        for slot in (0, 1):
            i, j, item = mine(l, 0, slot)
            delta = lax.rem(i - at[a2] + 4, 4)
            from_above = (delta == 1) | ((delta == 2) if slot == 0 else (delta == 5))
            other = jnp.where(from_above, near_in[l, 0, slot], near_in[l, 1, slot])
            arrived[slot, l] = jnp.where(delta == 0, held[l][j, item], other)

    for m in movers:
        m.near()
    for m in movers:
        m.relay()
    for l, m in enumerate(movers):
        m.finish()
        merge_far(l)
    for l in (0, 1):
        merge_near(l, 1, 0)
        merge_near(l, 0, 1)
    for l in (0, 1):
        merge_near(l, 0, 0)
        merge_near(l, 1, 1)
    for l in (0, 1):
        merge_end(l)
    for slot in (0, 1):
        i, j, item = mine(0, 0, slot)
        got_len[slot] = lens[p * 16 + i * 4 + j, item]
    wires.close()


def migrate(mig, lens, leaving):
    vm, an = pl.BlockSpec(memory_space=pltpu.VMEM), pl.BlockSpec(memory_space=pl.ANY)
    sm = pl.BlockSpec(memory_space=pltpu.SMEM)
    bf = jnp.bfloat16
    item = (576, 256)
    return pl.pallas_call(
        migrate_kernel,
        out_shape=(jax.ShapeDtypeStruct((2, 2) + item, bf), jax.ShapeDtypeStruct((2,), jnp.int32)),
        in_specs=[sm, sm, an],
        out_specs=(vm, sm),
        scratch_shapes=[
            pltpu.VMEM((4, 2) + item, bf), pltpu.VMEM((4, 2) + item, bf),
            pltpu.VMEM((2, 2) + item, bf), pltpu.VMEM((2, 2) + item, bf),
            pltpu.VMEM((2, 2, 2) + item, bf), pltpu.VMEM((2, 2, 2) + item, bf),
            pltpu.SemaphoreType.DMA((2,)), pltpu.SemaphoreType.DMA((24,)), pltpu.SemaphoreType.DMA((24,)),
        ],
        compiler_params=pltpu.CompilerParams(
            collective_id=3, has_side_effects=True, vmem_limit_bytes=67043328
        ),
        name="migrate",
    )(mig, lens, leaving)


def on_device(
    queries,
    new_latent,
    resident,
    leaving,
    res_len,
    leave_len,
    mig_dest,
    stream,
    dense_gain,
    w_gate,
    w_up,
    w_down,
    moe_gain,
    expert_gate,
    expert_up,
    expert_down,
    expert_ids,
    gate_scores,
):
    middle = dense(stream, dense_gain[None], w_gate, w_up, w_down)
    moved, moved_len = migrate(mig_dest, leave_len, jnp.swapaxes(leaving, 2, 3))
    arrived = jnp.swapaxes(moved, 2, 3)
    stay = resident.shape[0]
    context_stay = attend(queries[:stay], resident, res_len, new_latent[:stay])
    context_moved = attend(queries[stay:], arrived[:, 0], moved_len, new_latent[stay:])
    context = jnp.concatenate([context_stay, context_moved], axis=0)
    stream_out = moe(
        middle, moe_gain[None], expert_ids, gate_scores, expert_gate[0], expert_up[0], expert_down[0]
    )
    return (context, arrived, stream_out)


def solution(mesh):
    placed = (
        P(("dp", "tp"), None, None),
        P(("dp", "tp"), None),
        P(("dp", "tp"), None, None),
        P(("dp", "tp"), None, None, None),
        P(("dp", "tp")),
        P(),
        P(),
        P(("dp", "tp"), None),
        P(),
        P("dp", "tp"),
        P("dp", "tp"),
        P("tp", "dp"),
        P(),
        P("tp", None, "dp"),
        P("tp", None, "dp"),
        P("tp", "dp", None),
        P(("dp", "tp"), None),
        P(("dp", "tp"), None),
    )
    return jax.shard_map(
        on_device,
        mesh=mesh,
        in_specs=placed,
        out_specs=(
            P(("dp", "tp"), None, None),
            P(("dp", "tp"), None, None, None),
            P(("dp", "tp"), None),
        ),
        check_vma=False,
    )
```

```python
import functools

import jax
import jax.numpy as jnp
from jax import lax
from jax.experimental import pallas as pl
from jax.experimental.pallas import tpu as pltpu
from jax.sharding import PartitionSpec as P

MESH = pl.DeviceIdType.MESH

VDIM = 512
QKD = 192


EPS = 1e-06
ROUTE_SCALE = 2.5


def attend(queries, keys, lengths, newest):
    scale = QKD ** (-0.5)
    scores = jnp.einsum("rhl,rcl->rhc", queries, keys, preferred_element_type=jnp.float32) * scale
    positions = jnp.arange(keys.shape[1])
    valid = positions[None, None, :] < lengths[:, None, None]
    masked = jnp.where(valid, scores, -1e30)
    own_score = (
        jnp.einsum("rhl,rl->rh", queries, newest, preferred_element_type=jnp.float32) * scale
    )
    top = jnp.maximum(jnp.max(masked, axis=-1), own_score)
    expo = jnp.where(valid, jnp.exp(masked - top[..., None]), 0.0)
    own_expo = jnp.exp(own_score - top)
    total = jnp.sum(expo, axis=-1) + own_expo
    weights = (expo / total[..., None]).astype(jnp.bfloat16)
    own_weight = (own_expo / total).astype(jnp.bfloat16)
    context = jnp.einsum(
        "rhc,rcv->rhv", weights, keys[:, :, :VDIM], preferred_element_type=jnp.float32
    )
    context = context + own_weight.astype(jnp.float32)[..., None] * newest[:, None, :VDIM].astype(
        jnp.float32
    )
    return context.astype(jnp.bfloat16)


HALF = 3584
OFFS = (0, 1280, 2432)
DATA = (1280, 1152, 1152)
WIDE = (1280, 1280, 1152)
ORDERS = ((0, 1, 2), (1, 2, 0), (2, 0, 1))
CUT = 640


def place():
    p, t = lax.axis_index("dp"), lax.axis_index("tp")
    return [p // 2, t // 4, t % 4], p % 2, p, t


def device(at, core):
    return (at[0] * 2 + core, at[1] * 4 + at[2])


def beside(at, axis, step):
    return [lax.rem(at[a] + 4 + step, 4) if a == axis else at[a] for a in range(3)]


class Wires:
    def __init__(self, send, recv):
        self.send, self.recv, self.used = send, recv, 0
        self.open = []

    def start(self, src, dst, peer):
        i = self.used
        self.used += 1
        copy = pltpu.make_async_remote_copy(
            src_ref=src, dst_ref=dst, send_sem=self.send.at[i], recv_sem=self.recv.at[i],
            device_id=peer, device_id_type=MESH,
        )
        copy.start()
        self.open.append(copy)
        return copy

    def close(self):
        for copy in self.open:
            copy.wait_send()


def greet(peers):
    barrier = pltpu.get_barrier_semaphore()
    for peer in peers:
        pl.semaphore_signal(barrier, inc=1, device_id=peer, device_id_type=MESH)
    pl.semaphore_wait(barrier, len(peers))


def rms(rows, gain):
    mean_square = jnp.mean(rows * rows, axis=-1, keepdims=True)
    return (rows * lax.rsqrt(mean_square + EPS) * gain).astype(jnp.bfloat16)


def picks(axes_values):
    return tuple(axes_values)


def moe_kernel(
    middle, gain, ids, scores, eg, eu, ed, out,
    wgu, wd, acc, inner, swap, swap2, swap3, swap4,
    ag0, ag1, ag2, ot0, ot1, ot2, po0, po1, po2, pt0, pt1, pt2, pr0, pr1, pr2,
    ra0, ra1, ra2, rb0, rb1, rb2, rc0, rc1, rc2, rd0, rd1, rd2,
    q0, q1, q2, qa0, qa1, qa2, qb0, qb1, qb2, qc0, qc1, qc2, qd0, qd1, qd2,
    s0, s1, s2, sa0, sa1, sa2, sb0, sb1, sb2, sc0, sc1, sc2, sd0, sd1, sd2,
    load_sem, send_sem, recv_sem, xsend, xrecv,
):
    at, core, p, t = place()
    ag, ot, po, pt, pr = (ag0, ag1, ag2), (ot0, ot1, ot2), (po0, po1, po2), (pt0, pt1, pt2), (pr0, pr1, pr2)
    loads = [
        pltpu.make_async_copy(eg, wgu.at[:, 0:256], load_sem.at[0]),
        pltpu.make_async_copy(eu, wgu.at[:, 256:512], load_sem.at[1]),
        pltpu.make_async_copy(ed.at[:, 0:HALF], wd.at[0], load_sem.at[2]),
        pltpu.make_async_copy(ed.at[:, HALF:2 * HALF], wd.at[1], load_sem.at[3]),
    ]
    for load in loads:
        load.start()
    partner = device(at, 1 - core)
    greet([partner] + [device(beside(at, a, s), core) for a in range(3) for s in (1, -1)])
    wires = Wires(send_sem, recv_sem)

    rows = middle[...].astype(jnp.float32)
    mixed = rms(rows, gain[...]).astype(jnp.float32)
    given = scores[...]
    share = given / jnp.sum(given, axis=1, keepdims=True) * ROUTE_SCALE
    lane = lax.broadcasted_iota(jnp.int32, (8, 128), 1)
    spread = jnp.zeros((8, 128), jnp.float32)
    for k in range(8):
        spread = spread + jnp.where(lane == ids[:, k:k + 1], share[:, k:k + 1], 0.0)
    high = spread.astype(jnp.bfloat16).astype(jnp.float32)
    low = (spread - high).astype(jnp.bfloat16).astype(jnp.float32)
    packed = high + pltpu.roll(low, 16, 1)
    is_one = core == 1
    swap[:, 0:HALF] = jnp.where(is_one, mixed[:, 0:HALF], mixed[:, HALF:])
    swap[:, HALF:] = packed
    over = wires.start(swap, swap2, partner)
    mine = jnp.where(is_one, mixed[:, HALF:], mixed[:, 0:HALF])
    over.wait_recv()
    theirs = swap2[:, 0:HALF]
    first = jnp.where(is_one, theirs, mine)
    second = jnp.where(is_one, mine, theirs)
    block = jnp.concatenate([first, second], axis=0).astype(jnp.bfloat16)
    other_pack = swap2[:, HALF:]
    pack = jnp.concatenate(
        [jnp.where(is_one, other_pack, packed), jnp.where(is_one, packed, other_pack)], axis=0
    ).astype(jnp.bfloat16)
    for k in range(3):
        ag[k][at[0], at[1], at[2], :, 0:DATA[k]] = block[:, OFFS[k]:OFFS[k] + DATA[k]]
    ag1[at[0], at[1], at[2], :, DATA[1]:WIDE[1]] = pack

    def spot(k, fixed):
        return tuple(fixed.get(a, slice(None)) for a in range(3))

    def cols(k, part):
        return slice(0, CUT) if part == 0 else slice(CUT, WIDE[k])

    def ring(k, axis, fixed):
        here = spot(k, fixed)
        up, down = device(beside(at, axis, 1), core), device(beside(at, axis, -1), core)
        a = wires.start(ag[k].at[here], ag[k].at[here], up)
        b = wires.start(ag[k].at[here], ag[k].at[here], down)
        return a, b

    def forward(k, axis, fixed, pair):
        up, down = device(beside(at, axis, 1), core), device(beside(at, axis, -1), core)
        below, above = dict(fixed), dict(fixed)
        below[axis], above[axis] = lax.rem(at[axis] + 3, 4), lax.rem(at[axis] + 1, 4)
        pair[0].wait_recv()
        s = spot(k, below) + (slice(None), cols(k, 0))
        a = wires.start(ag[k].at[s], ag[k].at[s], up)
        pair[1].wait_recv()
        s = spot(k, above) + (slice(None), cols(k, 1))
        b = wires.start(ag[k].at[s], ag[k].at[s], down)
        return a, b

    own = [{a: at[a] for a in range(3)} for _ in range(3)]
    pairs = [ring(k, ORDERS[k][0], own[k]) for k in range(3)]
    pairs = [forward(k, ORDERS[k][0], own[k], pairs[k]) for k in range(3)]
    second_pairs, third = [None] * 3, [[], [], []]
    for k in range(3):
        a1, a2, a3 = ORDERS[k]
        for c in pairs[k]:
            c.wait_recv()
        fixed = {a2: at[a2], a3: at[a3]}
        second_pairs[k] = ring(k, a2, fixed)
        third[k].append((fixed, ring(k, a3, fixed)))
    done2 = [None] * 3
    for k in range(3):
        a1, a2, a3 = ORDERS[k]
        fixed = {a2: at[a2], a3: at[a3]}
        done2[k] = forward(k, a2, fixed, second_pairs[k])
        for step in (1, 3):
            fixed = {a2: lax.rem(at[a2] + step, 4), a3: at[a3]}
            third[k].append((fixed, ring(k, a3, fixed)))
    last = [[], [], []]
    for k in range(3):
        a1, a2, a3 = ORDERS[k]
        for c in done2[k]:
            c.wait_recv()
        fixed = {a2: lax.rem(at[a2] + 2, 4), a3: at[a3]}
        third[k].append((fixed, ring(k, a3, fixed)))

    def plane(k, step):
        return spot(k, {ORDERS[k][2]: lax.rem(at[ORDERS[k][2]] + step, 4)})

    across = [[None] * 4 for _ in range(3)]

    def hand(k, step):
        s = plane(k, step)
        across[k][step] = wires.start(ag[k].at[s], ot[k].at[s], partner)

    for k in range(3):
        hand(k, 0)
    loads[0].wait()
    loads[1].wait()

    def product(bufs, half, k, step, fresh):
        s = plane(k, step)
        left = bufs[k][s + (slice(None), slice(0, DATA[k]))].reshape(256, DATA[k])
        base = pl.multiple_of(half * HALF + OFFS[k], 128)
        part = jnp.dot(left, wgu[pl.ds(base, DATA[k]), :], preferred_element_type=jnp.float32)
        part = part.reshape(4, 4, 16, 512)
        acc[s] = acc[s] + part

    acc[...] = jnp.zeros_like(acc)
    for k in range(3):
        product(ag, core, k, 0, False)
    for n in range(4):
        for k in range(3):
            fixed, pair = third[k][n]
            last[k].append(forward(k, ORDERS[k][2], fixed, pair))
    for k in range(3):
        hand(k, 1)
        hand(k, 3)

    def side(n, _):
        for k in range(3):
            product(ag, core, k, 2 * n + 1, False)
        return _

    lax.fori_loop(0, 2, side, 0)
    for k in range(3):
        for step in (0, 1, 3):
            across[k][step].wait_recv()

    def side_other(n, _):
        for k in range(3):
            product(ot, 1 - core, k, n + n // 2, False)
        return _

    lax.fori_loop(0, 3, side_other, 0)
    for k in range(3):
        for pair in last[k]:
            for c in pair:
                c.wait_recv()
        hand(k, 2)
    for k in range(3):
        product(ag, core, k, 2, False)
    for k in range(3):
        across[k][2].wait_recv()
        product(ot, 1 - core, k, 2, False)

    lane = lax.broadcasted_iota(jnp.int32, (256, 128), 1)

    def activate(n, _):
        both = acc[n].reshape(256, 512)
        gate, up = both[:, 0:256], both[:, 256:512]
        packs = ag1[n, :, :, :, DATA[1]:WIDE[1]].reshape(256, 128).astype(jnp.float32)
        keep = (lane == t) | (lane == t + 16)
        weight = jnp.sum(jnp.where(keep, packs, 0.0), axis=1, keepdims=True)
        value = gate / (1.0 + jnp.exp(-gate)) * up * weight
        inner[n] = value.astype(jnp.bfloat16).reshape(4, 4, 16, 256)
        return _

    lax.fori_loop(0, 4, activate, 0)
    loads[2].wait()
    loads[3].wait()

    def group(k, step):
        a1 = ORDERS[k][0]
        return spot(k, {a1: lax.rem(at[a1] + step, 4)})

    def trade(k, n, step):
        s = group(k, step)
        return pltpu.make_async_remote_copy(
            src_ref=pt[k].at[s], dst_ref=pr[k].at[s], send_sem=xsend.at[k, n], recv_sem=xrecv.at[k, n],
            device_id=partner, device_id_type=MESH,
        )

    def step_of(n):
        return lax.rem(n * 3 + 2, 4) if not isinstance(n, int) else (n * 3 + 2) % 4

    def expand(n, _):
        for k in range(3):
            s = group(k, step_of(n))
            left = inner[s].reshape(256, 256)
            part = jnp.dot(left, wd[1 - core, :, OFFS[k]:OFFS[k] + DATA[k]], preferred_element_type=jnp.float32)
            pt[k][s] = part.astype(jnp.bfloat16).reshape(4, 4, 16, DATA[k])
            trade(k, n, step_of(n)).start()
            part = jnp.dot(left, wd[core, :, OFFS[k]:OFFS[k] + DATA[k]], preferred_element_type=jnp.float32)
            po[k][s] = part.astype(jnp.bfloat16).reshape(4, 4, 16, DATA[k])
        return _

    lax.fori_loop(0, 4, expand, 0)

    ra, rb, rc, rd = (ra0, ra1, ra2), (rb0, rb1, rb2), (rc0, rc1, rc2), (rd0, rd1, rd2)

    def dcols(k, part):
        return slice(0, CUT) if part == 0 else slice(CUT, DATA[k])

    def meet(k, n):
        trade(k, n, step_of(n)).wait_recv()
        s = group(k, step_of(n))
        po[k][s] = (po[k][s].astype(jnp.float32) + pr[k][s].astype(jnp.float32)).astype(jnp.bfloat16)

    def scatter(bufs, index, axis_of, ra, rb, rc, rd, prepare):
        state = []
        for k in range(3):
            up, down = device(beside(at, axis_of(k), 1), core), device(beside(at, axis_of(k), -1), core)
            prepare(k, 2)
            src = index(k, 2)
            a = wires.start(bufs[k].at[src + (slice(None), dcols(k, 0))], ra[k], down)
            b = wires.start(bufs[k].at[src + (slice(None), dcols(k, 1))], rb[k], up)
            state.append([up, down, a, b])
        for k in range(3):
            up, down, a, b = state[k]
            prepare(k, 1)
            prepare(k, 3)
            left, right = index(k, 3), index(k, 1)
            c = wires.start(
                bufs[k].at[left + (slice(None), dcols(k, 1))], rc[k].at[(slice(None),) * (len(rc[k].shape) - 1) + (dcols(k, 1),)], down
            )
            d = wires.start(
                bufs[k].at[right + (slice(None), dcols(k, 0))], rd[k].at[(slice(None),) * (len(rd[k].shape) - 1) + (dcols(k, 0),)], up
            )
            state[k] += [c, d]
        for k in range(3):
            up, down, a, b, c, d = state[k]
            left, right = index(k, 3), index(k, 1)
            a.wait_recv()
            s = left + (slice(None), dcols(k, 0))
            bufs[k][s] = (bufs[k][s].astype(jnp.float32) + ra[k][...].astype(jnp.float32)).astype(jnp.bfloat16)
            e = wires.start(bufs[k].at[s], rc[k].at[(slice(None),) * (len(rc[k].shape) - 1) + (dcols(k, 0),)], down)
            b.wait_recv()
            s = right + (slice(None), dcols(k, 1))
            bufs[k][s] = (bufs[k][s].astype(jnp.float32) + rb[k][...].astype(jnp.float32)).astype(jnp.bfloat16)
            f = wires.start(bufs[k].at[s], rd[k].at[(slice(None),) * (len(rd[k].shape) - 1) + (dcols(k, 1),)], up)
            state[k] += [e, f]
        sums = []
        for k in range(3):
            prepare(k, 0)
            for c in state[k][4:]:
                c.wait_recv()
            yield k, (
                bufs[k][index(k, 0)].astype(jnp.float32)
                + rc[k][...].astype(jnp.float32)
                + rd[k][...].astype(jnp.float32)
            )

    turn = {2: 0, 1: 1, 3: 3, 0: 2}
    assert all(step_of(n) == s for s, n in turn.items())
    q = (q0, q1, q2)
    for k, total in scatter(
        po, group, lambda k: ORDERS[k][0], ra, rb, rc, rd, lambda k, step: meet(k, turn[step])
    ):
        q[k][...] = total.astype(jnp.bfloat16)

    def group2(k, step):
        a1, a2, a3 = ORDERS[k]
        rest = [a for a in range(3) if a != a1]
        return tuple(lax.rem(at[a] + step, 4) if a == a2 else slice(None) for a in rest)

    s_ = (s0, s1, s2)
    for k, total in scatter(
        q, group2, lambda k: ORDERS[k][1], (qa0, qa1, qa2), (qb0, qb1, qb2), (qc0, qc1, qc2), (qd0, qd1, qd2), lambda k, step: None
    ):
        s_[k][...] = total.astype(jnp.bfloat16)

    def group3(k, step):
        return (lax.rem(at[ORDERS[k][2]] + step, 4),)

    for k, total in scatter(
        s_, group3, lambda k: ORDERS[k][2], (sa0, sa1, sa2), (sb0, sb1, sb2), (sc0, sc1, sc2), (sd0, sd1, sd2), lambda k, step: None
    ):
        swap3[:, :, OFFS[k]:OFFS[k] + DATA[k]] = total.reshape(2, 8, DATA[k])
    over = wires.start(swap3.at[1 - core], swap4, partner)
    over.wait_recv()
    lead = jnp.where(is_one, swap4[...], swap3[0])
    tail = jnp.where(is_one, swap3[1], swap4[...])
    out[:, 0:HALF] = (rows[:, 0:HALF] + lead).astype(jnp.bfloat16)
    out[:, HALF:] = (rows[:, HALF:] + tail).astype(jnp.bfloat16)
    for k in range(3):
        for n in range(4):
            trade(k, n, step_of(n)).wait_send()
    wires.close()


def moe(middle, gain, ids, scores, eg, eu, ed):
    vm, an = pl.BlockSpec(memory_space=pltpu.VMEM), pl.BlockSpec(memory_space=pl.ANY)
    bf = jnp.bfloat16

    def three(shape, widths):
        return [pltpu.VMEM(shape + (w,), bf) for w in widths]

    lead, rest = (CUT,) * 3, tuple(w - CUT for w in DATA)
    cube, face, line, row = (4, 4, 4, 16), (4, 4, 16), (4, 16), (16,)
    scratch = [
        pltpu.VMEM((7168, 512), bf),
        pltpu.VMEM((2, 256, HALF), bf),
        pltpu.VMEM((4, 4, 4, 16, 512), jnp.float32),
        pltpu.VMEM((4, 4, 4, 16, 256), bf),
        pltpu.VMEM((8, HALF + 128), jnp.float32),
        pltpu.VMEM((8, HALF + 128), jnp.float32),
        pltpu.VMEM((2, 8, HALF), jnp.float32),
        pltpu.VMEM((8, HALF), jnp.float32),
    ]
    scratch += three(cube, WIDE) + three(cube, WIDE)
    scratch += three(cube, DATA) + three(cube, DATA) + three(cube, DATA)
    scratch += three(face, lead) + three(face, rest) + three(face, DATA) + three(face, DATA)
    for shape in (line, row):
        big = (4,) + shape
        scratch += three(big, DATA) + three(shape, lead) + three(shape, rest) + three(shape, DATA) + three(shape, DATA)
    scratch += [
        pltpu.SemaphoreType.DMA((4,)),
        pltpu.SemaphoreType.DMA((160,)),
        pltpu.SemaphoreType.DMA((160,)),
        pltpu.SemaphoreType.DMA((3, 4)),
        pltpu.SemaphoreType.DMA((3, 4)),
    ]
    return pl.pallas_call(
        moe_kernel,
        out_shape=jax.ShapeDtypeStruct((8, 7168), bf),
        in_specs=[vm, vm, vm, vm, an, an, an],
        out_specs=vm,
        scratch_shapes=scratch,
        compiler_params=pltpu.CompilerParams(
            collective_id=1, has_side_effects=True, vmem_limit_bytes=67043328
        ),
        name="experts",
    )(middle, gain, ids, scores, eg, eu, ed)


class Sums:
    def __init__(self, wires, at, core, axis, buf, index, cut, width, ra, rb, rc, rd):
        self.wires, self.buf, self.index = wires, buf, index
        self.up, self.down = device(beside(at, axis, 1), core), device(beside(at, axis, -1), core)
        self.lead, self.rest = (slice(None), slice(0, cut)), (slice(None), slice(cut, width))
        self.ra, self.rb, self.rc, self.rd = ra, rb, rc, rd

    def part(self, ref, cols):
        return ref.at[(slice(None),) * (len(ref.shape) - 2) + cols]

    def far(self):
        s = self.index(2)
        self.a = self.wires.start(self.buf.at[s + self.lead], self.ra, self.down)
        self.b = self.wires.start(self.buf.at[s + self.rest], self.rb, self.up)

    def near(self):
        left, right = self.index(3), self.index(1)
        self.c = self.wires.start(self.buf.at[left + self.rest], self.part(self.rc, self.rest), self.down)
        self.d = self.wires.start(self.buf.at[right + self.lead], self.part(self.rd, self.lead), self.up)

    def add(self, s, other):
        self.buf[s] = (self.buf[s].astype(jnp.float32) + other[...].astype(jnp.float32)).astype(jnp.bfloat16)

    def relay(self):
        self.a.wait_recv()
        s = self.index(3) + self.lead
        self.add(s, self.ra)
        self.e = self.wires.start(self.buf.at[s], self.part(self.rc, self.lead), self.down)
        self.b.wait_recv()
        s = self.index(1) + self.rest
        self.add(s, self.rb)
        self.f = self.wires.start(self.buf.at[s], self.part(self.rd, self.rest), self.up)

    def total(self):
        for copy in (self.c, self.d, self.e, self.f):
            copy.wait_recv()
        return (
            self.buf[self.index(0)].astype(jnp.float32)
            + self.rc[...].astype(jnp.float32)
            + self.rd[...].astype(jnp.float32)
        )


class Spread:
    def __init__(self, wires, at, core, axis, buf, index, lead, rest):
        self.wires, self.buf, self.index, self.lead, self.rest = wires, buf, index, lead, rest
        self.up, self.down = device(beside(at, axis, 1), core), device(beside(at, axis, -1), core)

    def near(self):
        s = self.index(0)
        self.a = self.wires.start(self.buf.at[s], self.buf.at[s], self.up)
        self.b = self.wires.start(self.buf.at[s], self.buf.at[s], self.down)

    def relay(self):
        self.a.wait_recv()
        s = self.index(3) + self.lead
        self.c = self.wires.start(self.buf.at[s], self.buf.at[s], self.up)
        self.b.wait_recv()
        s = self.index(1) + self.rest
        self.d = self.wires.start(self.buf.at[s], self.buf.at[s], self.down)

    def finish(self):
        self.c.wait_recv()
        self.d.wait_recv()


PLANES = ((1, 2), (2, 1))
FF = 1152
FD = 896


def dense_kernel(
    stream, gain, wg, wu, wd, table, leaving, middle, arrived,
    vg, vu, vd, nbuf, land, ft, gu, gx, gra, grb, grc, grd, hid, dn,
    pa, pb, pc, pd, qs, qa, qb, qc, qd, fin, back,
    held0, held1, far_out, far_in, near_out, near_in,
    load_sem, send_sem, recv_sem,
):
    at, core, p, t = place()
    loads = [
        pltpu.make_async_copy(wg, vg, load_sem.at[0]),
        pltpu.make_async_copy(wu, vu, load_sem.at[1]),
        pltpu.make_async_copy(wd, vd, load_sem.at[2]),
        pltpu.make_async_copy(leaving.at[:, 0], held0.at[at[2]], load_sem.at[3]),
        pltpu.make_async_copy(leaving.at[:, 1], held1.at[at[1]], load_sem.at[4]),
    ]
    for load in loads:
        load.start()
    partner = device(at, 1 - core)
    line = [(lax.rem(p + q, 8), t) for q in range(1, 8)]
    greet(line + [device(beside(at, a, s), core) for a in (1, 2) for s in (1, -1)])
    wires = Wires(send_sem, recv_sem)

    rows = stream[...].astype(jnp.float32)
    normed = rms(rows, gain[...]).astype(jnp.float32)
    for o in range(8):
        nbuf[o] = normed[:, o * FD:(o + 1) * FD]
    sent = [wires.start(nbuf.at[peer[0]], land.at[p], peer) for peer in line]
    land[p] = nbuf[p]

    for copy in sent:
        copy.wait_recv()
    for x in range(4):
        ft[x // 2, x % 2, at[1], at[2]] = land[2 * x:2 * x + 2].reshape(16, FD).astype(jnp.bfloat16)

    def spots(b, k, fixed):
        return (b, k) + tuple(fixed.get(a, slice(None)) for a in (1, 2))

    fcut = ((slice(None), slice(0, 512)), (slice(None), slice(512, FD)))

    def spread_of(b, k, axis, other):
        def index(step):
            fixed = dict(other)
            fixed[axis] = lax.rem(at[axis] + step, 4)
            return spots(b, k, fixed)

        return Spread(wires, at, core, axis, ft, index, *fcut)

    def rem(axis, step):
        return lax.rem(at[axis] + step, 4)

    first = {(b, k): spread_of(b, k, PLANES[k][0], {PLANES[k][1]: at[PLANES[k][1]]}) for b in (0, 1) for k in (0, 1)}
    second = {
        (b, k, j): spread_of(b, k, PLANES[k][1], {PLANES[k][0]: rem(PLANES[k][0], j)})
        for b in (0, 1) for k in (0, 1) for j in range(4)
    }
    for b in (0, 1):
        for k in (0, 1):
            first[b, k].near()
            second[b, k, 0].near()
    for b in (0, 1):
        for k in (0, 1):
            first[b, k].relay()
            second[b, k, 3].near()
            second[b, k, 1].near()
            second[b, k, 0].relay()
        for k in (0, 1):
            first[b, k].finish()
            second[b, k, 2].near()
    for b in (0, 1):
        for j in (3, 1, 2):
            for k in (0, 1):
                second[b, k, j].relay()

    loads[3].wait()
    loads[4].wait()

    held = (held0, held1)

    def mover(l):
        a1 = (2, 1)[l]

        def index(step):
            return (rem(a1, step),)

        return Spread(wires, at, core, a1, held[l], index, (0,), (1,))

    movers = [mover(0), mover(1)]

    def mine(l, step, slot):
        a1, a2 = ((2, 1), (1, 2))[l]
        row = l * 4 + rem(a2, step)
        source = table[row, 2 * slot]
        item = table[row, 2 * slot + 1]
        y, z = source // 4, lax.rem(source, 4)
        j, i = (z, y) if l == 0 else (y, z)
        return i, j, item

    peers2 = [[device(beside(at, a2, 1), core), device(beside(at, a2, -1), core)] for a2 in (1, 2)]
    far_copies, near_copies = {}, {}

    def merge_far(l):
        for slot in (0, 1):
            i, j, item = mine(l, 2, slot)
            far_out[l, slot] = held[l][j, item]
            far_copies[l, slot] = wires.start(far_out.at[l, slot], far_in.at[l, slot], peers2[l][1 - slot])

    def merge_near(l, slot, side):
        step = (3, 1)[side]
        i, j, item = mine(l, step, slot)
        if slot == side:
            far_copies[l, slot].wait_recv()
            a2 = (1, 2)[l]
            near_out[l, side, slot] = jnp.where(i == at[a2], held[l][j, item], far_in[l, slot])
        else:
            near_out[l, side, slot] = held[l][j, item]
        near_copies[l, side, slot] = wires.start(
            near_out.at[l, side, slot], near_in.at[l, side, slot], peers2[l][1 - side]
        )

    def merge_end(l):
        a2 = (1, 2)[l]
        for side in (0, 1):
            for slot in (0, 1):
                near_copies[l, side, slot].wait_recv()
        for slot in (0, 1):
            i, j, item = mine(l, 0, slot)
            delta = lax.rem(i - at[a2] + 4, 4)
            from_above = (delta == 1) | ((delta == 2) if slot == 0 else (delta == 5))
            other = jnp.where(from_above, near_in[l, 0, slot], near_in[l, 1, slot])
            arrived[slot, l] = jnp.where(delta == 0, held[l][j, item], other)

    grows = [(gra.at[b], grb.at[b], grc.at[b], grd.at[b]) for b in (0, 1)]
    halves = [None, None]

    def project(b):
        for h in (0, 1):
            c = (1 - core) if h == 0 else core
            left = ft[b, c].reshape(256, FD)
            g = jnp.dot(left, vg[...], preferred_element_type=jnp.float32).astype(jnp.bfloat16)
            gu[b, c, :, :, 0:FF] = g.reshape(4, 64, FF)
            u = jnp.dot(left, vu[...], preferred_element_type=jnp.float32).astype(jnp.bfloat16)
            gu[b, c, :, :, FF:2 * FF] = u.reshape(4, 64, FF)
            if h == 0:
                halves[b] = wires.start(gu.at[b, c], gx.at[b], partner)

    def gsum(b):
        return Sums(
            wires, at, core, 0, gu, lambda step: (b, core, rem(0, step)), FF, 2 * FF, *grows[b]
        )

    gsums = [gsum(0), gsum(1)]

    def join(b):
        halves[b].wait_recv()

        gu[b, core] = (gu[b, core].astype(jnp.float32) + gx[b].astype(jnp.float32)).astype(jnp.bfloat16)
        gsums[b].far()
        gsums[b].near()

    hspread = [
        Spread(wires, at, core, 0, hid, lambda step, b=b: (b, core, rem(0, step)),
               (slice(None), slice(0, 640)), (slice(None), slice(640, FF)))
        for b in (0, 1)
    ]
    hcross = [[], []]

    def cross(b, step):
        s = (b, core, rem(0, step))
        hcross[b].append(wires.start(hid.at[s], hid.at[s], partner))

    def activate(b):
        both = gsums[b].total()
        g, u = both[:, 0:FF], both[:, FF:2 * FF]
        hid[b, core, at[0]] = (g / (1.0 + jnp.exp(-g)) * u).astype(jnp.bfloat16)
        hspread[b].near()
        cross(b, 0)

    def hrelay(b):
        hspread[b].relay()
        cross(b, 3)
        cross(b, 1)

    def dsum(b, k):
        a1, a2 = PLANES[k]
        return Sums(
            wires, at, core, a1, dn, lambda step: spots(b, k, {a1: rem(a1, step)}), 512, FD,
            pa.at[b, k], pb.at[b, k], pc.at[b, k], pd.at[b, k],
        )

    def dsum2(b, k):
        a1, a2 = PLANES[k]
        return Sums(
            wires, at, core, a2, qs, lambda step: (b, k, rem(a2, step)), 512, FD,
            qa.at[b, k], qb.at[b, k], qc.at[b, k], qd.at[b, k],
        )

    ds = {(b, k): dsum(b, k) for b in (0, 1) for k in (0, 1)}
    ds2 = {(b, k): dsum2(b, k) for b in (0, 1) for k in (0, 1)}

    def contract(b):
        hspread[b].finish()
        cross(b, 2)
        for copy in hcross[b]:
            copy.wait_recv()
        for k in (0, 1):
            left = hid[b, k].reshape(256, FF)
            part = jnp.dot(left, vd[...], preferred_element_type=jnp.float32)
            dn[b, k] = part.astype(jnp.bfloat16).reshape(4, 4, 16, FD)
            ds[b, k].far()
            ds[b, k].near()

    def drelay(b):
        for k in (0, 1):
            ds[b, k].relay()

    def dturn(b):
        for k in (0, 1):
            qs[b, k] = ds[b, k].total().astype(jnp.bfloat16)
            ds2[b, k].far()
            ds2[b, k].near()

    def dend(b):
        for k in (0, 1):
            ds2[b, k].relay()
        for k in (0, 1):
            x = 2 * b + k
            fin[2 * x:2 * x + 2] = ds2[b, k].total().reshape(2, 8, FD)

    for j in range(4):
        for k in (0, 1):
            second[0, k, j].finish()
    loads[0].wait()
    loads[1].wait()
    project(0)
    for j in range(4):
        for k in (0, 1):
            second[1, k, j].finish()
    for m in movers:
        m.near()
    join(0)
    project(1)
    gsums[0].relay()
    join(1)
    for m in movers:
        m.relay()
    activate(0)
    gsums[1].relay()
    hrelay(0)
    activate(1)
    for m in movers:
        m.finish()
    for l in (0, 1):
        merge_far(l)
    loads[2].wait()
    for l in (0, 1):
        merge_near(l, 1, 0)
        merge_near(l, 0, 1)
    contract(0)
    hrelay(1)
    for l in (0, 1):
        merge_near(l, 0, 0)
        merge_near(l, 1, 1)
    contract(1)
    drelay(0)
    drelay(1)
    for l in (0, 1):
        merge_end(l)
    dturn(0)
    dturn(1)
    dend(0)
    dend(1)
    sent = [wires.start(fin.at[peer[0]], back.at[p], peer) for peer in line]
    back[p] = fin[p]
    for copy in sent:
        copy.wait_recv()
    for o in range(8):
        cols = slice(o * FD, (o + 1) * FD)
        middle[:, cols] = (rows[:, cols] + back[o]).astype(jnp.bfloat16)
    wires.close()


def dense(stream, gain, wg, wu, wd, table, leaving):
    vm, an = pl.BlockSpec(memory_space=pltpu.VMEM), pl.BlockSpec(memory_space=pl.ANY)
    sm = pl.BlockSpec(memory_space=pltpu.SMEM)
    bf, f32 = jnp.bfloat16, jnp.float32
    item = (576, 256)
    scratch = [
        pltpu.VMEM((FD, FF), bf), pltpu.VMEM((FD, FF), bf), pltpu.VMEM((FF, FD), bf),
        pltpu.VMEM((8, 8, FD), f32), pltpu.VMEM((8, 8, FD), f32),
        pltpu.VMEM((2, 2, 4, 4, 16, FD), bf),
        pltpu.VMEM((2, 2, 4, 64, 2 * FF), bf), pltpu.VMEM((2, 4, 64, 2 * FF), bf),
        pltpu.VMEM((2, 64, FF), bf), pltpu.VMEM((2, 64, FF), bf),
        pltpu.VMEM((2, 64, 2 * FF), bf), pltpu.VMEM((2, 64, 2 * FF), bf),
        pltpu.VMEM((2, 2, 4, 64, FF), bf),
        pltpu.VMEM((2, 2, 4, 4, 16, FD), bf),
    ]
    for lead in ((2, 2, 4, 16), (2, 2, 16)):
        if len(lead) == 3:
            scratch.append(pltpu.VMEM((2, 2, 4, 16, FD), bf))
        scratch += [
            pltpu.VMEM(lead + (512,), bf), pltpu.VMEM(lead + (FD - 512,), bf),
            pltpu.VMEM(lead + (FD,), bf), pltpu.VMEM(lead + (FD,), bf),
        ]
    scratch += [
        pltpu.VMEM((8, 8, FD), f32), pltpu.VMEM((8, 8, FD), f32),
        pltpu.VMEM((4, 2) + item, bf), pltpu.VMEM((4, 2) + item, bf),
        pltpu.VMEM((2, 2) + item, bf), pltpu.VMEM((2, 2) + item, bf),
        pltpu.VMEM((2, 2, 2) + item, bf), pltpu.VMEM((2, 2, 2) + item, bf),
        pltpu.SemaphoreType.DMA((5,)), pltpu.SemaphoreType.DMA((240,)), pltpu.SemaphoreType.DMA((240,)),
    ]
    return pl.pallas_call(
        dense_kernel,
        out_shape=(
            jax.ShapeDtypeStruct((8, 7168), bf),
            jax.ShapeDtypeStruct((2, 2) + item, bf),
        ),
        in_specs=[vm, vm, an, an, an, sm, an],
        out_specs=(vm, vm),
        scratch_shapes=scratch,
        compiler_params=pltpu.CompilerParams(
            collective_id=2, has_side_effects=True, vmem_limit_bytes=67043328
        ),
        name="dense",
    )(stream, gain, wg, wu, wd, table, leaving)


def route_kernel(mig, lens, table, got_len):
    at, core, p, t = place()
    def look(n, state):
        source, item = n // 2, lax.rem(n, 2)
        dest = mig[p * 16 + source, item]
        new = []
        for i, (count, s0, m0, s1, m1) in enumerate(state):
            aim = i * 4 + at[2] if i < 4 else at[1] * 4 + (i - 4)
            hit = dest == aim
            s0, m0 = jnp.where(hit & (count == 0), source, s0), jnp.where(hit & (count == 0), item, m0)
            s1, m1 = jnp.where(hit & (count == 1), source, s1), jnp.where(hit & (count == 1), item, m1)
            new.append((count + jnp.where(hit, 1, 0), s0, m0, s1, m1))
        return tuple(new)

    zero = jnp.int32(0)
    state = lax.fori_loop(0, 32, look, ((zero,) * 5,) * 8)

    for i in range(8):
        for n in range(4):
            table[i, n] = state[i][1 + n]
    row = at[1]
    for slot in (0, 1):
        source, item = state[0][1 + 2 * slot], state[0][2 + 2 * slot]
        for i in range(1, 4):
            source = jnp.where(row == i, state[i][1 + 2 * slot], source)
            item = jnp.where(row == i, state[i][2 + 2 * slot], item)
        got_len[slot] = lens[p * 16 + source, item]


def route(mig, lens):
    sm = pl.BlockSpec(memory_space=pltpu.SMEM)
    return pl.pallas_call(
        route_kernel,
        out_shape=(jax.ShapeDtypeStruct((8, 4), jnp.int32), jax.ShapeDtypeStruct((2,), jnp.int32)),
        in_specs=[sm, sm],
        out_specs=(sm, sm),
        name="route",
    )(mig, lens)


def on_device(
    queries,
    new_latent,
    resident,
    leaving,
    res_len,
    leave_len,
    mig_dest,
    stream,
    dense_gain,
    w_gate,
    w_up,
    w_down,
    moe_gain,
    expert_gate,
    expert_up,
    expert_down,
    expert_ids,
    gate_scores,
):
    table, moved_len = route(mig_dest, leave_len)
    middle, moved = dense(
        stream, dense_gain[None], w_gate, w_up, w_down, table, jnp.swapaxes(leaving, 2, 3)
    )
    arrived = jnp.swapaxes(moved, 2, 3)
    stay = resident.shape[0]
    context_stay = attend(queries[:stay], resident, res_len, new_latent[:stay])
    context_moved = attend(queries[stay:], arrived[:, 0], moved_len, new_latent[stay:])
    context = jnp.concatenate([context_stay, context_moved], axis=0)
    stream_out = moe(
        middle, moe_gain[None], expert_ids, gate_scores, expert_gate[0], expert_up[0], expert_down[0]
    )
    return (context, arrived, stream_out)


def solution(mesh):
    placed = (
        P(("dp", "tp"), None, None),
        P(("dp", "tp"), None),
        P(("dp", "tp"), None, None),
        P(("dp", "tp"), None, None, None),
        P(("dp", "tp")),
        P(),
        P(),
        P(("dp", "tp"), None),
        P(),
        P("dp", "tp"),
        P("dp", "tp"),
        P("tp", "dp"),
        P(),
        P("tp", None, "dp"),
        P("tp", None, "dp"),
        P("tp", "dp", None),
        P(("dp", "tp"), None),
        P(("dp", "tp"), None),
    )
    return jax.shard_map(
        on_device,
        mesh=mesh,
        in_specs=placed,
        out_specs=(
            P(("dp", "tp"), None, None),
            P(("dp", "tp"), None, None, None),
            P(("dp", "tp"), None),
        ),
        check_vma=False,
    )
```

```python
import functools

import jax
import jax.numpy as jnp
from jax import lax
from jax.experimental import pallas as pl
from jax.experimental.pallas import tpu as pltpu
from jax.sharding import PartitionSpec as P

MESH = pl.DeviceIdType.MESH

VDIM = 512
QKD = 192


EPS = 1e-06
ROUTE_SCALE = 2.5


def attend(queries, keys, lengths, newest):
    scale = QKD ** (-0.5)
    scores = jnp.einsum("rhl,rcl->rhc", queries, keys, preferred_element_type=jnp.float32) * scale
    positions = jnp.arange(keys.shape[1])
    valid = positions[None, None, :] < lengths[:, None, None]
    masked = jnp.where(valid, scores, -1e30)
    own_score = (
        jnp.einsum("rhl,rl->rh", queries, newest, preferred_element_type=jnp.float32) * scale
    )
    top = jnp.maximum(jnp.max(masked, axis=-1), own_score)
    expo = jnp.where(valid, jnp.exp(masked - top[..., None]), 0.0)
    own_expo = jnp.exp(own_score - top)
    total = jnp.sum(expo, axis=-1) + own_expo
    weights = (expo / total[..., None]).astype(jnp.bfloat16)
    own_weight = (own_expo / total).astype(jnp.bfloat16)
    context = jnp.einsum(
        "rhc,rcv->rhv", weights, keys[:, :, :VDIM], preferred_element_type=jnp.float32
    )
    context = context + own_weight.astype(jnp.float32)[..., None] * newest[:, None, :VDIM].astype(
        jnp.float32
    )
    return context.astype(jnp.bfloat16)


HALF = 3584
OFFS = (0, 1280, 2432)
DATA = (1280, 1152, 1152)
WIDE = (1280, 1280, 1152)
ORDERS = ((0, 1, 2), (1, 2, 0), (2, 0, 1))
CUT = 640


def place():
    p, t = lax.axis_index("dp"), lax.axis_index("tp")
    return [p // 2, t // 4, t % 4], p % 2, p, t


def device(at, core):
    return (at[0] * 2 + core, at[1] * 4 + at[2])


def beside(at, axis, step):
    return [lax.rem(at[a] + 4 + step, 4) if a == axis else at[a] for a in range(3)]


class Wires:
    def __init__(self, send, recv):
        self.send, self.recv, self.used = send, recv, 0
        self.open = []

    def start(self, src, dst, peer):
        i = self.used
        self.used += 1
        copy = pltpu.make_async_remote_copy(
            src_ref=src, dst_ref=dst, send_sem=self.send.at[i], recv_sem=self.recv.at[i],
            device_id=peer, device_id_type=MESH,
        )
        copy.start()
        self.open.append(copy)
        return copy

    def close(self):
        for copy in self.open:
            copy.wait_send()


def greet(peers):
    barrier = pltpu.get_barrier_semaphore()
    for peer in peers:
        pl.semaphore_signal(barrier, inc=1, device_id=peer, device_id_type=MESH)
    pl.semaphore_wait(barrier, len(peers))


def rms(rows, gain):
    mean_square = jnp.mean(rows * rows, axis=-1, keepdims=True)
    return (rows * lax.rsqrt(mean_square + EPS) * gain).astype(jnp.bfloat16)


def picks(axes_values):
    return tuple(axes_values)


def moe_kernel(
    middle, gain, ids, scores, eg, eu, ed, out,
    wgu, wd, acc, inner, swap, swap2, swap3, swap4,
    ag0, ag1, ag2, ot0, ot1, ot2, po0, po1, po2, pt0, pt1, pt2, pr0, pr1, pr2,
    ra0, ra1, ra2, rb0, rb1, rb2, rc0, rc1, rc2, rd0, rd1, rd2,
    q0, q1, q2, qa0, qa1, qa2, qb0, qb1, qb2, qc0, qc1, qc2, qd0, qd1, qd2,
    s0, s1, s2, sx0, sx1, sx2,
    load_sem, send_sem, recv_sem, xsend, xrecv,
):
    at, core, p, t = place()
    ag, ot, po, pt, pr = (ag0, ag1, ag2), (ot0, ot1, ot2), (po0, po1, po2), (pt0, pt1, pt2), (pr0, pr1, pr2)
    loads = [
        pltpu.make_async_copy(eg, wgu.at[:, 0:256], load_sem.at[0]),
        pltpu.make_async_copy(eu, wgu.at[:, 256:512], load_sem.at[1]),
        pltpu.make_async_copy(ed.at[:, 0:HALF], wd.at[0], load_sem.at[2]),
        pltpu.make_async_copy(ed.at[:, HALF:2 * HALF], wd.at[1], load_sem.at[3]),
    ]
    partner = device(at, 1 - core)
    greet([partner] + [device(beside(at, a, s), core) for a in range(3) for s in (1, 2, 3)])
    wires = Wires(send_sem, recv_sem)

    rows = middle[...].astype(jnp.float32)
    mixed = rms(rows, gain[...]).astype(jnp.float32)
    given = scores[...]
    share = given / jnp.sum(given, axis=1, keepdims=True) * ROUTE_SCALE
    lane = lax.broadcasted_iota(jnp.int32, (8, 128), 1)
    spread = jnp.zeros((8, 128), jnp.float32)
    for k in range(8):
        spread = spread + jnp.where(lane == ids[:, k:k + 1], share[:, k:k + 1], 0.0)
    high = spread.astype(jnp.bfloat16).astype(jnp.float32)
    low = (spread - high).astype(jnp.bfloat16).astype(jnp.float32)
    packed = high + pltpu.roll(low, 16, 1)
    is_one = core == 1
    swap[:, 0:HALF] = jnp.where(is_one, mixed[:, 0:HALF], mixed[:, HALF:])
    swap[:, HALF:] = packed
    over = wires.start(swap, swap2, partner)
    mine = jnp.where(is_one, mixed[:, HALF:], mixed[:, 0:HALF])
    over.wait_recv()
    theirs = swap2[:, 0:HALF]
    first = jnp.where(is_one, theirs, mine)
    second = jnp.where(is_one, mine, theirs)
    block = jnp.concatenate([first, second], axis=0).astype(jnp.bfloat16)
    other_pack = swap2[:, HALF:]
    pack = jnp.concatenate(
        [jnp.where(is_one, other_pack, packed), jnp.where(is_one, packed, other_pack)], axis=0
    ).astype(jnp.bfloat16)
    for k in range(3):
        ag[k][at[0], at[1], at[2], :, 0:DATA[k]] = block[:, OFFS[k]:OFFS[k] + DATA[k]]
    ag1[at[0], at[1], at[2], :, DATA[1]:WIDE[1]] = pack

    def spot(k, fixed):
        return tuple(fixed.get(a, slice(None)) for a in range(3))

    def cols(k, part):
        return slice(0, CUT) if part == 0 else slice(CUT, WIDE[k])

    def ring(k, axis, fixed):
        here = spot(k, fixed)
        up, down = device(beside(at, axis, 1), core), device(beside(at, axis, -1), core)
        a = wires.start(ag[k].at[here], ag[k].at[here], up)
        b = wires.start(ag[k].at[here], ag[k].at[here], down)
        return a, b

    def forward(k, axis, fixed, pair):
        up, down = device(beside(at, axis, 1), core), device(beside(at, axis, -1), core)
        below, above = dict(fixed), dict(fixed)
        below[axis], above[axis] = lax.rem(at[axis] + 3, 4), lax.rem(at[axis] + 1, 4)
        pair[0].wait_recv()
        s = spot(k, below) + (slice(None), cols(k, 0))
        a = wires.start(ag[k].at[s], ag[k].at[s], up)
        pair[1].wait_recv()
        s = spot(k, above) + (slice(None), cols(k, 1))
        b = wires.start(ag[k].at[s], ag[k].at[s], down)
        return a, b

    own = [{a: at[a] for a in range(3)} for _ in range(3)]
    pairs = []
    for k in range(3):
        here = spot(k, own[k])
        pairs.append([
            wires.start(ag[k].at[here], ag[k].at[here], device(beside(at, ORDERS[k][0], d), core))
            for d in (2, 1, 3)
        ])
    for load in loads:
        load.start()
    second_pairs, third = [None] * 3, [[], [], []]
    for k in range(3):
        a1, a2, a3 = ORDERS[k]
        for c in pairs[k]:
            c.wait_recv()
        fixed = {a2: at[a2], a3: at[a3]}
        second_pairs[k] = ring(k, a2, fixed)
        third[k].append((fixed, ring(k, a3, fixed)))
    done2 = [None] * 3
    for k in range(3):
        a1, a2, a3 = ORDERS[k]
        fixed = {a2: at[a2], a3: at[a3]}
        done2[k] = forward(k, a2, fixed, second_pairs[k])
        for step in (1, 3):
            fixed = {a2: lax.rem(at[a2] + step, 4), a3: at[a3]}
            third[k].append((fixed, ring(k, a3, fixed)))
    last = [[], [], []]
    for k in range(3):
        a1, a2, a3 = ORDERS[k]
        for c in done2[k]:
            c.wait_recv()
        fixed = {a2: lax.rem(at[a2] + 2, 4), a3: at[a3]}
        third[k].append((fixed, ring(k, a3, fixed)))

    def plane(k, step):
        return spot(k, {ORDERS[k][2]: lax.rem(at[ORDERS[k][2]] + step, 4)})

    across = [[None] * 4 for _ in range(3)]

    def hand(k, step):
        s = plane(k, step)
        across[k][step] = wires.start(ag[k].at[s], ot[k].at[s], partner)

    for k in range(3):
        hand(k, 0)
    loads[0].wait()
    loads[1].wait()

    def product(bufs, half, k, step, fresh):
        s = plane(k, step)
        left = bufs[k][s + (slice(None), slice(0, DATA[k]))].reshape(256, DATA[k])
        base = pl.multiple_of(half * HALF + OFFS[k], 128)
        part = jnp.dot(left, wgu[pl.ds(base, DATA[k]), :], preferred_element_type=jnp.float32)
        part = part.reshape(4, 4, 16, 512)
        acc[s] = acc[s] + part

    acc[...] = jnp.zeros_like(acc)
    for k in range(3):
        product(ag, core, k, 0, False)
    for n in range(4):
        for k in range(3):
            fixed, pair = third[k][n]
            last[k].append(forward(k, ORDERS[k][2], fixed, pair))
    for k in range(3):
        hand(k, 1)
        hand(k, 3)

    def side(n, _):
        for k in range(3):
            product(ag, core, k, 2 * n + 1, False)
        return _

    lax.fori_loop(0, 2, side, 0)
    for k in range(3):
        for step in (0, 1, 3):
            across[k][step].wait_recv()

    def side_other(n, _):
        for k in range(3):
            product(ot, 1 - core, k, n + n // 2, False)
        return _

    lax.fori_loop(0, 3, side_other, 0)
    tails = [[], [], []]
    for n in range(4):
        for k in range(3):
            a2, a3 = ORDERS[k][1:]
            for c in last[k][n]:
                c.wait_recv()
            s = spot(k, {a2: third[k][n][0][a2], a3: lax.rem(at[a3] + 2, 4)})
            tails[k].append(wires.start(ag[k].at[s], ot[k].at[s], partner))
    for k in range(3):
        product(ag, core, k, 2, False)
    for k in range(3):
        for c in tails[k]:
            c.wait_recv()
        product(ot, 1 - core, k, 2, False)

    lane = lax.broadcasted_iota(jnp.int32, (256, 128), 1)

    def activate(n, _):
        both = acc[n].reshape(256, 512)
        gate, up = both[:, 0:256], both[:, 256:512]
        packs = ag1[n, :, :, :, DATA[1]:WIDE[1]].reshape(256, 128).astype(jnp.float32)
        keep = (lane == t) | (lane == t + 16)
        weight = jnp.sum(jnp.where(keep, packs, 0.0), axis=1, keepdims=True)
        value = gate / (1.0 + jnp.exp(-gate)) * up * weight
        inner[n] = value.astype(jnp.bfloat16).reshape(4, 4, 16, 256)
        return _

    lax.fori_loop(0, 4, activate, 0)
    loads[2].wait()
    loads[3].wait()

    def group(k, step):
        a1 = ORDERS[k][0]
        return spot(k, {a1: lax.rem(at[a1] + step, 4)})

    def trade(k, n, step):
        s = group(k, step)
        return pltpu.make_async_remote_copy(
            src_ref=pt[k].at[s], dst_ref=pr[k].at[s], send_sem=xsend.at[k, n], recv_sem=xrecv.at[k, n],
            device_id=partner, device_id_type=MESH,
        )

    def step_of(n):
        return lax.rem(n * 3 + 2, 4) if not isinstance(n, int) else (n * 3 + 2) % 4

    def expand(n, _):
        for k in range(3):
            s = group(k, step_of(n))
            left = inner[s].reshape(256, 256)
            part = jnp.dot(left, wd[1 - core, :, OFFS[k]:OFFS[k] + DATA[k]], preferred_element_type=jnp.float32)
            pt[k][s] = part.astype(jnp.bfloat16).reshape(4, 4, 16, DATA[k])
            trade(k, n, step_of(n)).start()
            part = jnp.dot(left, wd[core, :, OFFS[k]:OFFS[k] + DATA[k]], preferred_element_type=jnp.float32)
            po[k][s] = part.astype(jnp.bfloat16).reshape(4, 4, 16, DATA[k])
        return _

    def meet(k, n):
        trade(k, n, step_of(n)).wait_recv()
        s = group(k, step_of(n))
        po[k][s] = (po[k][s].astype(jnp.float32) + pr[k][s].astype(jnp.float32)).astype(jnp.bfloat16)

    sums = [
        Sums(
            wires, at, core, ORDERS[k][0], po[k], lambda step, k=k: group(k, step), CUT, DATA[k],
            (ra0, ra1, ra2)[k], (rb0, rb1, rb2)[k], (rc0, rc1, rc2)[k], (rd0, rd1, rd2)[k],
        )
        for k in range(3)
    ]
    lax.fori_loop(0, 2, expand, 0)
    for k in range(3):
        meet(k, 0)
        sums[k].far()
    lax.fori_loop(2, 4, expand, 0)
    for k in range(3):
        meet(k, 1)
        meet(k, 3)
        sums[k].near()
    for k in range(3):
        sums[k].relay()
    for k in range(3):
        meet(k, 2)
    q = (q0, q1, q2)

    def group2(k, step):
        a1, a2, a3 = ORDERS[k]
        rest = [a for a in range(3) if a != a1]
        return tuple(lax.rem(at[a] + step, 4) if a == a2 else slice(None) for a in rest)

    sums2 = [
        Sums(
            wires, at, core, ORDERS[k][1], q[k], lambda step, k=k: group2(k, step), CUT, DATA[k],
            (qa0, qa1, qa2)[k], (qb0, qb1, qb2)[k], (qc0, qc1, qc2)[k], (qd0, qd1, qd2)[k],
        )
        for k in range(3)
    ]
    for k in range(3):
        q[k][...] = sums[k].total().astype(jnp.bfloat16)
        sums2[k].far()
        sums2[k].near()
    for k in range(3):
        sums2[k].relay()
    s_, sx = (s0, s1, s2), (sx0, sx1, sx2)
    final = []
    for k in range(3):
        s_[k][...] = sums2[k].total().astype(jnp.bfloat16)
        a3 = ORDERS[k][2]
        final.append([
            wires.start(s_[k].at[lax.rem(at[a3] + d, 4)], sx[k].at[d - 1], device(beside(at, a3, d), core))
            for d in (2, 1, 3)
        ])
    for k in range(3):
        for copy in final[k]:
            copy.wait_recv()
        total = s_[k][at[ORDERS[k][2]]].astype(jnp.float32)
        for d in range(3):
            total = total + sx[k][d].astype(jnp.float32)
        swap3[:, :, OFFS[k]:OFFS[k] + DATA[k]] = total.reshape(2, 8, DATA[k])
    over = wires.start(swap3.at[1 - core], swap4, partner)
    over.wait_recv()
    lead = jnp.where(is_one, swap4[...], swap3[0])
    tail = jnp.where(is_one, swap3[1], swap4[...])
    out[:, 0:HALF] = (rows[:, 0:HALF] + lead).astype(jnp.bfloat16)
    out[:, HALF:] = (rows[:, HALF:] + tail).astype(jnp.bfloat16)
    for k in range(3):
        for n in range(4):
            trade(k, n, step_of(n)).wait_send()
    wires.close()


def moe(middle, gain, ids, scores, eg, eu, ed):
    vm, an = pl.BlockSpec(memory_space=pltpu.VMEM), pl.BlockSpec(memory_space=pl.ANY)
    bf = jnp.bfloat16

    def three(shape, widths):
        return [pltpu.VMEM(shape + (w,), bf) for w in widths]

    lead, rest = (CUT,) * 3, tuple(w - CUT for w in DATA)
    cube, face, line, row = (4, 4, 4, 16), (4, 4, 16), (4, 16), (16,)
    scratch = [
        pltpu.VMEM((7168, 512), bf),
        pltpu.VMEM((2, 256, HALF), bf),
        pltpu.VMEM((4, 4, 4, 16, 512), jnp.float32),
        pltpu.VMEM((4, 4, 4, 16, 256), bf),
        pltpu.VMEM((8, HALF + 128), jnp.float32),
        pltpu.VMEM((8, HALF + 128), jnp.float32),
        pltpu.VMEM((2, 8, HALF), jnp.float32),
        pltpu.VMEM((8, HALF), jnp.float32),
    ]
    scratch += three(cube, WIDE) + three(cube, WIDE)
    scratch += three(cube, DATA) + three(cube, DATA) + three(cube, DATA)
    scratch += three(face, lead) + three(face, rest) + three(face, DATA) + three(face, DATA)
    scratch += three((4,) + line, DATA)
    scratch += three(line, lead) + three(line, rest) + three(line, DATA) + three(line, DATA)
    scratch += three((4,) + row, DATA) + three((3,) + row, DATA)
    scratch += [
        pltpu.SemaphoreType.DMA((4,)),
        pltpu.SemaphoreType.DMA((160,)),
        pltpu.SemaphoreType.DMA((160,)),
        pltpu.SemaphoreType.DMA((3, 4)),
        pltpu.SemaphoreType.DMA((3, 4)),
    ]
    return pl.pallas_call(
        moe_kernel,
        out_shape=jax.ShapeDtypeStruct((8, 7168), bf),
        in_specs=[vm, vm, vm, vm, an, an, an],
        out_specs=vm,
        scratch_shapes=scratch,
        compiler_params=pltpu.CompilerParams(
            collective_id=1, has_side_effects=True, vmem_limit_bytes=67043328
        ),
        name="experts",
    )(middle, gain, ids, scores, eg, eu, ed)


class Sums:
    def __init__(self, wires, at, core, axis, buf, index, cut, width, ra, rb, rc, rd):
        self.wires, self.buf, self.index = wires, buf, index
        self.up, self.down = device(beside(at, axis, 1), core), device(beside(at, axis, -1), core)
        self.lead, self.rest = (slice(None), slice(0, cut)), (slice(None), slice(cut, width))
        self.ra, self.rb, self.rc, self.rd = ra, rb, rc, rd

    def part(self, ref, cols):
        return ref.at[(slice(None),) * (len(ref.shape) - 2) + cols]

    def far(self):
        s = self.index(2)
        self.a = self.wires.start(self.buf.at[s + self.lead], self.ra, self.down)
        self.b = self.wires.start(self.buf.at[s + self.rest], self.rb, self.up)

    def near(self):
        left, right = self.index(3), self.index(1)
        self.c = self.wires.start(self.buf.at[left + self.rest], self.part(self.rc, self.rest), self.down)
        self.d = self.wires.start(self.buf.at[right + self.lead], self.part(self.rd, self.lead), self.up)

    def add(self, s, other):
        self.buf[s] = (self.buf[s].astype(jnp.float32) + other[...].astype(jnp.float32)).astype(jnp.bfloat16)

    def relay(self):
        self.a.wait_recv()
        s = self.index(3) + self.lead
        self.add(s, self.ra)
        self.e = self.wires.start(self.buf.at[s], self.part(self.rc, self.lead), self.down)
        self.b.wait_recv()
        s = self.index(1) + self.rest
        self.add(s, self.rb)
        self.f = self.wires.start(self.buf.at[s], self.part(self.rd, self.rest), self.up)

    def total(self):
        for copy in (self.c, self.d, self.e, self.f):
            copy.wait_recv()
        return (
            self.buf[self.index(0)].astype(jnp.float32)
            + self.rc[...].astype(jnp.float32)
            + self.rd[...].astype(jnp.float32)
        )


class Spread:
    def __init__(self, wires, at, core, axis, buf, index, lead, rest):
        self.wires, self.buf, self.index, self.lead, self.rest = wires, buf, index, lead, rest
        self.up, self.down = device(beside(at, axis, 1), core), device(beside(at, axis, -1), core)

    def near(self):
        s = self.index(0)
        self.a = self.wires.start(self.buf.at[s], self.buf.at[s], self.up)
        self.b = self.wires.start(self.buf.at[s], self.buf.at[s], self.down)

    def relay(self):
        self.a.wait_recv()
        s = self.index(3) + self.lead
        self.c = self.wires.start(self.buf.at[s], self.buf.at[s], self.up)
        self.b.wait_recv()
        s = self.index(1) + self.rest
        self.d = self.wires.start(self.buf.at[s], self.buf.at[s], self.down)

    def finish(self):
        self.c.wait_recv()
        self.d.wait_recv()


PLANES = ((1, 2), (2, 1))
FF = 1152
FD = 896


def dense_kernel(
    stream, gain, wg, wu, wd, table, leaving, middle, arrived,
    vg, vu, vd, nbuf, land, ft, gu, gx, gra, grb, grc, grd, hid, dn,
    pa, pb, pc, pd, qs, qx, fin, back,
    held0, held1, far_out, far_in, near_out, near_in,
    load_sem, send_sem, recv_sem,
):
    at, core, p, t = place()
    loads = [
        pltpu.make_async_copy(wg, vg, load_sem.at[0]),
        pltpu.make_async_copy(wu, vu, load_sem.at[1]),
        pltpu.make_async_copy(wd, vd, load_sem.at[2]),
        pltpu.make_async_copy(leaving.at[:, 0], held0.at[at[2]], load_sem.at[3]),
        pltpu.make_async_copy(leaving.at[:, 1], held1.at[at[1]], load_sem.at[4]),
    ]
    partner = device(at, 1 - core)
    line = [(lax.rem(p + q, 8), t) for q in range(1, 8)]
    greet(line + [device(beside(at, a, s), core) for a in (1, 2) for s in (1, 2, 3)])
    wires = Wires(send_sem, recv_sem)

    rows = stream[...].astype(jnp.float32)
    normed = rms(rows, gain[...]).astype(jnp.float32)
    for o in range(8):
        nbuf[o] = normed[:, o * FD:(o + 1) * FD]
    sent = [wires.start(nbuf.at[peer[0]], land.at[p], peer) for peer in line]
    for load in loads:
        load.start()
    land[p] = nbuf[p]

    for copy in sent:
        copy.wait_recv()
    for x in range(4):
        ft[x // 2, x % 2, at[1], at[2]] = land[2 * x:2 * x + 2].reshape(16, FD).astype(jnp.bfloat16)

    def spots(b, k, fixed):
        return (b, k) + tuple(fixed.get(a, slice(None)) for a in (1, 2))

    fcut = ((slice(None), slice(0, 512)), (slice(None), slice(512, FD)))

    def spread_of(b, k, axis, other):
        def index(step):
            fixed = dict(other)
            fixed[axis] = lax.rem(at[axis] + step, 4)
            return spots(b, k, fixed)

        return Spread(wires, at, core, axis, ft, index, *fcut)

    def rem(axis, step):
        return lax.rem(at[axis] + step, 4)

    first = {}
    second = {
        (b, k, j): spread_of(b, k, PLANES[k][1], {PLANES[k][0]: rem(PLANES[k][0], j)})
        for b in (0, 1) for k in (0, 1) for j in range(4)
    }
    for b in (0, 1):
        for k in (0, 1):
            here = (b, k, at[1], at[2])
            first[b, k] = [
                wires.start(ft.at[here], ft.at[here], device(beside(at, PLANES[k][0], d), core)) for d in (1, 3, 2)
            ]
            second[b, k, 0].near()
    for b in (0, 1):
        for k in (0, 1):
            first[b, k][0].wait_recv()
            second[b, k, 3].near()
            first[b, k][1].wait_recv()
            second[b, k, 1].near()
            first[b, k][2].wait_recv()
            second[b, k, 2].near()
        for k in (0, 1):
            second[b, k, 0].relay()
    for b in (0, 1):
        for j in (3, 1, 2):
            for k in (0, 1):
                second[b, k, j].relay()

    loads[3].wait()
    loads[4].wait()

    held = (held0, held1)

    def mover(l):
        a1 = (2, 1)[l]

        def index(step):
            return (rem(a1, step),)

        return Spread(wires, at, core, a1, held[l], index, (0,), (1,))

    movers = [mover(0), mover(1)]

    def mine(l, step, slot):
        a1, a2 = ((2, 1), (1, 2))[l]
        row = l * 4 + rem(a2, step)
        pick = table[row, slot]
        source, item = pick // 2, lax.rem(pick, 2)
        y, z = source // 4, lax.rem(source, 4)
        j, i = (z, y) if l == 0 else (y, z)
        return i, j, item

    peers2 = [[device(beside(at, a2, 1), core), device(beside(at, a2, -1), core)] for a2 in (1, 2)]
    far_copies, near_copies = {}, {}

    def merge_far(l):
        for slot in (0, 1):
            i, j, item = mine(l, 2, slot)
            far_out[l, slot] = held[l][j, item]
            far_copies[l, slot] = wires.start(far_out.at[l, slot], far_in.at[l, slot], peers2[l][1 - slot])

    def merge_near(l, slot, side):
        step = (3, 1)[side]
        i, j, item = mine(l, step, slot)
        if slot == side:
            far_copies[l, slot].wait_recv()
            a2 = (1, 2)[l]
            near_out[l, side, slot] = jnp.where(i == at[a2], held[l][j, item], far_in[l, slot])
        else:
            near_out[l, side, slot] = held[l][j, item]
        near_copies[l, side, slot] = wires.start(
            near_out.at[l, side, slot], near_in.at[l, side, slot], peers2[l][1 - side]
        )

    def merge_end(l):
        a2 = (1, 2)[l]
        for side in (0, 1):
            for slot in (0, 1):
                near_copies[l, side, slot].wait_recv()
        for slot in (0, 1):
            i, j, item = mine(l, 0, slot)
            delta = lax.rem(i - at[a2] + 4, 4)
            from_above = (delta == 1) | ((delta == 2) if slot == 0 else (delta == 5))
            other = jnp.where(from_above, near_in[l, 0, slot], near_in[l, 1, slot])
            arrived[slot, l] = jnp.where(delta == 0, held[l][j, item], other)

    grows = [(gra.at[b], grb.at[b], grc.at[b], grd.at[b]) for b in (0, 1)]
    halves = [None, None]

    def project(b):
        for h in (0, 1):
            c = (1 - core) if h == 0 else core
            left = ft[b, c].reshape(256, FD)
            g = jnp.dot(left, vg[...], preferred_element_type=jnp.float32).astype(jnp.bfloat16)
            gu[b, c, :, :, 0:FF] = g.reshape(4, 64, FF)
            u = jnp.dot(left, vu[...], preferred_element_type=jnp.float32).astype(jnp.bfloat16)
            gu[b, c, :, :, FF:2 * FF] = u.reshape(4, 64, FF)
            if h == 0:
                halves[b] = wires.start(gu.at[b, c], gx.at[b], partner)

    def gsum(b):
        return Sums(
            wires, at, core, 0, gu, lambda step: (b, core, rem(0, step)), FF, 2 * FF, *grows[b]
        )

    gsums = [gsum(0), gsum(1)]

    def join(b):
        halves[b].wait_recv()

        gu[b, core] = (gu[b, core].astype(jnp.float32) + gx[b].astype(jnp.float32)).astype(jnp.bfloat16)
        gsums[b].far()
        gsums[b].near()

    hspread = [
        Spread(wires, at, core, 0, hid, lambda step, b=b: (b, core, rem(0, step)),
               (slice(None), slice(0, 640)), (slice(None), slice(640, FF)))
        for b in (0, 1)
    ]
    hcross = [[], []]

    def cross(b, step):
        s = (b, core, rem(0, step))
        hcross[b].append(wires.start(hid.at[s], hid.at[s], partner))

    def activate(b):
        both = gsums[b].total()
        g, u = both[:, 0:FF], both[:, FF:2 * FF]
        hid[b, core, at[0]] = (g / (1.0 + jnp.exp(-g)) * u).astype(jnp.bfloat16)
        hspread[b].near()
        cross(b, 0)

    def hrelay(b):
        hspread[b].relay()
        cross(b, 3)
        cross(b, 1)

    def dsum(b, k):
        a1, a2 = PLANES[k]
        return Sums(
            wires, at, core, a1, dn, lambda step: spots(b, k, {a1: rem(a1, step)}), 512, FD,
            pa.at[b, k], pb.at[b, k], pc.at[b, k], pd.at[b, k],
        )

    ds = {(b, k): dsum(b, k) for b in (0, 1) for k in (0, 1)}
    ds2 = {}

    def contract(b):
        hspread[b].finish()
        cross(b, 2)
        for copy in hcross[b]:
            copy.wait_recv()
        for k in (0, 1):
            left = hid[b, k].reshape(256, FF)
            part = jnp.dot(left, vd[...], preferred_element_type=jnp.float32)
            dn[b, k] = part.astype(jnp.bfloat16).reshape(4, 4, 16, FD)
            ds[b, k].far()
            ds[b, k].near()

    def drelay(b):
        for k in (0, 1):
            ds[b, k].relay()

    def dturn(b):
        for k in (0, 1):
            qs[b, k] = ds[b, k].total().astype(jnp.bfloat16)
            a2 = PLANES[k][1]
            ds2[b, k] = [
                wires.start(qs.at[b, k, rem(a2, d)], qx.at[b, k, d - 1], device(beside(at, a2, d), core))
                for d in (2, 1, 3)
            ]

    def dend(b):
        for k in (0, 1):
            x = 2 * b + k
            for copy in ds2[b, k]:
                copy.wait_recv()
            total = qs[b, k, at[PLANES[k][1]]].astype(jnp.float32)
            for d in range(3):
                total = total + qx[b, k, d].astype(jnp.float32)
            fin[2 * x:2 * x + 2] = total.reshape(2, 8, FD)

    for j in range(4):
        for k in (0, 1):
            second[0, k, j].finish()
    loads[0].wait()
    loads[1].wait()
    project(0)
    for j in range(4):
        for k in (0, 1):
            second[1, k, j].finish()
    for m in movers:
        m.near()
    project(1)
    join(0)
    join(1)
    gsums[0].relay()
    for m in movers:
        m.relay()
    gsums[1].relay()
    activate(0)
    for m in movers:
        m.finish()
    for l in (0, 1):
        merge_far(l)
    for l in (0, 1):
        merge_near(l, 1, 0)
        merge_near(l, 0, 1)
    activate(1)
    hrelay(0)
    for l in (0, 1):
        merge_near(l, 0, 0)
        merge_near(l, 1, 1)
    hrelay(1)
    loads[2].wait()
    contract(0)
    contract(1)
    drelay(0)
    drelay(1)
    for l in (0, 1):
        merge_end(l)
    dturn(0)
    dturn(1)
    dend(0)
    dend(1)
    sent = [wires.start(fin.at[peer[0]], back.at[p], peer) for peer in line]
    back[p] = fin[p]
    for copy in sent:
        copy.wait_recv()
    for o in range(8):
        cols = slice(o * FD, (o + 1) * FD)
        middle[:, cols] = (rows[:, cols] + back[o]).astype(jnp.bfloat16)
    wires.close()


def dense(stream, gain, wg, wu, wd, table, leaving):
    vm, an = pl.BlockSpec(memory_space=pltpu.VMEM), pl.BlockSpec(memory_space=pl.ANY)
    sm = pl.BlockSpec(memory_space=pltpu.SMEM)
    bf, f32 = jnp.bfloat16, jnp.float32
    item = (576, 256)
    scratch = [
        pltpu.VMEM((FD, FF), bf), pltpu.VMEM((FD, FF), bf), pltpu.VMEM((FF, FD), bf),
        pltpu.VMEM((8, 8, FD), f32), pltpu.VMEM((8, 8, FD), f32),
        pltpu.VMEM((2, 2, 4, 4, 16, FD), bf),
        pltpu.VMEM((2, 2, 4, 64, 2 * FF), bf), pltpu.VMEM((2, 4, 64, 2 * FF), bf),
        pltpu.VMEM((2, 64, FF), bf), pltpu.VMEM((2, 64, FF), bf),
        pltpu.VMEM((2, 64, 2 * FF), bf), pltpu.VMEM((2, 64, 2 * FF), bf),
        pltpu.VMEM((2, 2, 4, 64, FF), bf),
        pltpu.VMEM((2, 2, 4, 4, 16, FD), bf),
    ]
    lead = (2, 2, 4, 16)
    scratch += [
        pltpu.VMEM(lead + (512,), bf), pltpu.VMEM(lead + (FD - 512,), bf),
        pltpu.VMEM(lead + (FD,), bf), pltpu.VMEM(lead + (FD,), bf),
        pltpu.VMEM((2, 2, 4, 16, FD), bf), pltpu.VMEM((2, 2, 3, 16, FD), bf),
        pltpu.VMEM((8, 8, FD), f32), pltpu.VMEM((8, 8, FD), f32),
        pltpu.VMEM((4, 2) + item, bf), pltpu.VMEM((4, 2) + item, bf),
        pltpu.VMEM((2, 2) + item, bf), pltpu.VMEM((2, 2) + item, bf),
        pltpu.VMEM((2, 2, 2) + item, bf), pltpu.VMEM((2, 2, 2) + item, bf),
        pltpu.SemaphoreType.DMA((5,)), pltpu.SemaphoreType.DMA((240,)), pltpu.SemaphoreType.DMA((240,)),
    ]
    return pl.pallas_call(
        dense_kernel,
        out_shape=(
            jax.ShapeDtypeStruct((8, 7168), bf),
            jax.ShapeDtypeStruct((2, 2) + item, bf),
        ),
        in_specs=[vm, vm, an, an, an, sm, an],
        out_specs=(vm, vm),
        scratch_shapes=scratch,
        compiler_params=pltpu.CompilerParams(
            collective_id=2, has_side_effects=True, vmem_limit_bytes=67043328
        ),
        name="dense",
    )(stream, gain, wg, wu, wd, table, leaving)


def route(mig_dest, leave_len):
    p, t = lax.axis_index("dp"), lax.axis_index("tp")
    group = lax.dynamic_slice_in_dim(mig_dest, p * 16, 16, 0).reshape(1, 32)
    lens = lax.dynamic_slice_in_dim(leave_len, p * 16, 16, 0).reshape(1, 32)
    step = jnp.arange(4)
    aims = jnp.concatenate([step * 4 + t % 4, t // 4 * 4 + step, t[None]])[:, None]
    hit = group == aims
    order = jnp.arange(32)[None, :]
    low = jnp.min(jnp.where(hit, order, 32), axis=1)
    high = jnp.max(jnp.where(hit, order, -1), axis=1)
    ends = jnp.stack([low, high], axis=1)
    got = jnp.sum(jnp.where(order == ends[8][:, None], lens, 0), axis=1)
    return ends, got


def on_device(
    queries,
    new_latent,
    resident,
    leaving,
    res_len,
    leave_len,
    mig_dest,
    stream,
    dense_gain,
    w_gate,
    w_up,
    w_down,
    moe_gain,
    expert_gate,
    expert_up,
    expert_down,
    expert_ids,
    gate_scores,
):
    table, moved_len = route(mig_dest, leave_len)
    middle, moved = dense(
        stream, dense_gain[None], w_gate, w_up, w_down, table, jnp.swapaxes(leaving, 2, 3)
    )
    arrived = jnp.swapaxes(moved, 2, 3)
    stay = resident.shape[0]
    context_stay = attend(queries[:stay], resident, res_len, new_latent[:stay])
    context_moved = attend(queries[stay:], arrived[:, 0], moved_len, new_latent[stay:])
    context = jnp.concatenate([context_stay, context_moved], axis=0)
    stream_out = moe(
        middle, moe_gain[None], expert_ids, gate_scores, expert_gate[0], expert_up[0], expert_down[0]
    )
    return (context, arrived, stream_out)


def solution(mesh):
    placed = (
        P(("dp", "tp"), None, None),
        P(("dp", "tp"), None),
        P(("dp", "tp"), None, None),
        P(("dp", "tp"), None, None, None),
        P(("dp", "tp")),
        P(),
        P(),
        P(("dp", "tp"), None),
        P(),
        P("dp", "tp"),
        P("dp", "tp"),
        P("tp", "dp"),
        P(),
        P("tp", None, "dp"),
        P("tp", None, "dp"),
        P("tp", "dp", None),
        P(("dp", "tp"), None),
        P(("dp", "tp"), None),
    )
    return jax.shard_map(
        on_device,
        mesh=mesh,
        in_specs=placed,
        out_specs=(
            P(("dp", "tp"), None, None),
            P(("dp", "tp"), None, None, None),
            P(("dp", "tp"), None),
        ),
        check_vma=False,
    )
```

```python
import functools

import jax
import jax.numpy as jnp
from jax import lax
from jax.experimental import pallas as pl
from jax.experimental.pallas import tpu as pltpu
from jax.sharding import PartitionSpec as P

MESH = pl.DeviceIdType.MESH

VDIM = 512
QKD = 192


EPS = 1e-06
ROUTE_SCALE = 2.5


HALF = 3584
OFFS = (0, 1280, 2432)
DATA = (1280, 1152, 1152)
WIDE = (1280, 1280, 1152)
ORDERS = ((0, 1, 2), (1, 2, 0), (2, 0, 1))
CUT = 640


def place():
    p, t = lax.axis_index("dp"), lax.axis_index("tp")
    return [p // 2, t // 4, t % 4], p % 2, p, t


def device(at, core):
    return (at[0] * 2 + core, at[1] * 4 + at[2])


def beside(at, axis, step):
    return [lax.rem(at[a] + 4 + step, 4) if a == axis else at[a] for a in range(3)]


class Wires:
    def __init__(self, send, recv):
        self.send, self.recv, self.used = send, recv, 0
        self.open = []

    def start(self, src, dst, peer):
        i = self.used
        self.used += 1
        copy = pltpu.make_async_remote_copy(
            src_ref=src, dst_ref=dst, send_sem=self.send.at[i], recv_sem=self.recv.at[i],
            device_id=peer, device_id_type=MESH,
        )
        copy.start()
        self.open.append(copy)
        return copy

    def close(self):
        for copy in self.open:
            copy.wait_send()


def greet(peers):
    barrier = pltpu.get_barrier_semaphore()
    for peer in peers:
        pl.semaphore_signal(barrier, inc=1, device_id=peer, device_id_type=MESH)
    pl.semaphore_wait(barrier, len(peers))


def rms(rows, gain):
    mean_square = jnp.mean(rows * rows, axis=-1, keepdims=True)
    return (rows * lax.rsqrt(mean_square + EPS) * gain).astype(jnp.bfloat16)


def picks(axes_values):
    return tuple(axes_values)


def moe_kernel(
    middle, gain, ids, scores, eg, eu, ed, out,
    wgu, wd, acc, inner, swap, swap2, swap3, swap4,
    ag0, ag1, ag2, ot0, ot1, ot2, po0, po1, po2, pt0, pt1, pt2, pr0, pr1, pr2,
    ra0, ra1, ra2, rb0, rb1, rb2, rc0, rc1, rc2, rd0, rd1, rd2,
    q0, q1, q2, qa0, qa1, qa2, qb0, qb1, qb2, qc0, qc1, qc2, qd0, qd1, qd2,
    s0, s1, s2, sx0, sx1, sx2,
    load_sem, send_sem, recv_sem, xsend, xrecv,
):
    at, core, p, t = place()
    ag, ot, po, pt, pr = (ag0, ag1, ag2), (ot0, ot1, ot2), (po0, po1, po2), (pt0, pt1, pt2), (pr0, pr1, pr2)
    loads = [
        pltpu.make_async_copy(eg, wgu.at[:, 0:256], load_sem.at[0]),
        pltpu.make_async_copy(eu, wgu.at[:, 256:512], load_sem.at[1]),
        pltpu.make_async_copy(ed.at[:, 0:HALF], wd.at[0], load_sem.at[2]),
        pltpu.make_async_copy(ed.at[:, HALF:2 * HALF], wd.at[1], load_sem.at[3]),
    ]
    partner = device(at, 1 - core)
    greet([partner] + [device(beside(at, a, s), core) for a in range(3) for s in (1, 2, 3)])
    wires = Wires(send_sem, recv_sem)

    rows = middle[...].astype(jnp.float32)
    mixed = rms(rows, gain[...]).astype(jnp.float32)
    given = scores[...]
    share = given / jnp.sum(given, axis=1, keepdims=True) * ROUTE_SCALE
    lane = lax.broadcasted_iota(jnp.int32, (8, 128), 1)
    spread = jnp.zeros((8, 128), jnp.float32)
    for k in range(8):
        spread = spread + jnp.where(lane == ids[:, k:k + 1], share[:, k:k + 1], 0.0)
    high = spread.astype(jnp.bfloat16).astype(jnp.float32)
    low = (spread - high).astype(jnp.bfloat16).astype(jnp.float32)
    packed = high + pltpu.roll(low, 16, 1)
    is_one = core == 1
    swap[:, 0:HALF] = jnp.where(is_one, mixed[:, 0:HALF], mixed[:, HALF:])
    swap[:, HALF:] = packed
    over = wires.start(swap, swap2, partner)
    mine = jnp.where(is_one, mixed[:, HALF:], mixed[:, 0:HALF])
    over.wait_recv()
    theirs = swap2[:, 0:HALF]
    first = jnp.where(is_one, theirs, mine)
    second = jnp.where(is_one, mine, theirs)
    block = jnp.concatenate([first, second], axis=0).astype(jnp.bfloat16)
    other_pack = swap2[:, HALF:]
    pack = jnp.concatenate(
        [jnp.where(is_one, other_pack, packed), jnp.where(is_one, packed, other_pack)], axis=0
    ).astype(jnp.bfloat16)
    for k in range(3):
        ag[k][at[0], at[1], at[2], :, 0:DATA[k]] = block[:, OFFS[k]:OFFS[k] + DATA[k]]
    ag1[at[0], at[1], at[2], :, DATA[1]:WIDE[1]] = pack

    def spot(k, fixed):
        return tuple(fixed.get(a, slice(None)) for a in range(3))

    def cols(k, part):
        return slice(0, CUT) if part == 0 else slice(CUT, WIDE[k])

    def ring(k, axis, fixed):
        here = spot(k, fixed)
        up, down = device(beside(at, axis, 1), core), device(beside(at, axis, -1), core)
        a = wires.start(ag[k].at[here], ag[k].at[here], up)
        b = wires.start(ag[k].at[here], ag[k].at[here], down)
        return a, b

    def forward(k, axis, fixed, pair):
        up, down = device(beside(at, axis, 1), core), device(beside(at, axis, -1), core)
        below, above = dict(fixed), dict(fixed)
        below[axis], above[axis] = lax.rem(at[axis] + 3, 4), lax.rem(at[axis] + 1, 4)
        pair[0].wait_recv()
        s = spot(k, below) + (slice(None), cols(k, 0))
        a = wires.start(ag[k].at[s], ag[k].at[s], up)
        pair[1].wait_recv()
        s = spot(k, above) + (slice(None), cols(k, 1))
        b = wires.start(ag[k].at[s], ag[k].at[s], down)
        return a, b

    own = [{a: at[a] for a in range(3)} for _ in range(3)]
    pairs = []
    for k in range(3):
        here = spot(k, own[k])
        pairs.append([
            wires.start(ag[k].at[here], ag[k].at[here], device(beside(at, ORDERS[k][0], d), core))
            for d in (2, 1, 3)
        ])
    for load in loads:
        load.start()
    second_pairs, third = [None] * 3, [[], [], []]
    for k in range(3):
        a1, a2, a3 = ORDERS[k]
        for c in pairs[k]:
            c.wait_recv()
        fixed = {a2: at[a2], a3: at[a3]}
        second_pairs[k] = ring(k, a2, fixed)
        third[k].append((fixed, ring(k, a3, fixed)))
    done2 = [None] * 3
    for k in range(3):
        a1, a2, a3 = ORDERS[k]
        fixed = {a2: at[a2], a3: at[a3]}
        done2[k] = forward(k, a2, fixed, second_pairs[k])
        for step in (1, 3):
            fixed = {a2: lax.rem(at[a2] + step, 4), a3: at[a3]}
            third[k].append((fixed, ring(k, a3, fixed)))
    last = [[], [], []]
    for k in range(3):
        a1, a2, a3 = ORDERS[k]
        for c in done2[k]:
            c.wait_recv()
        fixed = {a2: lax.rem(at[a2] + 2, 4), a3: at[a3]}
        third[k].append((fixed, ring(k, a3, fixed)))

    def plane(k, step):
        return spot(k, {ORDERS[k][2]: lax.rem(at[ORDERS[k][2]] + step, 4)})

    across = [[None] * 4 for _ in range(3)]

    def hand(k, step):
        s = plane(k, step)
        across[k][step] = wires.start(ag[k].at[s], ot[k].at[s], partner)

    for k in range(3):
        hand(k, 0)
    loads[0].wait()
    loads[1].wait()

    def product(bufs, half, k, step, fresh):
        s = plane(k, step)
        left = bufs[k][s + (slice(None), slice(0, DATA[k]))].reshape(256, DATA[k])
        base = pl.multiple_of(half * HALF + OFFS[k], 128)
        part = jnp.dot(left, wgu[pl.ds(base, DATA[k]), :], preferred_element_type=jnp.float32)
        part = part.reshape(4, 4, 16, 512)
        acc[s] = acc[s] + part

    acc[...] = jnp.zeros_like(acc)
    for k in range(3):
        product(ag, core, k, 0, False)
    for n in range(4):
        for k in range(3):
            fixed, pair = third[k][n]
            last[k].append(forward(k, ORDERS[k][2], fixed, pair))
    for k in range(3):
        hand(k, 1)
        hand(k, 3)

    def side(n, _):
        for k in range(3):
            product(ag, core, k, 2 * n + 1, False)
        return _

    lax.fori_loop(0, 2, side, 0)
    for k in range(3):
        for step in (0, 1, 3):
            across[k][step].wait_recv()

    def side_other(n, _):
        for k in range(3):
            product(ot, 1 - core, k, n + n // 2, False)
        return _

    lax.fori_loop(0, 3, side_other, 0)
    tails = [[], [], []]
    for n in range(4):
        for k in range(3):
            a2, a3 = ORDERS[k][1:]
            for c in last[k][n]:
                c.wait_recv()
            s = spot(k, {a2: third[k][n][0][a2], a3: lax.rem(at[a3] + 2, 4)})
            tails[k].append(wires.start(ag[k].at[s], ot[k].at[s], partner))
    for k in range(3):
        product(ag, core, k, 2, False)
    for k in range(3):
        for c in tails[k]:
            c.wait_recv()
        product(ot, 1 - core, k, 2, False)

    lane = lax.broadcasted_iota(jnp.int32, (256, 128), 1)

    def activate(n, _):
        both = acc[n].reshape(256, 512)
        gate, up = both[:, 0:256], both[:, 256:512]
        packs = ag1[n, :, :, :, DATA[1]:WIDE[1]].reshape(256, 128).astype(jnp.float32)
        keep = (lane == t) | (lane == t + 16)
        weight = jnp.sum(jnp.where(keep, packs, 0.0), axis=1, keepdims=True)
        value = gate / (1.0 + jnp.exp(-gate)) * up * weight
        inner[n] = value.astype(jnp.bfloat16).reshape(4, 4, 16, 256)
        return _

    lax.fori_loop(0, 4, activate, 0)
    loads[2].wait()
    loads[3].wait()

    def group(k, step):
        a1 = ORDERS[k][0]
        return spot(k, {a1: lax.rem(at[a1] + step, 4)})

    def trade(k, n, step):
        s = group(k, step)
        return pltpu.make_async_remote_copy(
            src_ref=pt[k].at[s], dst_ref=pr[k].at[s], send_sem=xsend.at[k, n], recv_sem=xrecv.at[k, n],
            device_id=partner, device_id_type=MESH,
        )

    def step_of(n):
        return lax.rem(n * 3 + 2, 4) if not isinstance(n, int) else (n * 3 + 2) % 4

    def expand(n, _):
        for k in range(3):
            s = group(k, step_of(n))
            left = inner[s].reshape(256, 256)
            part = jnp.dot(left, wd[1 - core, :, OFFS[k]:OFFS[k] + DATA[k]], preferred_element_type=jnp.float32)
            pt[k][s] = part.astype(jnp.bfloat16).reshape(4, 4, 16, DATA[k])
            trade(k, n, step_of(n)).start()
            part = jnp.dot(left, wd[core, :, OFFS[k]:OFFS[k] + DATA[k]], preferred_element_type=jnp.float32)
            po[k][s] = part.astype(jnp.bfloat16).reshape(4, 4, 16, DATA[k])
        return _

    def meet(k, n):
        trade(k, n, step_of(n)).wait_recv()
        s = group(k, step_of(n))
        po[k][s] = (po[k][s].astype(jnp.float32) + pr[k][s].astype(jnp.float32)).astype(jnp.bfloat16)

    sums = [
        Sums(
            wires, at, core, ORDERS[k][0], po[k], lambda step, k=k: group(k, step), CUT, DATA[k],
            (ra0, ra1, ra2)[k], (rb0, rb1, rb2)[k], (rc0, rc1, rc2)[k], (rd0, rd1, rd2)[k],
        )
        for k in range(3)
    ]
    lax.fori_loop(0, 2, expand, 0)
    for k in range(3):
        meet(k, 0)
        sums[k].far()
    lax.fori_loop(2, 4, expand, 0)
    for k in range(3):
        meet(k, 1)
        meet(k, 3)
        sums[k].near()
    for k in range(3):
        sums[k].relay()
    for k in range(3):
        meet(k, 2)
    q = (q0, q1, q2)

    def group2(k, step):
        a1, a2, a3 = ORDERS[k]
        rest = [a for a in range(3) if a != a1]
        return tuple(lax.rem(at[a] + step, 4) if a == a2 else slice(None) for a in rest)

    sums2 = [
        Sums(
            wires, at, core, ORDERS[k][1], q[k], lambda step, k=k: group2(k, step), CUT, DATA[k],
            (qa0, qa1, qa2)[k], (qb0, qb1, qb2)[k], (qc0, qc1, qc2)[k], (qd0, qd1, qd2)[k],
        )
        for k in range(3)
    ]
    for k in range(3):
        q[k][...] = sums[k].total().astype(jnp.bfloat16)
        sums2[k].far()
        sums2[k].near()
    for k in range(3):
        sums2[k].relay()
    s_, sx = (s0, s1, s2), (sx0, sx1, sx2)
    final = []
    for k in range(3):
        s_[k][...] = sums2[k].total().astype(jnp.bfloat16)
        a3 = ORDERS[k][2]
        final.append([
            wires.start(s_[k].at[lax.rem(at[a3] + d, 4)], sx[k].at[d - 1], device(beside(at, a3, d), core))
            for d in (2, 1, 3)
        ])
    for k in range(3):
        for copy in final[k]:
            copy.wait_recv()
        total = s_[k][at[ORDERS[k][2]]].astype(jnp.float32)
        for d in range(3):
            total = total + sx[k][d].astype(jnp.float32)
        swap3[:, :, OFFS[k]:OFFS[k] + DATA[k]] = total.reshape(2, 8, DATA[k])
    over = wires.start(swap3.at[1 - core], swap4, partner)
    over.wait_recv()
    lead = jnp.where(is_one, swap4[...], swap3[0])
    tail = jnp.where(is_one, swap3[1], swap4[...])
    out[:, 0:HALF] = (rows[:, 0:HALF] + lead).astype(jnp.bfloat16)
    out[:, HALF:] = (rows[:, HALF:] + tail).astype(jnp.bfloat16)
    for k in range(3):
        for n in range(4):
            trade(k, n, step_of(n)).wait_send()
    wires.close()


def moe(middle, gain, ids, scores, eg, eu, ed):
    vm, an = pl.BlockSpec(memory_space=pltpu.VMEM), pl.BlockSpec(memory_space=pl.ANY)
    bf = jnp.bfloat16

    def three(shape, widths):
        return [pltpu.VMEM(shape + (w,), bf) for w in widths]

    lead, rest = (CUT,) * 3, tuple(w - CUT for w in DATA)
    cube, face, line, row = (4, 4, 4, 16), (4, 4, 16), (4, 16), (16,)
    scratch = [
        pltpu.VMEM((7168, 512), bf),
        pltpu.VMEM((2, 256, HALF), bf),
        pltpu.VMEM((4, 4, 4, 16, 512), jnp.float32),
        pltpu.VMEM((4, 4, 4, 16, 256), bf),
        pltpu.VMEM((8, HALF + 128), jnp.float32),
        pltpu.VMEM((8, HALF + 128), jnp.float32),
        pltpu.VMEM((2, 8, HALF), jnp.float32),
        pltpu.VMEM((8, HALF), jnp.float32),
    ]
    scratch += three(cube, WIDE) + three(cube, WIDE)
    scratch += three(cube, DATA) + three(cube, DATA) + three(cube, DATA)
    scratch += three(face, lead) + three(face, rest) + three(face, DATA) + three(face, DATA)
    scratch += three((4,) + line, DATA)
    scratch += three(line, lead) + three(line, rest) + three(line, DATA) + three(line, DATA)
    scratch += three((4,) + row, DATA) + three((3,) + row, DATA)
    scratch += [
        pltpu.SemaphoreType.DMA((4,)),
        pltpu.SemaphoreType.DMA((160,)),
        pltpu.SemaphoreType.DMA((160,)),
        pltpu.SemaphoreType.DMA((3, 4)),
        pltpu.SemaphoreType.DMA((3, 4)),
    ]
    return pl.pallas_call(
        moe_kernel,
        out_shape=jax.ShapeDtypeStruct((8, 7168), bf),
        in_specs=[vm, vm, vm, vm, an, an, an],
        out_specs=vm,
        scratch_shapes=scratch,
        compiler_params=pltpu.CompilerParams(
            collective_id=1, has_side_effects=True, vmem_limit_bytes=67043328
        ),
        name="experts",
    )(middle, gain, ids, scores, eg, eu, ed)


class Sums:
    def __init__(self, wires, at, core, axis, buf, index, cut, width, ra, rb, rc, rd):
        self.wires, self.buf, self.index = wires, buf, index
        self.up, self.down = device(beside(at, axis, 1), core), device(beside(at, axis, -1), core)
        self.lead, self.rest = (slice(None), slice(0, cut)), (slice(None), slice(cut, width))
        self.ra, self.rb, self.rc, self.rd = ra, rb, rc, rd

    def part(self, ref, cols):
        return ref.at[(slice(None),) * (len(ref.shape) - 2) + cols]

    def far(self):
        s = self.index(2)
        self.a = self.wires.start(self.buf.at[s + self.lead], self.ra, self.down)
        self.b = self.wires.start(self.buf.at[s + self.rest], self.rb, self.up)

    def near(self):
        left, right = self.index(3), self.index(1)
        self.c = self.wires.start(self.buf.at[left + self.rest], self.part(self.rc, self.rest), self.down)
        self.d = self.wires.start(self.buf.at[right + self.lead], self.part(self.rd, self.lead), self.up)

    def add(self, s, other):
        self.buf[s] = (self.buf[s].astype(jnp.float32) + other[...].astype(jnp.float32)).astype(jnp.bfloat16)

    def relay(self):
        self.a.wait_recv()
        s = self.index(3) + self.lead
        self.add(s, self.ra)
        self.e = self.wires.start(self.buf.at[s], self.part(self.rc, self.lead), self.down)
        self.b.wait_recv()
        s = self.index(1) + self.rest
        self.add(s, self.rb)
        self.f = self.wires.start(self.buf.at[s], self.part(self.rd, self.rest), self.up)

    def total(self):
        for copy in (self.c, self.d, self.e, self.f):
            copy.wait_recv()
        return (
            self.buf[self.index(0)].astype(jnp.float32)
            + self.rc[...].astype(jnp.float32)
            + self.rd[...].astype(jnp.float32)
        )


class Spread:
    def __init__(self, wires, at, core, axis, buf, index, lead, rest):
        self.wires, self.buf, self.index, self.lead, self.rest = wires, buf, index, lead, rest
        self.up, self.down = device(beside(at, axis, 1), core), device(beside(at, axis, -1), core)

    def near(self):
        s = self.index(0)
        self.a = self.wires.start(self.buf.at[s], self.buf.at[s], self.up)
        self.b = self.wires.start(self.buf.at[s], self.buf.at[s], self.down)

    def relay(self):
        self.a.wait_recv()
        s = self.index(3) + self.lead
        self.c = self.wires.start(self.buf.at[s], self.buf.at[s], self.up)
        self.b.wait_recv()
        s = self.index(1) + self.rest
        self.d = self.wires.start(self.buf.at[s], self.buf.at[s], self.down)

    def finish(self):
        self.c.wait_recv()
        self.d.wait_recv()


PLANES = ((1, 2), (2, 1))
FF = 1152
FD = 896


def dense_kernel(
    stream, gain, wg, wu, wd, table, leaving, queries, resident, new_cols, new_rows, res_len, got_len,
    middle, arrived, context,
    vg, vu, vd, nbuf, land, ft, gu, gx, gra, grb, grc, grd, hid, dn,
    pa, pb, pc, pd, qs, qx, fin, back,
    held0, held1, far_out, far_in, near_out, near_in, vq, vk,
    load_sem, send_sem, recv_sem,
):
    at, core, p, t = place()
    loads = [
        pltpu.make_async_copy(wg, vg, load_sem.at[0]),
        pltpu.make_async_copy(wu, vu, load_sem.at[1]),
        pltpu.make_async_copy(wd, vd, load_sem.at[2]),
        pltpu.make_async_copy(leaving.at[:, 0], held0.at[at[2]], load_sem.at[3]),
        pltpu.make_async_copy(leaving.at[:, 1], held1.at[at[1]], load_sem.at[4]),
        pltpu.make_async_copy(queries, vq, load_sem.at[5]),
        pltpu.make_async_copy(resident, vk, load_sem.at[6]),
    ]
    loads[3].start()
    loads[4].start()
    partner = device(at, 1 - core)
    line = [(lax.rem(p + q, 8), t) for q in range(1, 8)]
    greet(line + [device(beside(at, a, s), core) for a in (1, 2) for s in (1, 2, 3)])
    wires = Wires(send_sem, recv_sem)

    rows = stream[...].astype(jnp.float32)
    normed = rms(rows, gain[...]).astype(jnp.float32)
    for o in range(8):
        nbuf[o] = normed[:, o * FD:(o + 1) * FD]
    sent = [wires.start(nbuf.at[peer[0]], land.at[p], peer) for peer in line]
    land[p] = nbuf[p]

    loads[3].wait()
    loads[4].wait()
    held = (held0, held1)
    ways, hops, on = [], [{}, {}], [{}, {}]
    for l in (0, 1):
        a1 = (2, 1)[l]
        ways.append((device(beside(at, a1, 1), core), device(beside(at, a1, -1), core)))

    def carry(l, item):
        s = (at[(2, 1)[l]], item)
        hops[l][item] = [wires.start(held[l].at[s], held[l].at[s], way) for way in ways[l]]

    def relay_item(l, item):
        hops[l][item][item].wait_recv()
        s = (lax.rem(at[(2, 1)[l]] + (3, 1)[item], 4), item)
        on[l][item] = wires.start(held[l].at[s], held[l].at[s], ways[l][item])

    def settle(l):
        hops[l][0][1].wait_recv()
        hops[l][1][0].wait_recv()
        on[l][0].wait_recv()
        on[l][1].wait_recv()

    for l in (0, 1):
        carry(l, 0)
    for n in (0, 1, 5, 6, 2):
        loads[n].start()

    for copy in sent:
        copy.wait_recv()
    for x in range(4):
        ft[x // 2, x % 2, at[1], at[2]] = land[2 * x:2 * x + 2].reshape(16, FD).astype(jnp.bfloat16)

    lane256 = lax.broadcasted_iota(jnp.int32, (128, 256), 1)
    lane8 = lax.broadcasted_iota(jnp.int32, (128, 8), 1)
    scale = QKD ** (-0.5)
    cross_first = (((0,), (0,)), ((), ()))

    def attend(r, keys, length):
        query = vq[r]
        scores = lax.dot_general(query, keys, cross_first, preferred_element_type=jnp.float32) * scale
        newest = lax.dot_general(query, new_cols[...], cross_first, preferred_element_type=jnp.float32)
        own = jnp.sum(jnp.where(lane8 == r, newest, 0.0), axis=1, keepdims=True) * scale
        valid = lane256 < length
        masked = jnp.where(valid, scores, -1e30)
        top = jnp.maximum(jnp.max(masked, axis=1, keepdims=True), own)
        expo = jnp.where(valid, jnp.exp(masked - top), 0.0)
        own_expo = jnp.exp(own - top)
        total = jnp.sum(expo, axis=1, keepdims=True) + own_expo
        weights = (expo / total).astype(jnp.bfloat16)
        own_weight = (own_expo / total).astype(jnp.bfloat16).astype(jnp.float32)
        found = lax.dot_general(
            weights, keys[0:VDIM], (((1,), (1,)), ((), ())), preferred_element_type=jnp.float32
        )
        context[r] = (found + own_weight * new_rows[pl.ds(r, 1), 0:VDIM]).astype(jnp.bfloat16)

    def attend_stay(r, _):
        attend(r, vk[r], res_len[r])
        return _

    def spots(b, k, fixed):
        return (b, k) + tuple(fixed.get(a, slice(None)) for a in (1, 2))

    fcut = ((slice(None), slice(0, 512)), (slice(None), slice(512, FD)))

    def spread_of(b, k, axis, other):
        def index(step):
            fixed = dict(other)
            fixed[axis] = lax.rem(at[axis] + step, 4)
            return spots(b, k, fixed)

        return Spread(wires, at, core, axis, ft, index, *fcut)

    def rem(axis, step):
        return lax.rem(at[axis] + step, 4)

    first = {}
    second = {
        (b, k, j): spread_of(b, k, PLANES[k][1], {PLANES[k][0]: rem(PLANES[k][0], j)})
        for b in (0, 1) for k in (0, 1) for j in range(4)
    }
    for b in (0, 1):
        for k in (0, 1):
            here = (b, k, at[1], at[2])
            first[b, k] = [
                wires.start(ft.at[here], ft.at[here], device(beside(at, PLANES[k][0], d), core)) for d in (1, 3, 2)
            ]
            second[b, k, 0].near()
    for b in (0, 1):
        for k in (0, 1):
            first[b, k][0].wait_recv()
            second[b, k, 3].near()
            first[b, k][1].wait_recv()
            second[b, k, 1].near()
            first[b, k][2].wait_recv()
            second[b, k, 2].near()
        for k in (0, 1):
            second[b, k, 0].relay()
    loads[5].wait()
    loads[6].wait()
    lax.fori_loop(0, 2, attend_stay, 0)
    for b in (0, 1):
        for j in (3, 1, 2):
            for k in (0, 1):
                second[b, k, j].relay()
    lax.fori_loop(2, 4, attend_stay, 0)

    def mine(l, step, slot):
        a1, a2 = ((2, 1), (1, 2))[l]
        row = l * 4 + rem(a2, step)
        pick = table[row, slot]
        source, item = pick // 2, lax.rem(pick, 2)
        y, z = source // 4, lax.rem(source, 4)
        j, i = (z, y) if l == 0 else (y, z)
        return i, j, item

    peers2 = [[device(beside(at, a2, 1), core), device(beside(at, a2, -1), core)] for a2 in (1, 2)]
    far_copies, near_copies = {}, {}

    def merge_far(l):
        for slot in (0, 1):
            i, j, item = mine(l, 2, slot)
            far_out[l, slot] = held[l][j, item]
            far_copies[l, slot] = wires.start(far_out.at[l, slot], far_in.at[l, slot], peers2[l][1 - slot])

    def merge_near(l, slot, side):
        step = (3, 1)[side]
        i, j, item = mine(l, step, slot)
        if slot == side:
            far_copies[l, slot].wait_recv()
            a2 = (1, 2)[l]
            near_out[l, side, slot] = jnp.where(i == at[a2], held[l][j, item], far_in[l, slot])
        else:
            near_out[l, side, slot] = held[l][j, item]
        near_copies[l, side, slot] = wires.start(
            near_out.at[l, side, slot], near_in.at[l, side, slot], peers2[l][1 - side]
        )

    def merge_end(l):
        a2 = (1, 2)[l]
        for side in (0, 1):
            for slot in (0, 1):
                near_copies[l, side, slot].wait_recv()
        for slot in (0, 1):
            i, j, item = mine(l, 0, slot)
            delta = lax.rem(i - at[a2] + 4, 4)
            from_above = (delta == 1) | ((delta == 2) if slot == 0 else (delta == 5))
            other = jnp.where(from_above, near_in[l, 0, slot], near_in[l, 1, slot])
            arrived[slot, l] = jnp.where(delta == 0, held[l][j, item], other)

    grows = [(gra.at[b], grb.at[b], grc.at[b], grd.at[b]) for b in (0, 1)]
    halves = [None, None]

    def project(b):
        for h in (0, 1):
            c = (1 - core) if h == 0 else core
            left = ft[b, c].reshape(256, FD)
            g = jnp.dot(left, vg[...], preferred_element_type=jnp.float32).astype(jnp.bfloat16)
            gu[b, c, :, :, 0:FF] = g.reshape(4, 64, FF)
            u = jnp.dot(left, vu[...], preferred_element_type=jnp.float32).astype(jnp.bfloat16)
            gu[b, c, :, :, FF:2 * FF] = u.reshape(4, 64, FF)
            if h == 0:
                halves[b] = wires.start(gu.at[b, c], gx.at[b], partner)

    def gsum(b):
        return Sums(
            wires, at, core, 0, gu, lambda step: (b, core, rem(0, step)), FF, 2 * FF, *grows[b]
        )

    gsums = [gsum(0), gsum(1)]

    def join(b):
        halves[b].wait_recv()

        gu[b, core] = (gu[b, core].astype(jnp.float32) + gx[b].astype(jnp.float32)).astype(jnp.bfloat16)
        gsums[b].far()
        gsums[b].near()

    hspread = [
        Spread(wires, at, core, 0, hid, lambda step, b=b: (b, core, rem(0, step)),
               (slice(None), slice(0, 640)), (slice(None), slice(640, FF)))
        for b in (0, 1)
    ]
    hcross = [[], []]

    def cross(b, step):
        s = (b, core, rem(0, step))
        hcross[b].append(wires.start(hid.at[s], hid.at[s], partner))

    def activate(b):
        both = gsums[b].total()
        g, u = both[:, 0:FF], both[:, FF:2 * FF]
        hid[b, core, at[0]] = (g / (1.0 + jnp.exp(-g)) * u).astype(jnp.bfloat16)
        hspread[b].near()
        cross(b, 0)

    def hrelay(b):
        hspread[b].relay()
        cross(b, 3)
        cross(b, 1)

    def dsum(b, k):
        a1, a2 = PLANES[k]
        return Sums(
            wires, at, core, a1, dn, lambda step: spots(b, k, {a1: rem(a1, step)}), 512, FD,
            pa.at[b, k], pb.at[b, k], pc.at[b, k], pd.at[b, k],
        )

    ds = {(b, k): dsum(b, k) for b in (0, 1) for k in (0, 1)}
    ds2 = {}

    def contract(b):
        hspread[b].finish()
        cross(b, 2)
        for copy in hcross[b]:
            copy.wait_recv()
        for k in (0, 1):
            left = hid[b, k].reshape(256, FF)
            part = jnp.dot(left, vd[...], preferred_element_type=jnp.float32)
            dn[b, k] = part.astype(jnp.bfloat16).reshape(4, 4, 16, FD)
            ds[b, k].far()
            ds[b, k].near()

    def drelay(b):
        for k in (0, 1):
            ds[b, k].relay()

    def dturn(b):
        for k in (0, 1):
            qs[b, k] = ds[b, k].total().astype(jnp.bfloat16)
            a2 = PLANES[k][1]
            ds2[b, k] = [
                wires.start(qs.at[b, k, rem(a2, d)], qx.at[b, k, d - 1], device(beside(at, a2, d), core))
                for d in (2, 1, 3)
            ]

    def dend(b):
        for k in (0, 1):
            x = 2 * b + k
            for copy in ds2[b, k]:
                copy.wait_recv()
            total = qs[b, k, at[PLANES[k][1]]].astype(jnp.float32)
            for d in range(3):
                total = total + qx[b, k, d].astype(jnp.float32)
            fin[2 * x:2 * x + 2] = total.reshape(2, 8, FD)

    for j in range(4):
        for k in (0, 1):
            second[0, k, j].finish()
    loads[0].wait()
    loads[1].wait()
    project(0)
    for j in range(4):
        for k in (0, 1):
            second[1, k, j].finish()
    for l in (0, 1):
        carry(l, 1)
    for l in (0, 1):
        relay_item(l, 0)
    project(1)
    join(0)
    join(1)
    for l in (0, 1):
        relay_item(l, 1)
    gsums[0].relay()
    lax.fori_loop(4, 6, attend_stay, 0)
    gsums[1].relay()
    for l in (0, 1):
        settle(l)
    for l in (0, 1):
        merge_far(l)
    activate(0)
    for l in (0, 1):
        merge_near(l, 1, 0)
        merge_near(l, 0, 1)
    activate(1)
    hrelay(0)
    for l in (0, 1):
        merge_near(l, 0, 0)
        merge_near(l, 1, 1)
    hrelay(1)
    loads[2].wait()
    contract(0)
    contract(1)
    drelay(0)
    drelay(1)
    for l in (0, 1):
        merge_end(l)
    dturn(0)
    dturn(1)
    for slot in (0, 1):
        attend(6 + slot, arrived[slot, 0], got_len[slot])
    dend(0)
    dend(1)
    sent = [wires.start(fin.at[peer[0]], back.at[p], peer) for peer in line]
    back[p] = fin[p]
    for copy in sent:
        copy.wait_recv()
    for o in range(8):
        cols = slice(o * FD, (o + 1) * FD)
        middle[:, cols] = (rows[:, cols] + back[o]).astype(jnp.bfloat16)
    wires.close()


def dense(stream, gain, wg, wu, wd, table, leaving, queries, resident, new_cols, new_rows, res_len, got_len):
    vm, an = pl.BlockSpec(memory_space=pltpu.VMEM), pl.BlockSpec(memory_space=pl.ANY)
    sm = pl.BlockSpec(memory_space=pltpu.SMEM)
    bf, f32 = jnp.bfloat16, jnp.float32
    item = (576, 256)
    scratch = [
        pltpu.VMEM((FD, FF), bf), pltpu.VMEM((FD, FF), bf), pltpu.VMEM((FF, FD), bf),
        pltpu.VMEM((8, 8, FD), f32), pltpu.VMEM((8, 8, FD), f32),
        pltpu.VMEM((2, 2, 4, 4, 16, FD), bf),
        pltpu.VMEM((2, 2, 4, 64, 2 * FF), bf), pltpu.VMEM((2, 4, 64, 2 * FF), bf),
        pltpu.VMEM((2, 64, FF), bf), pltpu.VMEM((2, 64, FF), bf),
        pltpu.VMEM((2, 64, 2 * FF), bf), pltpu.VMEM((2, 64, 2 * FF), bf),
        pltpu.VMEM((2, 2, 4, 64, FF), bf),
        pltpu.VMEM((2, 2, 4, 4, 16, FD), bf),
    ]
    lead = (2, 2, 4, 16)
    scratch += [
        pltpu.VMEM(lead + (512,), bf), pltpu.VMEM(lead + (FD - 512,), bf),
        pltpu.VMEM(lead + (FD,), bf), pltpu.VMEM(lead + (FD,), bf),
        pltpu.VMEM((2, 2, 4, 16, FD), bf), pltpu.VMEM((2, 2, 3, 16, FD), bf),
        pltpu.VMEM((8, 8, FD), f32), pltpu.VMEM((8, 8, FD), f32),
        pltpu.VMEM((4, 2) + item, bf), pltpu.VMEM((4, 2) + item, bf),
        pltpu.VMEM((2, 2) + item, bf), pltpu.VMEM((2, 2) + item, bf),
        pltpu.VMEM((2, 2, 2) + item, bf), pltpu.VMEM((2, 2, 2) + item, bf),
        pltpu.VMEM((8, 576, 128), bf), pltpu.VMEM((6, 576, 256), bf),
        pltpu.SemaphoreType.DMA((7,)), pltpu.SemaphoreType.DMA((240,)), pltpu.SemaphoreType.DMA((240,)),
    ]
    return pl.pallas_call(
        dense_kernel,
        out_shape=(
            jax.ShapeDtypeStruct((8, 7168), bf),
            jax.ShapeDtypeStruct((2, 2) + item, bf),
            jax.ShapeDtypeStruct((8, 128, 512), bf),
        ),
        in_specs=[vm, vm, an, an, an, sm, an, an, an, vm, vm, sm, sm],
        out_specs=(vm, vm, vm),
        scratch_shapes=scratch,
        compiler_params=pltpu.CompilerParams(
            collective_id=2, has_side_effects=True, vmem_limit_bytes=67043328
        ),
        name="dense",
    )(stream, gain, wg, wu, wd, table, leaving, queries, resident, new_cols, new_rows, res_len, got_len)


def route(mig_dest, leave_len):
    p, t = lax.axis_index("dp"), lax.axis_index("tp")
    group = lax.dynamic_slice_in_dim(mig_dest, p * 16, 16, 0).reshape(1, 32)
    lens = lax.dynamic_slice_in_dim(leave_len, p * 16, 16, 0).reshape(1, 32)
    step = jnp.arange(4)
    aims = jnp.concatenate([step * 4 + t % 4, t // 4 * 4 + step, t[None]])[:, None]
    hit = group == aims
    order = jnp.arange(32)[None, :]
    low = jnp.min(jnp.where(hit, order, 32), axis=1)
    high = jnp.max(jnp.where(hit, order, -1), axis=1)
    ends = jnp.stack([low, high], axis=1)
    got = jnp.sum(jnp.where(order == ends[8][:, None], lens, 0), axis=1)
    return ends, got


def on_device(
    queries,
    new_latent,
    resident,
    leaving,
    res_len,
    leave_len,
    mig_dest,
    stream,
    dense_gain,
    w_gate,
    w_up,
    w_down,
    moe_gain,
    expert_gate,
    expert_up,
    expert_down,
    expert_ids,
    gate_scores,
):
    table, moved_len = route(mig_dest, leave_len)
    middle, moved, context = dense(
        stream, dense_gain[None], w_gate, w_up, w_down, table, jnp.swapaxes(leaving, 2, 3),
        jnp.swapaxes(queries, 1, 2), jnp.swapaxes(resident, 1, 2), new_latent.T,
        new_latent.astype(jnp.float32), res_len, moved_len,
    )
    arrived = jnp.swapaxes(moved, 2, 3)
    stream_out = moe(
        middle, moe_gain[None], expert_ids, gate_scores, expert_gate[0], expert_up[0], expert_down[0]
    )
    return (context, arrived, stream_out)


def solution(mesh):
    placed = (
        P(("dp", "tp"), None, None),
        P(("dp", "tp"), None),
        P(("dp", "tp"), None, None),
        P(("dp", "tp"), None, None, None),
        P(("dp", "tp")),
        P(),
        P(),
        P(("dp", "tp"), None),
        P(),
        P("dp", "tp"),
        P("dp", "tp"),
        P("tp", "dp"),
        P(),
        P("tp", None, "dp"),
        P("tp", None, "dp"),
        P("tp", "dp", None),
        P(("dp", "tp"), None),
        P(("dp", "tp"), None),
    )
    return jax.shard_map(
        on_device,
        mesh=mesh,
        in_specs=placed,
        out_specs=(
            P(("dp", "tp"), None, None),
            P(("dp", "tp"), None, None, None),
            P(("dp", "tp"), None),
        ),
        check_vma=False,
    )
```

```python
import functools

import jax
import jax.numpy as jnp
from jax import lax
from jax.experimental import pallas as pl
from jax.experimental.pallas import tpu as pltpu
from jax.sharding import PartitionSpec as P

MESH = pl.DeviceIdType.MESH

VDIM = 512
QKD = 192


EPS = 1e-06
ROUTE_SCALE = 2.5


HALF = 3584
OFFS = (0, 1280, 2432)
DATA = (1280, 1152, 1152)
WIDE = (1280, 1280, 1152)
ORDERS = ((0, 1, 2), (1, 2, 0), (2, 0, 1))
CUT = 640


def place():
    p, t = lax.axis_index("dp"), lax.axis_index("tp")
    return [p // 2, t // 4, t % 4], p % 2, p, t


def device(at, core):
    return (at[0] * 2 + core, at[1] * 4 + at[2])


def beside(at, axis, step):
    return [lax.rem(at[a] + 4 + step, 4) if a == axis else at[a] for a in range(3)]


class Wires:
    def __init__(self, send, recv):
        self.send, self.recv, self.used = send, recv, 0
        self.open = []

    def start(self, src, dst, peer):
        i = self.used
        self.used += 1
        copy = pltpu.make_async_remote_copy(
            src_ref=src, dst_ref=dst, send_sem=self.send.at[i], recv_sem=self.recv.at[i],
            device_id=peer, device_id_type=MESH,
        )
        copy.start()
        self.open.append(copy)
        return copy

    def close(self):
        for copy in self.open:
            copy.wait_send()


def greet(peers):
    barrier = pltpu.get_barrier_semaphore()
    for peer in peers:
        pl.semaphore_signal(barrier, inc=1, device_id=peer, device_id_type=MESH)
    pl.semaphore_wait(barrier, len(peers))


def rms(rows, gain):
    mean_square = jnp.mean(rows * rows, axis=-1, keepdims=True)
    return (rows * lax.rsqrt(mean_square + EPS) * gain).astype(jnp.bfloat16)


def picks(axes_values):
    return tuple(axes_values)


def moe_kernel(
    middle, gain, ids, scores, eg, eu, ed, out,
    wgu, wd, acc, inner, swap, swap2, swap3, swap4,
    ag0, ag1, ag2, ot0, ot1, ot2, po0, po1, po2, pt0, pt1, pt2, pr0, pr1, pr2,
    ra0, ra1, ra2, rb0, rb1, rb2, rc0, rc1, rc2, rd0, rd1, rd2,
    q0, q1, q2, qa0, qa1, qa2, qb0, qb1, qb2, qc0, qc1, qc2, qd0, qd1, qd2,
    s0, s1, s2, sx0, sx1, sx2,
    load_sem, send_sem, recv_sem, xsend, xrecv,
):
    at, core, p, t = place()
    ag, ot, po, pt, pr = (ag0, ag1, ag2), (ot0, ot1, ot2), (po0, po1, po2), (pt0, pt1, pt2), (pr0, pr1, pr2)
    loads = [
        pltpu.make_async_copy(eg, wgu.at[:, 0:256], load_sem.at[0]),
        pltpu.make_async_copy(eu, wgu.at[:, 256:512], load_sem.at[1]),
        pltpu.make_async_copy(ed.at[:, 0:HALF], wd.at[0], load_sem.at[2]),
        pltpu.make_async_copy(ed.at[:, HALF:2 * HALF], wd.at[1], load_sem.at[3]),
    ]
    partner = device(at, 1 - core)
    greet([partner] + [device(beside(at, a, s), core) for a in range(3) for s in (1, 2, 3)])
    wires = Wires(send_sem, recv_sem)

    rows = middle[...].astype(jnp.float32)
    mixed = rms(rows, gain[...]).astype(jnp.float32)
    given = scores[...]
    share = given / jnp.sum(given, axis=1, keepdims=True) * ROUTE_SCALE
    lane = lax.broadcasted_iota(jnp.int32, (8, 128), 1)
    spread = jnp.zeros((8, 128), jnp.float32)
    for k in range(8):
        spread = spread + jnp.where(lane == ids[:, k:k + 1], share[:, k:k + 1], 0.0)
    high = spread.astype(jnp.bfloat16).astype(jnp.float32)
    low = (spread - high).astype(jnp.bfloat16).astype(jnp.float32)
    packed = high + pltpu.roll(low, 16, 1)
    is_one = core == 1
    swap[:, 0:HALF] = jnp.where(is_one, mixed[:, 0:HALF], mixed[:, HALF:])
    swap[:, HALF:] = packed
    over = wires.start(swap, swap2, partner)
    mine = jnp.where(is_one, mixed[:, HALF:], mixed[:, 0:HALF])
    over.wait_recv()
    theirs = swap2[:, 0:HALF]
    first = jnp.where(is_one, theirs, mine)
    second = jnp.where(is_one, mine, theirs)
    block = jnp.concatenate([first, second], axis=0).astype(jnp.bfloat16)
    other_pack = swap2[:, HALF:]
    pack = jnp.concatenate(
        [jnp.where(is_one, other_pack, packed), jnp.where(is_one, packed, other_pack)], axis=0
    ).astype(jnp.bfloat16)
    for k in range(3):
        ag[k][at[0], at[1], at[2], :, 0:DATA[k]] = block[:, OFFS[k]:OFFS[k] + DATA[k]]
    ag1[at[0], at[1], at[2], :, DATA[1]:WIDE[1]] = pack

    def spot(k, fixed):
        return tuple(fixed.get(a, slice(None)) for a in range(3))

    def cols(k, part):
        return slice(0, CUT) if part == 0 else slice(CUT, WIDE[k])

    def ring(k, axis, fixed):
        here = spot(k, fixed)
        up, down = device(beside(at, axis, 1), core), device(beside(at, axis, -1), core)
        a = wires.start(ag[k].at[here], ag[k].at[here], up)
        b = wires.start(ag[k].at[here], ag[k].at[here], down)
        return a, b

    def forward(k, axis, fixed, pair):
        up, down = device(beside(at, axis, 1), core), device(beside(at, axis, -1), core)
        below, above = dict(fixed), dict(fixed)
        below[axis], above[axis] = lax.rem(at[axis] + 3, 4), lax.rem(at[axis] + 1, 4)
        pair[0].wait_recv()
        s = spot(k, below) + (slice(None), cols(k, 0))
        a = wires.start(ag[k].at[s], ag[k].at[s], up)
        pair[1].wait_recv()
        s = spot(k, above) + (slice(None), cols(k, 1))
        b = wires.start(ag[k].at[s], ag[k].at[s], down)
        return a, b

    own = [{a: at[a] for a in range(3)} for _ in range(3)]
    pairs = []
    for k in range(3):
        here = spot(k, own[k])
        pairs.append([
            wires.start(ag[k].at[here], ag[k].at[here], device(beside(at, ORDERS[k][0], d), core))
            for d in (2, 1, 3)
        ])
    for load in loads:
        load.start()
    second_pairs, third = [None] * 3, [[], [], []]
    for k in range(3):
        a1, a2, a3 = ORDERS[k]
        for c in pairs[k]:
            c.wait_recv()
        fixed = {a2: at[a2], a3: at[a3]}
        second_pairs[k] = ring(k, a2, fixed)
        third[k].append((fixed, ring(k, a3, fixed)))
    done2 = [None] * 3
    for k in range(3):
        a1, a2, a3 = ORDERS[k]
        fixed = {a2: at[a2], a3: at[a3]}
        done2[k] = forward(k, a2, fixed, second_pairs[k])
        for step in (1, 3):
            fixed = {a2: lax.rem(at[a2] + step, 4), a3: at[a3]}
            third[k].append((fixed, ring(k, a3, fixed)))
    last = [[], [], []]
    for k in range(3):
        a1, a2, a3 = ORDERS[k]
        for c in done2[k]:
            c.wait_recv()
        fixed = {a2: lax.rem(at[a2] + 2, 4), a3: at[a3]}
        third[k].append((fixed, ring(k, a3, fixed)))

    def plane(k, step):
        return spot(k, {ORDERS[k][2]: lax.rem(at[ORDERS[k][2]] + step, 4)})

    across = [[None] * 4 for _ in range(3)]

    def hand(k, step):
        s = plane(k, step)
        across[k][step] = wires.start(ag[k].at[s], ot[k].at[s], partner)

    for k in range(3):
        hand(k, 0)
    loads[0].wait()
    loads[1].wait()

    def product(bufs, half, k, step, fresh):
        s = plane(k, step)
        left = bufs[k][s + (slice(None), slice(0, DATA[k]))].reshape(256, DATA[k])
        base = pl.multiple_of(half * HALF + OFFS[k], 128)
        part = jnp.dot(left, wgu[pl.ds(base, DATA[k]), :], preferred_element_type=jnp.float32)
        part = part.reshape(4, 4, 16, 512)
        acc[s] = acc[s] + part

    acc[...] = jnp.zeros_like(acc)
    for k in range(3):
        product(ag, core, k, 0, False)
    for n in range(4):
        for k in range(3):
            fixed, pair = third[k][n]
            last[k].append(forward(k, ORDERS[k][2], fixed, pair))
        if n == 1:
            for k in range(3):
                across[k][0].wait_recv()
                product(ot, 1 - core, k, 0, False)
    for k in range(3):
        hand(k, 1)
        hand(k, 3)

    def side(n, _):
        for k in range(3):
            product(ag, core, k, 2 * n + 1, False)
        return _

    lax.fori_loop(0, 2, side, 0)
    for k in range(3):
        for step in (1, 3):
            across[k][step].wait_recv()

    def side_other(n, _):
        for k in range(3):
            product(ot, 1 - core, k, 2 * n + 1, False)
        return _

    lax.fori_loop(0, 2, side_other, 0)
    tails = [[], [], []]
    for n in range(4):
        for k in range(3):
            a2, a3 = ORDERS[k][1:]
            for c in last[k][n]:
                c.wait_recv()
            s = spot(k, {a2: third[k][n][0][a2], a3: lax.rem(at[a3] + 2, 4)})
            tails[k].append(wires.start(ag[k].at[s], ot[k].at[s], partner))
    for k in range(3):
        product(ag, core, k, 2, False)
    for k in range(3):
        for c in tails[k]:
            c.wait_recv()
        product(ot, 1 - core, k, 2, False)

    lane = lax.broadcasted_iota(jnp.int32, (256, 128), 1)

    def activate(n, _):
        both = acc[n].reshape(256, 512)
        gate, up = both[:, 0:256], both[:, 256:512]
        packs = ag1[n, :, :, :, DATA[1]:WIDE[1]].reshape(256, 128).astype(jnp.float32)
        keep = (lane == t) | (lane == t + 16)
        weight = jnp.sum(jnp.where(keep, packs, 0.0), axis=1, keepdims=True)
        value = gate / (1.0 + jnp.exp(-gate)) * up * weight
        inner[n] = value.astype(jnp.bfloat16).reshape(4, 4, 16, 256)
        return _

    lax.fori_loop(0, 4, activate, 0)
    loads[2].wait()
    loads[3].wait()

    def group(k, step):
        a1 = ORDERS[k][0]
        return spot(k, {a1: lax.rem(at[a1] + step, 4)})

    def trade(k, n, step):
        s = group(k, step)
        return pltpu.make_async_remote_copy(
            src_ref=pt[k].at[s], dst_ref=pr[k].at[s], send_sem=xsend.at[k, n], recv_sem=xrecv.at[k, n],
            device_id=partner, device_id_type=MESH,
        )

    def step_of(n):
        return lax.rem(n * 3 + 2, 4) if not isinstance(n, int) else (n * 3 + 2) % 4

    def expand(n, _):
        for k in range(3):
            s = group(k, step_of(n))
            left = inner[s].reshape(256, 256)
            part = jnp.dot(left, wd[1 - core, :, OFFS[k]:OFFS[k] + DATA[k]], preferred_element_type=jnp.float32)
            pt[k][s] = part.astype(jnp.bfloat16).reshape(4, 4, 16, DATA[k])
            trade(k, n, step_of(n)).start()
            part = jnp.dot(left, wd[core, :, OFFS[k]:OFFS[k] + DATA[k]], preferred_element_type=jnp.float32)
            po[k][s] = part.astype(jnp.bfloat16).reshape(4, 4, 16, DATA[k])
        return _

    def meet(k, n):
        trade(k, n, step_of(n)).wait_recv()
        s = group(k, step_of(n))
        po[k][s] = (po[k][s].astype(jnp.float32) + pr[k][s].astype(jnp.float32)).astype(jnp.bfloat16)

    sums = [
        Sums(
            wires, at, core, ORDERS[k][0], po[k], lambda step, k=k: group(k, step), CUT, DATA[k],
            (ra0, ra1, ra2)[k], (rb0, rb1, rb2)[k], (rc0, rc1, rc2)[k], (rd0, rd1, rd2)[k],
        )
        for k in range(3)
    ]
    lax.fori_loop(0, 2, expand, 0)
    for k in range(3):
        meet(k, 0)
        sums[k].far()
    lax.fori_loop(2, 4, expand, 0)
    for k in range(3):
        meet(k, 1)
        meet(k, 3)
        sums[k].near()
    for k in range(3):
        sums[k].relay()
    for k in range(3):
        meet(k, 2)
    q = (q0, q1, q2)

    def group2(k, step):
        a1, a2, a3 = ORDERS[k]
        rest = [a for a in range(3) if a != a1]
        return tuple(lax.rem(at[a] + step, 4) if a == a2 else slice(None) for a in rest)

    sums2 = [
        Sums(
            wires, at, core, ORDERS[k][1], q[k], lambda step, k=k: group2(k, step), CUT, DATA[k],
            (qa0, qa1, qa2)[k], (qb0, qb1, qb2)[k], (qc0, qc1, qc2)[k], (qd0, qd1, qd2)[k],
        )
        for k in range(3)
    ]
    for k in range(3):
        q[k][...] = sums[k].total().astype(jnp.bfloat16)
        sums2[k].far()
        sums2[k].near()
    for k in range(3):
        sums2[k].relay()
    s_, sx = (s0, s1, s2), (sx0, sx1, sx2)
    final = []
    for k in range(3):
        s_[k][...] = sums2[k].total().astype(jnp.bfloat16)
        a3 = ORDERS[k][2]
        final.append([
            wires.start(s_[k].at[lax.rem(at[a3] + d, 4)], sx[k].at[d - 1], device(beside(at, a3, d), core))
            for d in (2, 1, 3)
        ])
    for k in range(3):
        for copy in final[k]:
            copy.wait_recv()
        total = s_[k][at[ORDERS[k][2]]].astype(jnp.float32)
        for d in range(3):
            total = total + sx[k][d].astype(jnp.float32)
        swap3[:, :, OFFS[k]:OFFS[k] + DATA[k]] = total.reshape(2, 8, DATA[k])
    over = wires.start(swap3.at[1 - core], swap4, partner)
    over.wait_recv()
    lead = jnp.where(is_one, swap4[...], swap3[0])
    tail = jnp.where(is_one, swap3[1], swap4[...])
    out[:, 0:HALF] = (rows[:, 0:HALF] + lead).astype(jnp.bfloat16)
    out[:, HALF:] = (rows[:, HALF:] + tail).astype(jnp.bfloat16)
    for k in range(3):
        for n in range(4):
            trade(k, n, step_of(n)).wait_send()
    wires.close()


def moe(middle, gain, ids, scores, eg, eu, ed):
    vm, an = pl.BlockSpec(memory_space=pltpu.VMEM), pl.BlockSpec(memory_space=pl.ANY)
    bf = jnp.bfloat16

    def three(shape, widths):
        return [pltpu.VMEM(shape + (w,), bf) for w in widths]

    lead, rest = (CUT,) * 3, tuple(w - CUT for w in DATA)
    cube, face, line, row = (4, 4, 4, 16), (4, 4, 16), (4, 16), (16,)
    scratch = [
        pltpu.VMEM((7168, 512), bf),
        pltpu.VMEM((2, 256, HALF), bf),
        pltpu.VMEM((4, 4, 4, 16, 512), jnp.float32),
        pltpu.VMEM((4, 4, 4, 16, 256), bf),
        pltpu.VMEM((8, HALF + 128), jnp.float32),
        pltpu.VMEM((8, HALF + 128), jnp.float32),
        pltpu.VMEM((2, 8, HALF), jnp.float32),
        pltpu.VMEM((8, HALF), jnp.float32),
    ]
    scratch += three(cube, WIDE) + three(cube, WIDE)
    scratch += three(cube, DATA) + three(cube, DATA) + three(cube, DATA)
    scratch += three(face, lead) + three(face, rest) + three(face, DATA) + three(face, DATA)
    scratch += three((4,) + line, DATA)
    scratch += three(line, lead) + three(line, rest) + three(line, DATA) + three(line, DATA)
    scratch += three((4,) + row, DATA) + three((3,) + row, DATA)
    scratch += [
        pltpu.SemaphoreType.DMA((4,)),
        pltpu.SemaphoreType.DMA((160,)),
        pltpu.SemaphoreType.DMA((160,)),
        pltpu.SemaphoreType.DMA((3, 4)),
        pltpu.SemaphoreType.DMA((3, 4)),
    ]
    return pl.pallas_call(
        moe_kernel,
        out_shape=jax.ShapeDtypeStruct((8, 7168), bf),
        in_specs=[vm, vm, vm, vm, an, an, an],
        out_specs=vm,
        scratch_shapes=scratch,
        compiler_params=pltpu.CompilerParams(
            collective_id=1, has_side_effects=True, vmem_limit_bytes=67043328
        ),
        name="experts",
    )(middle, gain, ids, scores, eg, eu, ed)


class Sums:
    def __init__(self, wires, at, core, axis, buf, index, cut, width, ra, rb, rc, rd):
        self.wires, self.buf, self.index = wires, buf, index
        self.up, self.down = device(beside(at, axis, 1), core), device(beside(at, axis, -1), core)
        self.lead, self.rest = (slice(None), slice(0, cut)), (slice(None), slice(cut, width))
        self.ra, self.rb, self.rc, self.rd = ra, rb, rc, rd

    def part(self, ref, cols):
        return ref.at[(slice(None),) * (len(ref.shape) - 2) + cols]

    def far(self):
        s = self.index(2)
        self.a = self.wires.start(self.buf.at[s + self.lead], self.ra, self.down)
        self.b = self.wires.start(self.buf.at[s + self.rest], self.rb, self.up)

    def near(self):
        left, right = self.index(3), self.index(1)
        self.c = self.wires.start(self.buf.at[left + self.rest], self.part(self.rc, self.rest), self.down)
        self.d = self.wires.start(self.buf.at[right + self.lead], self.part(self.rd, self.lead), self.up)

    def add(self, s, other):
        self.buf[s] = (self.buf[s].astype(jnp.float32) + other[...].astype(jnp.float32)).astype(jnp.bfloat16)

    def relay(self):
        self.a.wait_recv()
        s = self.index(3) + self.lead
        self.add(s, self.ra)
        self.e = self.wires.start(self.buf.at[s], self.part(self.rc, self.lead), self.down)
        self.b.wait_recv()
        s = self.index(1) + self.rest
        self.add(s, self.rb)
        self.f = self.wires.start(self.buf.at[s], self.part(self.rd, self.rest), self.up)

    def total(self):
        for copy in (self.c, self.d, self.e, self.f):
            copy.wait_recv()
        return (
            self.buf[self.index(0)].astype(jnp.float32)
            + self.rc[...].astype(jnp.float32)
            + self.rd[...].astype(jnp.float32)
        )


class Spread:
    def __init__(self, wires, at, core, axis, buf, index, lead, rest):
        self.wires, self.buf, self.index, self.lead, self.rest = wires, buf, index, lead, rest
        self.up, self.down = device(beside(at, axis, 1), core), device(beside(at, axis, -1), core)

    def near(self):
        s = self.index(0)
        self.a = self.wires.start(self.buf.at[s], self.buf.at[s], self.up)
        self.b = self.wires.start(self.buf.at[s], self.buf.at[s], self.down)

    def relay(self):
        self.a.wait_recv()
        s = self.index(3) + self.lead
        self.c = self.wires.start(self.buf.at[s], self.buf.at[s], self.up)
        self.b.wait_recv()
        s = self.index(1) + self.rest
        self.d = self.wires.start(self.buf.at[s], self.buf.at[s], self.down)

    def finish(self):
        self.c.wait_recv()
        self.d.wait_recv()


PLANES = ((1, 2), (2, 1))
FF = 1152
FD = 896


def dense_kernel(
    stream, gain, wg, wu, wd, table, leaving, queries, resident, new_rows, res_len, got_len,
    middle, arrived, context,
    vg, vu, vd, nbuf, land, ft, gu, gx, gra, grb, grc, grd, hid, dn,
    pa, pb, pc, pd, qs, qx, fin, back,
    held0, held1, far_out, far_in, near_out, near_in, vq, vk,
    load_sem, send_sem, recv_sem,
):
    at, core, p, t = place()
    loads = [
        pltpu.make_async_copy(wg, vg, load_sem.at[0]),
        pltpu.make_async_copy(wu, vu, load_sem.at[1]),
        pltpu.make_async_copy(wd, vd, load_sem.at[2]),
        pltpu.make_async_copy(leaving.at[:, 0], held0.at[at[2]], load_sem.at[3]),
        pltpu.make_async_copy(leaving.at[:, 1], held1.at[at[1]], load_sem.at[4]),
        pltpu.make_async_copy(queries, vq, load_sem.at[5]),
        pltpu.make_async_copy(resident, vk, load_sem.at[6]),
    ]
    loads[3].start()
    loads[4].start()
    partner = device(at, 1 - core)
    line = [(lax.rem(p + q, 8), t) for q in range(1, 8)]
    greet(line + [device(beside(at, a, s), core) for a in (1, 2) for s in (1, 2, 3)])
    wires = Wires(send_sem, recv_sem)

    rows = stream[...].astype(jnp.float32)
    normed = rms(rows, gain[...]).astype(jnp.float32)
    for o in range(8):
        nbuf[o] = normed[:, o * FD:(o + 1) * FD]
    sent = [wires.start(nbuf.at[peer[0]], land.at[p], peer) for peer in line]
    land[p] = nbuf[p]

    loads[3].wait()
    loads[4].wait()
    held = (held0, held1)
    ways, hops, on = [], [{}, {}], [{}, {}]
    for l in (0, 1):
        a1 = (2, 1)[l]
        ways.append((device(beside(at, a1, 1), core), device(beside(at, a1, -1), core)))

    def carry(l, item):
        s = (at[(2, 1)[l]], item)
        hops[l][item] = [wires.start(held[l].at[s], held[l].at[s], way) for way in ways[l]]

    def relay_item(l, item):
        hops[l][item][item].wait_recv()
        s = (lax.rem(at[(2, 1)[l]] + (3, 1)[item], 4), item)
        on[l][item] = wires.start(held[l].at[s], held[l].at[s], ways[l][item])

    def settle(l):
        hops[l][0][1].wait_recv()
        hops[l][1][0].wait_recv()
        on[l][0].wait_recv()
        on[l][1].wait_recv()

    for l in (0, 1):
        carry(l, 0)
    for n in (0, 1, 5, 6, 2):
        loads[n].start()

    for copy in sent:
        copy.wait_recv()
    for x in range(4):
        ft[x // 2, x % 2, at[1], at[2]] = land[2 * x:2 * x + 2].reshape(16, FD).astype(jnp.bfloat16)

    lane256 = lax.broadcasted_iota(jnp.int32, (128, 256), 1)
    lane8 = lax.broadcasted_iota(jnp.int32, (128, 8), 1)
    sub8 = lax.broadcasted_iota(jnp.int32, (8, VDIM), 0)
    scale = QKD ** (-0.5)
    cross_first = (((0,), (0,)), ((), ()))

    def attend(r, keys, length):
        query = vq[r]
        scores = lax.dot_general(query, keys, cross_first, preferred_element_type=jnp.float32) * scale
        newest = jnp.dot(new_rows[...], query, preferred_element_type=jnp.float32).T
        own = jnp.sum(jnp.where(lane8 == r, newest, 0.0), axis=1, keepdims=True) * scale
        valid = lane256 < length
        masked = jnp.where(valid, scores, -1e30)
        top = jnp.maximum(jnp.max(masked, axis=1, keepdims=True), own)
        expo = jnp.where(valid, jnp.exp(masked - top), 0.0)
        own_expo = jnp.exp(own - top)
        total = jnp.sum(expo, axis=1, keepdims=True) + own_expo
        weights = (expo / total).astype(jnp.bfloat16)
        own_weight = (own_expo / total).astype(jnp.bfloat16).astype(jnp.float32)
        found = lax.dot_general(
            weights, keys[0:VDIM], (((1,), (1,)), ((), ())), preferred_element_type=jnp.float32
        )
        row = new_rows[:, 0:VDIM].astype(jnp.float32)
        row = jnp.sum(jnp.where(sub8 == r, row, 0.0), axis=0, keepdims=True)
        context[r] = (found + own_weight * row).astype(jnp.bfloat16)

    def attend_stay(r, _):
        attend(r, vk[r], res_len[r])
        return _

    def spots(b, k, fixed):
        return (b, k) + tuple(fixed.get(a, slice(None)) for a in (1, 2))

    fcut = ((slice(None), slice(0, 512)), (slice(None), slice(512, FD)))

    def spread_of(b, k, axis, other):
        def index(step):
            fixed = dict(other)
            fixed[axis] = lax.rem(at[axis] + step, 4)
            return spots(b, k, fixed)

        return Spread(wires, at, core, axis, ft, index, *fcut)

    def rem(axis, step):
        return lax.rem(at[axis] + step, 4)

    first = {}
    second = {
        (b, k, j): spread_of(b, k, PLANES[k][1], {PLANES[k][0]: rem(PLANES[k][0], j)})
        for b in (0, 1) for k in (0, 1) for j in range(4)
    }
    for b in (0, 1):
        for k in (0, 1):
            here = (b, k, at[1], at[2])
            first[b, k] = [
                wires.start(ft.at[here], ft.at[here], device(beside(at, PLANES[k][0], d), core)) for d in (1, 3, 2)
            ]
            second[b, k, 0].near()
    for b in (0, 1):
        for k in (0, 1):
            first[b, k][0].wait_recv()
            second[b, k, 3].near()
            first[b, k][1].wait_recv()
            second[b, k, 1].near()
            first[b, k][2].wait_recv()
            second[b, k, 2].near()
        for k in (0, 1):
            second[b, k, 0].relay()
    loads[5].wait()
    loads[6].wait()
    lax.fori_loop(0, 2, attend_stay, 0)
    for b in (0, 1):
        for j in (3, 1, 2):
            for k in (0, 1):
                second[b, k, j].relay()
    lax.fori_loop(2, 4, attend_stay, 0)

    def mine(l, step, slot):
        a1, a2 = ((2, 1), (1, 2))[l]
        row = l * 4 + rem(a2, step)
        pick = table[row, slot]
        source, item = pick // 2, lax.rem(pick, 2)
        y, z = source // 4, lax.rem(source, 4)
        j, i = (z, y) if l == 0 else (y, z)
        return i, j, item

    peers2 = [[device(beside(at, a2, 1), core), device(beside(at, a2, -1), core)] for a2 in (1, 2)]
    far_copies, near_copies = {}, {}

    def merge_far(l):
        for slot in (0, 1):
            i, j, item = mine(l, 2, slot)
            far_out[l, slot] = held[l][j, item]
            far_copies[l, slot] = wires.start(far_out.at[l, slot], far_in.at[l, slot], peers2[l][1 - slot])

    def merge_near(l, slot, side):
        step = (3, 1)[side]
        i, j, item = mine(l, step, slot)
        if slot == side:
            far_copies[l, slot].wait_recv()
            a2 = (1, 2)[l]
            near_out[l, side, slot] = jnp.where(i == at[a2], held[l][j, item], far_in[l, slot])
        else:
            near_out[l, side, slot] = held[l][j, item]
        near_copies[l, side, slot] = wires.start(
            near_out.at[l, side, slot], near_in.at[l, side, slot], peers2[l][1 - side]
        )

    def merge_end(l):
        a2 = (1, 2)[l]
        for side in (0, 1):
            for slot in (0, 1):
                near_copies[l, side, slot].wait_recv()
        for slot in (0, 1):
            i, j, item = mine(l, 0, slot)
            delta = lax.rem(i - at[a2] + 4, 4)
            from_above = (delta == 1) | ((delta == 2) if slot == 0 else (delta == 5))
            other = jnp.where(from_above, near_in[l, 0, slot], near_in[l, 1, slot])
            arrived[slot, l] = jnp.where(delta == 0, held[l][j, item], other)

    grows = [(gra.at[b], grb.at[b], grc.at[b], grd.at[b]) for b in (0, 1)]
    halves = [None, None]

    def project(b):
        for h in (0, 1):
            c = (1 - core) if h == 0 else core
            left = ft[b, c].reshape(256, FD)
            g = jnp.dot(left, vg[...], preferred_element_type=jnp.float32).astype(jnp.bfloat16)
            gu[b, c, :, :, 0:FF] = g.reshape(4, 64, FF)
            u = jnp.dot(left, vu[...], preferred_element_type=jnp.float32).astype(jnp.bfloat16)
            gu[b, c, :, :, FF:2 * FF] = u.reshape(4, 64, FF)
            if h == 0:
                halves[b] = wires.start(gu.at[b, c], gx.at[b], partner)

    def gsum(b):
        return Sums(
            wires, at, core, 0, gu, lambda step: (b, core, rem(0, step)), FF, 2 * FF, *grows[b]
        )

    gsums = [gsum(0), gsum(1)]

    def join(b):
        halves[b].wait_recv()

        gu[b, core] = (gu[b, core].astype(jnp.float32) + gx[b].astype(jnp.float32)).astype(jnp.bfloat16)
        gsums[b].far()
        gsums[b].near()

    hspread = [
        Spread(wires, at, core, 0, hid, lambda step, b=b: (b, core, rem(0, step)),
               (slice(None), slice(0, 640)), (slice(None), slice(640, FF)))
        for b in (0, 1)
    ]
    hcross = [[], []]

    def cross(b, step):
        s = (b, core, rem(0, step))
        hcross[b].append(wires.start(hid.at[s], hid.at[s], partner))

    def activate(b):
        both = gsums[b].total()
        g, u = both[:, 0:FF], both[:, FF:2 * FF]
        hid[b, core, at[0]] = (g / (1.0 + jnp.exp(-g)) * u).astype(jnp.bfloat16)
        hspread[b].near()
        cross(b, 0)

    def hrelay(b):
        hspread[b].relay()
        cross(b, 3)
        cross(b, 1)

    def dsum(b, k):
        a1, a2 = PLANES[k]
        return Sums(
            wires, at, core, a1, dn, lambda step: spots(b, k, {a1: rem(a1, step)}), 512, FD,
            pa.at[b, k], pb.at[b, k], pc.at[b, k], pd.at[b, k],
        )

    ds = {(b, k): dsum(b, k) for b in (0, 1) for k in (0, 1)}
    ds2 = {}

    def contract(b):
        hspread[b].finish()
        cross(b, 2)
        for copy in hcross[b]:
            copy.wait_recv()
        for k in (0, 1):
            left = hid[b, k].reshape(256, FF)
            part = jnp.dot(left, vd[...], preferred_element_type=jnp.float32)
            dn[b, k] = part.astype(jnp.bfloat16).reshape(4, 4, 16, FD)
            ds[b, k].far()
            ds[b, k].near()

    def drelay(b):
        for k in (0, 1):
            ds[b, k].relay()

    def dturn(b):
        for k in (0, 1):
            qs[b, k] = ds[b, k].total().astype(jnp.bfloat16)
            a2 = PLANES[k][1]
            ds2[b, k] = [
                wires.start(qs.at[b, k, rem(a2, d)], qx.at[b, k, d - 1], device(beside(at, a2, d), core))
                for d in (2, 1, 3)
            ]

    def dend(b):
        for k in (0, 1):
            x = 2 * b + k
            for copy in ds2[b, k]:
                copy.wait_recv()
            total = qs[b, k, at[PLANES[k][1]]].astype(jnp.float32)
            for d in range(3):
                total = total + qx[b, k, d].astype(jnp.float32)
            fin[2 * x:2 * x + 2] = total.reshape(2, 8, FD)

    for j in range(4):
        for k in (0, 1):
            second[0, k, j].finish()
    loads[0].wait()
    loads[1].wait()
    project(0)
    for j in range(4):
        for k in (0, 1):
            second[1, k, j].finish()
    for l in (0, 1):
        carry(l, 1)
    for l in (0, 1):
        relay_item(l, 0)
    project(1)
    join(0)
    join(1)
    for l in (0, 1):
        relay_item(l, 1)
    gsums[0].relay()
    lax.fori_loop(4, 6, attend_stay, 0)
    gsums[1].relay()
    for l in (0, 1):
        settle(l)
    for l in (0, 1):
        merge_far(l)
    activate(0)
    for l in (0, 1):
        merge_near(l, 1, 0)
        merge_near(l, 0, 1)
    activate(1)
    hrelay(0)
    for l in (0, 1):
        merge_near(l, 0, 0)
        merge_near(l, 1, 1)
    hrelay(1)
    loads[2].wait()
    contract(0)
    contract(1)
    drelay(0)
    drelay(1)
    for l in (0, 1):
        merge_end(l)
    dturn(0)
    dturn(1)
    for slot in (0, 1):
        attend(6 + slot, arrived[slot, 0], got_len[slot])
    dend(0)
    dend(1)
    sent = [wires.start(fin.at[peer[0]], back.at[p], peer) for peer in line]
    back[p] = fin[p]
    for copy in sent:
        copy.wait_recv()
    for o in range(8):
        cols = slice(o * FD, (o + 1) * FD)
        middle[:, cols] = (rows[:, cols] + back[o]).astype(jnp.bfloat16)
    wires.close()


def dense(stream, gain, wg, wu, wd, table, leaving, queries, resident, new_rows, res_len, got_len):
    vm, an = pl.BlockSpec(memory_space=pltpu.VMEM), pl.BlockSpec(memory_space=pl.ANY)
    sm = pl.BlockSpec(memory_space=pltpu.SMEM)
    bf, f32 = jnp.bfloat16, jnp.float32
    item = (576, 256)
    scratch = [
        pltpu.VMEM((FD, FF), bf), pltpu.VMEM((FD, FF), bf), pltpu.VMEM((FF, FD), bf),
        pltpu.VMEM((8, 8, FD), f32), pltpu.VMEM((8, 8, FD), f32),
        pltpu.VMEM((2, 2, 4, 4, 16, FD), bf),
        pltpu.VMEM((2, 2, 4, 64, 2 * FF), bf), pltpu.VMEM((2, 4, 64, 2 * FF), bf),
        pltpu.VMEM((2, 64, FF), bf), pltpu.VMEM((2, 64, FF), bf),
        pltpu.VMEM((2, 64, 2 * FF), bf), pltpu.VMEM((2, 64, 2 * FF), bf),
        pltpu.VMEM((2, 2, 4, 64, FF), bf),
        pltpu.VMEM((2, 2, 4, 4, 16, FD), bf),
    ]
    lead = (2, 2, 4, 16)
    scratch += [
        pltpu.VMEM(lead + (512,), bf), pltpu.VMEM(lead + (FD - 512,), bf),
        pltpu.VMEM(lead + (FD,), bf), pltpu.VMEM(lead + (FD,), bf),
        pltpu.VMEM((2, 2, 4, 16, FD), bf), pltpu.VMEM((2, 2, 3, 16, FD), bf),
        pltpu.VMEM((8, 8, FD), f32), pltpu.VMEM((8, 8, FD), f32),
        pltpu.VMEM((4, 2) + item, bf), pltpu.VMEM((4, 2) + item, bf),
        pltpu.VMEM((2, 2) + item, bf), pltpu.VMEM((2, 2) + item, bf),
        pltpu.VMEM((2, 2, 2) + item, bf), pltpu.VMEM((2, 2, 2) + item, bf),
        pltpu.VMEM((8, 576, 128), bf), pltpu.VMEM((6, 576, 256), bf),
        pltpu.SemaphoreType.DMA((7,)), pltpu.SemaphoreType.DMA((240,)), pltpu.SemaphoreType.DMA((240,)),
    ]
    return pl.pallas_call(
        dense_kernel,
        out_shape=(
            jax.ShapeDtypeStruct((8, 7168), bf),
            jax.ShapeDtypeStruct((2, 2) + item, bf),
            jax.ShapeDtypeStruct((8, 128, 512), bf),
        ),
        in_specs=[vm, vm, an, an, an, sm, an, an, an, vm, sm, sm],
        out_specs=(vm, vm, vm),
        scratch_shapes=scratch,
        compiler_params=pltpu.CompilerParams(
            collective_id=2, has_side_effects=True, vmem_limit_bytes=67043328
        ),
        name="dense",
    )(stream, gain, wg, wu, wd, table, leaving, queries, resident, new_rows, res_len, got_len)


def route(mig_dest, leave_len):
    p, t = lax.axis_index("dp"), lax.axis_index("tp")
    group = lax.dynamic_slice_in_dim(mig_dest, p * 16, 16, 0).reshape(1, 32)
    lens = lax.dynamic_slice_in_dim(leave_len, p * 16, 16, 0).reshape(1, 32)
    step = jnp.arange(4)
    aims = jnp.concatenate([step * 4 + t % 4, t // 4 * 4 + step, t[None]])[:, None]
    hit = group == aims
    order = jnp.arange(32)[None, :]
    low = jnp.min(jnp.where(hit, order, 32), axis=1)
    high = jnp.max(jnp.where(hit, order, -1), axis=1)
    ends = jnp.stack([low, high], axis=1)
    got = jnp.sum(jnp.where(order == ends[8][:, None], lens, 0), axis=1)
    return ends, got


def on_device(
    queries,
    new_latent,
    resident,
    leaving,
    res_len,
    leave_len,
    mig_dest,
    stream,
    dense_gain,
    w_gate,
    w_up,
    w_down,
    moe_gain,
    expert_gate,
    expert_up,
    expert_down,
    expert_ids,
    gate_scores,
):
    table, moved_len = route(mig_dest, leave_len)
    middle, moved, context = dense(
        stream, dense_gain[None], w_gate, w_up, w_down, table, jnp.swapaxes(leaving, 2, 3),
        jnp.swapaxes(queries, 1, 2), jnp.swapaxes(resident, 1, 2), new_latent,
        res_len, moved_len,
    )
    arrived = jnp.swapaxes(moved, 2, 3)
    stream_out = moe(
        middle, moe_gain[None], expert_ids, gate_scores, expert_gate[0], expert_up[0], expert_down[0]
    )
    return (context, arrived, stream_out)


def solution(mesh):
    placed = (
        P(("dp", "tp"), None, None),
        P(("dp", "tp"), None),
        P(("dp", "tp"), None, None),
        P(("dp", "tp"), None, None, None),
        P(("dp", "tp")),
        P(),
        P(),
        P(("dp", "tp"), None),
        P(),
        P("dp", "tp"),
        P("dp", "tp"),
        P("tp", "dp"),
        P(),
        P("tp", None, "dp"),
        P("tp", None, "dp"),
        P("tp", "dp", None),
        P(("dp", "tp"), None),
        P(("dp", "tp"), None),
    )
    return jax.shard_map(
        on_device,
        mesh=mesh,
        in_specs=placed,
        out_specs=(
            P(("dp", "tp"), None, None),
            P(("dp", "tp"), None, None, None),
            P(("dp", "tp"), None),
        ),
        check_vma=False,
    )
```
